256 devices in a mesh: node: 64 (over y, z, core), feat: 4 (over x).
Axes of the slice: x: 4, y: 4, z: 8, core: 2. Of those that a mesh axis runs over, the one named last changes fastest.
Arguments:
- features: bfloat16 [32768, 128], P('node', 'feat'), may hold values from -10 to 10
- send_rows: int32 [64, 64, 64], P('node'), may hold values from 0 to 511
- send_count: int32 [64, 64], P('node'), may hold values from 1 to 64, 2048 in all within a row
- tile_src: int32 [256, 16], P('node'), may hold values from 0 to 35
- tile_val: bfloat16 [256, 16, 128, 128], P('node'), may hold values from 0 to 0.0009765625
- labels: int32 [32768], P('node'), may hold values from 0 to 171
- w_self1: bfloat16 [128, 1024], P('feat'), may hold values from -0.5 to 0.5
- w_neigh1: bfloat16 [128, 1024], P('feat'), may hold values from -0.5 to 0.5
- w_self2: bfloat16 [1024, 172], P('feat'), may hold values from -0.5 to 0.5
- w_neigh2: bfloat16 [1024, 172], P('feat'), may hold values from -0.1875 to 0.1875
Outputs:
- mean_loss: float32 [], replicated
- grad_self1: float32 [128, 1024], P('feat')
- grad_neigh1: float32 [128, 1024], P('feat')
- grad_self2: float32 [1024, 172], P('feat')
- grad_neigh2: float32 [1024, 172], P('feat')
The draws below stay inside these ranges and needn't reach their ends.
Inputs may be any that keep to these rules, and one draw needn't show every extreme that they name: `send_rows`: row indices within the sending partition's 512 rows. Each row of send_count sums to 2048 and holds 64 at least once. `tile_src`: block numbers of the destination partition's source rows: numbers below 4 name its own rows, the others its halo slots.
All inputs are finite; a program needn't handle non-finite values.
Results may differ from the reference program's by a relative error of at most 0.00095.
The reference program's roundings to bfloat16 on the way count: a program that leaves them out, or rounds other values in their place, can miss the bound.
Values may be sent and summed in bfloat16 or wider, within the bound.
A program may use at most 64 MiB of HBM per device.

```python
import math
import jax
import jax.numpy as jnp
import numpy as np
from jax import lax

F_IN = 128
HID = 1024
CLASSES = 172
NODE_DEV = 512
CAP = 64
K = 16
NODES = 32768
N_NODE = 64


def draw_features(key, part):
    base = jnp.clip(jax.random.normal(key, (NODES, F_IN), jnp.float32), -4.0, 4.0)
    return base.astype(jnp.bfloat16)


def draw_w_self2(key, part):
    noise = jnp.clip(jax.random.normal(key, (HID, CLASSES), jnp.float32), -4.0, 4.0)
    return (noise * HID ** (-0.5)).astype(jnp.bfloat16)


def place_ends(entries, own_key, low, largest):
    longest = entries.shape.index(max(entries.shape))
    spots = []
    for shift in (0, 1):
        where = [jax.random.randint(jax.random.fold_in(own_key, axis), (), 0, length) for axis, length in enumerate(entries.shape)]
        where[longest] = (where[longest] + shift) % entries.shape[longest]
        spots.append(tuple(where))
    return entries.at[spots[0]].set(low).at[spots[1]].set(largest)


def shard_levels(own_key, dims, shards, low, top_value):
    factor_of, own = 1.0, jax.random.fold_in(own_key, 6)
    for dim, blocks in shards:
        draws = jnp.exp(jax.random.uniform(jax.random.fold_in(own, dim), (blocks,), jnp.float32, low / len(shards), top_value / len(shards)))
        factor_of = factor_of * jnp.repeat(draws, dims[dim] // blocks).reshape([-1 if axis == dim else 1 for axis in range(len(dims))])
    return factor_of


def split_up(amount, total, limit, lean):
    portions = [(1 << 20) // math.isqrt(grade ** lean) + 1 for grade in range(2, amount + 1)]
    surplus, holding = total - limit - (amount - 1), [1] * (amount - 1)
    while surplus > 0:
        free = [i for i in range(amount - 1) if holding[i] < limit]
        whole, remaining = sum([portions[i] for i in free]), surplus
        for i in free:
            more = min(limit - holding[i], max(1, remaining * portions[i] // whole), surplus)
            holding[i] = holding[i] + more
            surplus = surplus - more
    return np.array([limit] + holding)


def uneven(own_key, number_of, total, limit, skew):
    if number_of == 2:
        one = jax.random.randint(own_key, (), max(1, total - limit), min(limit, total - 1) + 1)
        return jnp.stack([one, total - one])
    tallies = jnp.asarray(split_up(number_of, total, limit, skew), jnp.int32)
    pairs = (number_of - 1) // 2
    source_of, taker = tallies[1:1 + 2 * pairs:2], tallies[2:2 + 2 * pairs:2]
    slack = jnp.minimum(source_of - 1, limit - taker)
    moved = jax.random.randint(jax.random.fold_in(own_key, 1), (pairs,), 0, 1 << 20) % (slack + 1)
    tallies = tallies.at[1:1 + 2 * pairs:2].set(source_of - moved).at[2:2 + 2 * pairs:2].set(taker + moved)
    return tallies[jax.random.permutation(jax.random.fold_in(own_key, 2), number_of)]


def centred(stream_key, dims, width, most, shards=(), held_as=jnp.bfloat16):
    factor_of = shard_levels(stream_key, dims, shards, -0.22, 0.18) if shards else 1.0
    entries = jax.random.normal(stream_key, dims, jnp.float32) * width * factor_of
    return jnp.minimum(jnp.maximum(entries, -most), most).astype(held_as)


def setup_inputs(seed: int = 0) -> dict:
    seeds = jax.random.split(jax.random.key(seed), 11)
    return {
        "features": draw_features(jax.random.fold_in(seeds[10], 71), 0),
        "send_rows": place_ends(jax.random.randint(seeds[1], (N_NODE, N_NODE, CAP), 0, NODE_DEV), jax.random.fold_in(seeds[1], 1), 0, NODE_DEV - 1).astype(jnp.int32),
        "send_count": jax.vmap(lambda own: uneven(own, N_NODE, N_NODE * CAP // 2, CAP, 2))(jax.random.split(seeds[2], N_NODE)).reshape((N_NODE, N_NODE)).astype(jnp.int32),
        "tile_src": place_ends(jax.random.randint(seeds[3], (NODES // 128, K), 0, (NODE_DEV + N_NODE * CAP) // 128), jax.random.fold_in(seeds[3], 1), 0, ((NODE_DEV + N_NODE * CAP) // 128) - 1).astype(jnp.int32),
        "tile_val": jnp.clip(0.0009765625 * jax.random.uniform(seeds[4], (NODES // 128, K, 128, 128), jnp.float32) ** shard_levels(seeds[4], (NODES // 128, K, 128, 128), ((0, 64),), -0.2, 0.2), 0.0, 0.0009765625).astype(jnp.bfloat16),
        "labels": place_ends(jax.random.randint(seeds[5], (NODES,), 0, CLASSES), jax.random.fold_in(seeds[5], 1), 0, CLASSES - 1).astype(jnp.int32),
        "w_self1": centred(seeds[6], (F_IN, HID), F_IN ** -0.5, 0.5, ((0, 4),)),
        "w_neigh1": centred(seeds[7], (F_IN, HID), F_IN ** -0.5, 0.5, ((0, 4),)),
        "w_self2": draw_w_self2(jax.random.fold_in(seeds[10], 71), 0),
        "w_neigh2": centred(seeds[9], (HID, CLASSES), HID ** -0.5, 0.1875, ((0, 4),)),
    }


def halo_rows(values, send_rows, send_count, dest_part):
    slot_total = send_rows.shape[2]
    offsets = (jnp.arange(N_NODE, dtype=jnp.int32) * NODE_DEV)[:, None]
    row_index = (send_rows[:, dest_part, :] + offsets).reshape(-1).astype(jnp.int32)
    picked = jnp.take(values, row_index, axis=0)
    in_use = (jnp.arange(slot_total, dtype=jnp.int32)[None, :] < send_count[:, dest_part][:, None]).reshape(-1)
    return (jnp.where(in_use[:, None], picked, jnp.zeros_like(picked)), row_index, in_use)

def aggregate_all(values, send_rows, send_count, tile_src, tile_val):
    col_count = values.shape[1]
    part_src = tile_src.reshape(N_NODE, NODE_DEV // 128, K)
    part_val = tile_val.reshape(N_NODE, NODE_DEV // 128, K, 128, 128)

    def one_part(packed):
        dest_part, src_ids, tile_block = packed
        own_rows = lax.dynamic_slice_in_dim(values, dest_part * NODE_DEV, NODE_DEV, 0)
        arrived = halo_rows(values, send_rows, send_count, dest_part)[0]
        blocks = jnp.concatenate([own_rows, arrived], 0).reshape(-1, 128, col_count)
        chosen = jnp.take(blocks, src_ids, axis=0)
        summed = jnp.einsum('bkij,bkjh->bih', tile_block.astype(jnp.float32), chosen.astype(jnp.float32), precision=lax.Precision.HIGHEST)
        return summed.reshape(NODE_DEV, col_count).astype(jnp.bfloat16)
    result = lax.map(one_part, (jnp.arange(N_NODE, dtype=jnp.int32), part_src, part_val))
    return result.reshape(N_NODE * NODE_DEV, col_count)

def spread_all(grads, send_rows, send_count, tile_src, tile_val):
    col_count = grads.shape[1]
    src_total = NODE_DEV + N_NODE * CAP
    block_total = src_total // 128
    part_src = tile_src.reshape(N_NODE, NODE_DEV // 128, K)
    part_val = tile_val.reshape(N_NODE, NODE_DEV // 128, K, 128, 128)

    def one_part(carried, packed):
        dest_part, src_ids, tile_block = packed
        own_grads = lax.dynamic_slice_in_dim(grads, dest_part * NODE_DEV, NODE_DEV, 0)
        per_tile = jnp.einsum('bkij,bih->bkjh', tile_block.astype(jnp.float32), own_grads.reshape(-1, 128, col_count).astype(jnp.float32), precision=lax.Precision.HIGHEST)
        one_hot = (src_ids.reshape(-1)[None, :] == jnp.arange(block_total, dtype=jnp.int32)[:, None]).astype(jnp.float32)
        landed = jnp.dot(one_hot, per_tile.reshape(one_hot.shape[1], -1), precision=lax.Precision.HIGHEST, preferred_element_type=jnp.float32).reshape(src_total, col_count)
        own_index = (dest_part * NODE_DEV + jnp.arange(NODE_DEV, dtype=jnp.int32)).astype(jnp.int32)
        carried = carried.at[own_index].add(landed[:NODE_DEV])
        unused, row_index, in_use = halo_rows(grads, send_rows, send_count, dest_part)
        halo_part = jnp.where(in_use[:, None], landed[NODE_DEV:], jnp.zeros_like(landed[NODE_DEV:]))
        carried = carried.at[row_index].add(halo_part)
        return (carried, None)
    start_value = jnp.zeros((N_NODE * NODE_DEV, col_count), jnp.float32)
    result, unused = lax.scan(one_part, start_value, (jnp.arange(N_NODE, dtype=jnp.int32), part_src, part_val))
    return result

def cross_entropy(logits, labels, grad_scale):
    row_max = lax.optimization_barrier(jnp.max(logits, axis=1, keepdims=True))
    shifted = logits - row_max
    total_exp = lax.optimization_barrier(jnp.sum(jnp.exp(shifted), axis=1, keepdims=True))
    classes = jnp.arange(logits.shape[1], dtype=jnp.int32)
    target = (labels[:, None] == classes[None, :]).astype(jnp.float32)
    row_loss = jnp.log(total_exp)[:, 0] - lax.optimization_barrier(jnp.sum(shifted * target, axis=1))
    grads = ((jnp.exp(shifted) / total_exp - target) * grad_scale).astype(jnp.bfloat16)
    return (row_loss, grads)

def reference(features, send_rows, send_count, tile_src, tile_val, labels, w_self1, w_neigh1, w_self2, w_neigh2):
    node_total = N_NODE * NODE_DEV
    agg_one = aggregate_all(features, send_rows, send_count, tile_src, tile_val)
    pre_act = jnp.dot(features, w_self1, preferred_element_type=jnp.float32)
    pre_act = pre_act + jnp.dot(agg_one, w_neigh1, preferred_element_type=jnp.float32)
    activated, pullback = jax.vjp(lambda inner: jax.nn.gelu(inner, approximate=True), pre_act)
    hidden = activated.astype(jnp.bfloat16)
    agg_two = aggregate_all(hidden, send_rows, send_count, tile_src, tile_val)
    logits = jnp.dot(hidden, w_self2, preferred_element_type=jnp.float32)
    logits = logits + jnp.dot(agg_two, w_neigh2, preferred_element_type=jnp.float32)
    grad_scale = float(node_total) ** (-0.5)
    row_loss, dlogits = cross_entropy(logits, labels, grad_scale)
    mean_loss = jnp.sum(row_loss) / node_total
    grad_self2 = jnp.dot(hidden.T, dlogits, preferred_element_type=jnp.float32)
    grad_neigh2 = jnp.dot(agg_two.T, dlogits, preferred_element_type=jnp.float32)
    back_grad = jnp.dot(dlogits, w_neigh2.T, preferred_element_type=jnp.float32).astype(jnp.bfloat16)
    direct = jnp.dot(dlogits, w_self2.T, preferred_element_type=jnp.float32)
    back_hidden = direct + spread_all(back_grad, send_rows, send_count, tile_src, tile_val)
    back_pre = pullback(back_hidden)[0].astype(jnp.bfloat16)
    grad_self1 = jnp.dot(features.T, back_pre, preferred_element_type=jnp.float32)
    grad_neigh1 = jnp.dot(agg_one.T, back_pre, preferred_element_type=jnp.float32)
    return (mean_loss, grad_self1, grad_neigh1, grad_self2, grad_neigh2)
```

```python
import functools
import math

import jax
import jax.numpy as jnp
from jax import lax
from jax.experimental import pallas as pl
from jax.experimental.pallas import tpu as pltpu
from jax.sharding import PartitionSpec as P

MESH = pl.DeviceIdType.MESH
F32 = jnp.float32
BF = jnp.bfloat16
ROWS = 512
SLOTS = 64
NODES = 64
FEATS = 4
CHIPS = NODES // 2
TILES = 64
BLOCKS = 36
CLS = 43
GELU_C = math.sqrt(2.0 / math.pi)


def g1_row(chip):
    y, z = chip // 8, chip % 8
    keep = (y + z) % 4
    rt = y * 2 + z // 4
    return (rt // 4) * 128 + 32 * keep + 8 * (rt % 4), keep, rt


def lane_roll(value, shift):
    shift = shift % value.shape[-1]
    return pltpu.roll(value, shift, value.ndim - 1) if shift else value


def dot(a, b):
    return jnp.dot(a, b, preferred_element_type=F32)


def step_kernel(
    grad_scale,
    table, xcat, slot_col, slot_row, tiles, labels, w1s, w1n, w2p,
    loss_ref, ogs1_ref, ogn1_ref, ogs2_ref, ogn2_ref,
    hot, hot_t, tiles_t, src, run, ptile,
    out1, recv1, xrecv, w1s_full, w1n_full, aggp, agg_recv, xfull, aggf,
    slope, hid, hid_t, xa_t, pf, ycat, ypack, yown, yrecv, spack, srecv,
    out2, recv2, stat, dlp, ret, recvb, gp, dg,
    dpart, dpeer, dsum, rrecv, rtile, trecv, fin01, fin2, half01, half2,
    s_x, r_x, s_w, r_w, s_e1, r_e1, s_agg, r_agg, s_y, r_y, s_s, r_s, s_e2, r_e2,
    s_st, r_st, s_dl, r_dl, s_eb, r_eb, s_g, r_g, s_d, r_d, s_rs, r_rs,
    s_t, r_t, s_f, r_f, s_f2, r_f2, s_h, r_h, s_h2, r_h2,
):
    me = lax.axis_index("node")
    f = lax.axis_index("feat")
    chip, core = me // 2, me % 2
    partner = me + 1 - 2 * core

    def wait_bytes(ref, sem):
        pltpu.make_async_copy(ref, ref, sem).wait()

    def send(s, d, ssem, rsem, node, feat):
        pltpu.make_async_remote_copy(
            src_ref=s, dst_ref=d, send_sem=ssem, recv_sem=rsem,
            device_id=(node, feat), device_id_type=MESH,
        ).start()

    def to_nodes(s, d, ssem, rsem):
        def body(i, c):
            p = lax.rem(me + i, NODES)
            send(s.at[p], d.at[me], ssem, rsem, p, f)
            return c
        lax.fori_loop(1, NODES, body, 0)

    def to_feats(s, d, ssem, rsem, same=False):
        for i in range(1, FEATS):
            g = lax.rem(f + i, FEATS)
            send(s if same else s.at[g], d.at[f], ssem, rsem, me, g)

    lane = lambda r, n=128: lax.broadcasted_iota(jnp.int32, (r, n), 1)

    bar = pltpu.get_barrier_semaphore()

    def hello(i, c):
        pl.semaphore_signal(bar, inc=1, device_id=(lax.rem(me + i, NODES), f), device_id_type=MESH)
        return c

    lax.fori_loop(1, NODES, hello, 0)
    for i in range(1, FEATS):
        pl.semaphore_signal(bar, inc=1, device_id=(me, lax.rem(f + i, FEATS)), device_id_type=MESH)

    def build_hot(d, c):
        col = jnp.sum(jnp.where(lane(SLOTS) == d, slot_col[...], 0), axis=1, keepdims=True)
        hot[d] = jnp.where(col == lane(SLOTS, ROWS), 1.0, 0.0).astype(BF)
        return c

    lax.fori_loop(0, NODES, build_hot, 0)

    def pack1(m, c):
        d0 = pl.multiple_of(m * 32, 32)
        acc = jnp.zeros((ROWS, 128), F32)
        for q in range(4):
            sel = hot[pl.ds(d0, 32), 16 * q:16 * q + 16, :].reshape(512, ROWS)
            acc = acc + dot(sel, xcat[q])
        out1[pl.ds(d0, 32)] = acc.astype(BF).reshape(32, 16, 128)
        return c

    lax.fori_loop(0, 2, pack1, 0)
    pl.semaphore_wait(bar, NODES - 1 + FEATS - 1)

    to_nodes(out1, recv1, s_e1, r_e1)
    for i in range(1, FEATS):
        g = lax.rem(f + i, FEATS)
        send(xcat.at[f], xrecv.at[f], s_x, r_x, me, g)
        send(w1s.at[g], w1s_full.at[f], s_w.at[0], r_w.at[0], me, g)
        send(w1n.at[g], w1n_full.at[f], s_w.at[1], r_w.at[1], me, g)

    recv1[me] = out1[me]
    xrecv[f] = xcat[f]
    w1s_full[f] = w1s[f]
    w1n_full[f] = w1n[f]
    for b in range(4):
        src[b] = xcat[0, 128 * b:128 * b + 128, :]

    def turn(t, c):
        tiles_t[t] = jnp.transpose(tiles[t])
        return c

    lax.fori_loop(0, TILES, turn, 0)

    def build_hot_t(m, c):
        r0 = pl.multiple_of(m * 64, 64)
        rows = lax.broadcasted_iota(jnp.int32, (64, 2048), 0) + r0
        for h in range(2):
            hot_t[h, pl.ds(r0, 64), :] = jnp.where(rows == slot_row[h:h + 1, :], 1.0, 0.0).astype(BF)
        return c

    lax.fori_loop(0, 8, build_hot_t, 0)

    wait_bytes(recv1.at[pl.ds(0, NODES - 1)], r_e1)

    def unpack1(j, c):
        for p in range(2):
            v = recv1[2 * j + p].astype(F32)
            for q in range(4):
                src[4 + j, 64 * p + 16 * q:64 * p + 16 * q + 16, :] = lane_roll(v, -32 * q).astype(BF)
        return c

    lax.fori_loop(0, 32, unpack1, 0)

    def tile_product(b):
        lhs = jnp.concatenate([tiles[16 * b + k] for k in range(16)], axis=1)
        rhs = jnp.concatenate([src[table[16 * b + k]] for k in range(16)], axis=0)
        return dot(lhs, rhs)

    packed = jnp.zeros((128, 128), F32)
    group = lane(128) // 32
    for b in range(4):
        packed = packed + lane_roll(jnp.where(group == 0, tile_product(b), 0.0), 32 * b)
    aggp[...] = packed.astype(BF)
    to_feats(aggp, agg_recv, s_agg, r_agg, same=True)
    agg_recv[f] = aggp[...]

    wait_bytes(xrecv.at[pl.ds(0, FEATS - 1)], r_x)
    wait_bytes(w1s_full.at[pl.ds(0, FEATS - 1)], r_w.at[0])
    wait_bytes(w1n_full.at[pl.ds(0, FEATS - 1)], r_w.at[1])
    xf = xrecv[0] + xrecv[1] + xrecv[2] + xrecv[3]
    xfull[...] = xf
    wait_bytes(agg_recv.at[pl.ds(0, FEATS - 1)], r_agg)
    for b in range(4):
        acc = jnp.zeros((128, 128), F32)
        for g in range(4):
            acc = jnp.where(group == g, lane_roll(agg_recv[g].astype(F32), 32 * (g - b)), acc)
        aggf[128 * b:128 * b + 128, :] = acc.astype(BF)

    pre = dot(xfull[...], w1s_full[...].reshape(128, 256)) + dot(aggf[...], w1n_full[...].reshape(128, 256))
    th = jnp.tanh(GELU_C * (pre + 0.044715 * (pre * pre * pre)))
    cdf = 0.5 * (1.0 + th)
    slope[...] = cdf + pre * (0.5 * (1.0 - th * th)) * (GELU_C * (1.0 + 3.0 * 0.044715 * (pre * pre)))
    hid[...] = (pre * cdf).astype(BF)

    low256 = lane(256) < 64
    for g in range(4):
        v = dot(hid[...], w2p[:, 128 * g:128 * g + 128])
        va, vb = v[0:256], v[256:512]
        yv = jnp.where(low256, lane_roll(va, 64), vb)
        yown[g] = yv
        ypack[g] = yv.astype(BF)
        spack[g] = jnp.where(low256, va, lane_roll(vb, 64))
    to_feats(ypack, yrecv, s_y, r_y)
    to_feats(spack, srecv, s_s, r_s)
    yrecv[f] = jnp.zeros((256, 128), BF)
    srecv[f] = spack[f]
    wait_bytes(yrecv.at[pl.ds(0, FEATS - 1)], r_y)
    ys = yown[f]
    for g in range(4):
        ys = ys + yrecv[g].astype(F32)
    yr = lane_roll(ys, 64)
    ycat[0, 0:256, :] = jnp.where(low256, ys, 0.0).astype(BF)
    ycat[0, 256:512, :] = jnp.where(low256, yr, 0.0).astype(BF)
    ycat[1, 0:256, :] = jnp.where(low256, 0.0, yr).astype(BF)
    ycat[1, 256:512, :] = jnp.where(low256, 0.0, ys).astype(BF)

    def pack2(m, c):
        d0 = pl.multiple_of(m * 16, 16)
        acc = dot(hot[pl.ds(d0, 16), 0:32, :].reshape(512, ROWS), ycat[0])
        acc = acc + dot(hot[pl.ds(d0, 16), 32:64, :].reshape(512, ROWS), ycat[1])
        out2[pl.ds(d0, 16)] = acc.astype(BF).reshape(16, 32, 128)
        return c

    lax.fori_loop(0, 4, pack2, 0)
    to_nodes(out2, recv2, s_e2, r_e2)

    recv2[me] = out2[me]
    for b in range(4):
        src[b] = ycat[0, 128 * b:128 * b + 128, :]
    hid_t[...] = jnp.transpose(hid[...])
    xa_t[0:128, :] = jnp.transpose(xfull[...])
    xa_t[128:256, :] = jnp.transpose(aggf[...])

    wait_bytes(recv2.at[pl.ds(0, NODES - 1)], r_e2)

    def unpack2(j, c):
        for p in range(2):
            v = recv2[2 * j + p]
            src[4 + j, 64 * p:64 * p + 32, :] = v
            src[4 + j, 64 * p + 32:64 * p + 64, :] = lane_roll(v.astype(F32), 64).astype(BF)
        return c

    lax.fori_loop(0, 32, unpack2, 0)

    wait_bytes(srecv.at[pl.ds(0, FEATS - 1)], r_s)
    ss = srecv[0] + srecv[1] + srecv[2] + srecv[3]
    pf[0, 0:256, :] = ss
    pf[0, 256:512, :] = lane_roll(ss, 64)

    mine = lane(128) < CLS
    lane128 = lane(128)
    for b in range(4):
        r = slice(128 * b, 128 * b + 128)
        lg = jnp.where(mine, pf[0, r, :] + tile_product(b), -1e30)
        top = jnp.max(lg, axis=1, keepdims=True)
        ex = jnp.exp(lg - top)
        tot = jnp.sum(ex, axis=1, keepdims=True)
        want = mine & ((labels[r, :] - CLS * f) == lane128)
        hit = jnp.sum(jnp.where(want, lg, 0.0), axis=1, keepdims=True)
        st = jnp.where(lane128 == 0, top, jnp.where(lane128 == 1, tot, jnp.where(lane128 == 2, hit, 0.0)))
        stat[f, :, r] = jnp.transpose(st)[0:8, :]
        pf[1, r, :] = ex
        pf[2, r, :] = jnp.where(want, 1.0, 0.0)
    to_feats(stat.at[f], stat, s_st, r_st, same=True)
    wait_bytes(stat.at[pl.ds(0, FEATS - 1)], r_st)

    tops = [stat[g, 0:1, :] for g in range(4)]
    best = jnp.maximum(jnp.maximum(tops[0], tops[1]), jnp.maximum(tops[2], tops[3]))
    total = jnp.zeros_like(best)
    hits = jnp.zeros_like(best)
    for g in range(4):
        total = total + stat[g, 1:2, :] * jnp.exp(tops[g] - best)
        hits = hits + stat[g, 2:3, :]
    loss = jnp.sum(jnp.log(total) + best - hits)
    factor = jnp.exp(stat[f, 0:1, :] - best) / total
    factor = jnp.broadcast_to(factor, (128, ROWS))
    for b in range(4):
        r = slice(128 * b, 128 * b + 128)
        fac = jnp.transpose(factor[:, 128 * b:128 * b + 128])
        d = (pf[1, r, :] * fac - pf[2, r, :]) * grad_scale
        dl = d.astype(BF)
        hi = b // 2
        rows = slice(128 * (b % 2), 128 * (b % 2) + 128)
        if hi == 0:
            dlp[f, rows, :] = dl
        else:
            dlp[f, rows, :] = (dlp[f, rows, :].astype(F32) + lane_roll(dl.astype(F32), 64)).astype(BF)
        lhs = tiles_t[16 * b:16 * b + 16].reshape(2048, 128)
        ptile[16 * b:16 * b + 16] = dot(lhs, dl).reshape(16, 128, 128)
    to_feats(dlp.at[f], dlp, s_dl, r_dl, same=True)

    def gather_sum(t, acc):
        keep = table[128 + t].astype(F32)
        acc = acc * keep + ptile[table[64 + t]]
        run[t] = acc
        return acc

    lax.fori_loop(0, TILES, gather_sum, jnp.zeros((128, 128), F32))

    def landed(j):
        return run[table[192 + j]] * table[256 + j].astype(F32)

    def pack_back(j, c):
        blk = landed(4 + j)
        for p in range(2):
            v = blk[64 * p:64 * p + 32, :] + lane_roll(blk[64 * p + 32:64 * p + 64, :], 64)
            ret[2 * j + p] = v.astype(BF)
        return c

    lax.fori_loop(0, 32, pack_back, 0)
    to_nodes(ret, recvb, s_eb, r_eb)
    recvb[me] = ret[me]
    for b in range(4):
        pf[3, 128 * b:128 * b + 128, :] = landed(b)

    wait_bytes(recvb.at[pl.ds(0, NODES - 1)], r_eb)
    back = recvb[...].reshape(2048, 128)
    low = lane(ROWS) < 64
    g_sum = pf[3] + jnp.where(low, dot(hot_t[0], back), 0.0)
    g_sum = g_sum + jnp.where(low, lane_roll(dot(hot_t[1], back), 64), 0.0)
    gp[f] = (g_sum[0:256] + lane_roll(g_sum[256:512], 64)).astype(BF)
    to_feats(gp.at[f], gp, s_g, r_g, same=True)
    wait_bytes(dlp.at[pl.ds(0, FEATS - 1)], r_dl)
    wait_bytes(gp.at[pl.ds(0, FEATS - 1)], r_g)
    for g in range(4):
        a, b = dlp[g].astype(F32), gp[g].astype(F32)
        dg[0:256, 128 * g:128 * g + 128] = jnp.where(low256, a, lane_roll(b, 64)).astype(BF)
        dg[256:512, 128 * g:128 * g + 128] = jnp.where(low256, lane_roll(a, 64), b).astype(BF)

    bh = lax.dot_general(dg[...], w2p[...], (((1,), (1,)), ((), ())), preferred_element_type=F32)
    bp = (bh * slope[...]).astype(BF)
    g1 = dot(xa_t[...], bp)
    g2 = dot(hid_t[...], dg[...])
    lane2 = lane(256, 256)
    zero = jnp.zeros((256, 128), F32)
    first = (lax.broadcasted_iota(jnp.int32, (256, 256), 0) == 0) & (lane2 == 255)
    gs2 = jnp.where(first, loss, 0.0)
    gn2 = jnp.zeros((256, 256), F32)
    l1 = lane(256)
    for g in range(4):
        blk = g2[:, 128 * g:128 * g + 128]
        s_part = jnp.concatenate([jnp.where(l1 < CLS, blk, 0.0), zero], axis=1)
        n_part = jnp.concatenate([jnp.where(l1 < 64, 0.0, blk), zero], axis=1)
        gs2 = gs2 + lane_roll(s_part, CLS * g)
        gn2 = gn2 + lane_roll(n_part, CLS * g - 64)
    for l in range(2):
        c = slice(128 * l, 128 * l + 128)
        dpart[l, :, 0] = gs2[:, c].reshape(CHIPS, 8, 128)
        dpart[l, :, 1] = gn2[:, c].reshape(CHIPS, 8, 128)
        for ch in range(CHIPS):
            r0 = g1_row(ch)[0]
            dpart[l, ch, 2] = g1[r0:r0 + 8, c]

    send(dpart.at[1 - core], dpeer, s_d, r_d, partner, f)
    wait_bytes(dpeer, r_d)
    dsum[...] = dpart[core] + dpeer[...]

    def scatter(i, c):
        p = lax.rem(chip + i, CHIPS)
        send(dsum.at[p], rrecv.at[chip], s_rs, r_rs, 2 * p + core, f)
        return c

    lax.fori_loop(1, CHIPS, scatter, 0)
    rrecv[chip] = dsum[chip]
    wait_bytes(rrecv.at[pl.ds(0, CHIPS - 1)], r_rs)
    rtile[...] = jnp.sum(rrecv[...], axis=0)

    y, z = chip // 8, lax.rem(chip, 8)
    keep = lax.rem(y + z, 4)
    rt = y * 2 + z // 4
    mine_keep = keep == f

    @pl.when(jnp.logical_not(mine_keep))
    def _():
        send(rtile.at[2], trecv.at[f], s_t, r_t, me, keep)

    def spread01(i, c):
        p = lax.rem(chip + i, CHIPS)
        send(rtile.at[pl.ds(0, 2)], fin01.at[chip], s_f, r_f, 2 * p + core, f)
        return c

    lax.fori_loop(1, CHIPS, spread01, 0)
    fin01[chip] = rtile[0:2]

    @pl.when(mine_keep)
    def _():
        trecv[f] = rtile[2]
        wait_bytes(trecv.at[pl.ds(0, FEATS - 1)], r_t)

        def spread2(i, c):
            p = lax.rem(chip + i, CHIPS)
            send(trecv, fin2.at[rt], s_f2, r_f2, 2 * p + core, f)
            return c

        lax.fori_loop(1, CHIPS, spread2, 0)
        fin2[rt] = trecv[...]
        wait_bytes(fin2.at[pl.ds(0, 7)], r_f2)

    @pl.when(jnp.logical_not(mine_keep))
    def _():
        wait_bytes(fin2, r_f2)

    send(fin2, half2, s_h2, r_h2, partner, f)
    wait_bytes(fin01.at[pl.ds(0, CHIPS - 1)], r_f)
    send(fin01, half01, s_h, r_h, partner, f)

    def emit(l, a01, a2):
        for blk, ref in ((0, ogs2_ref), (1, ogn2_ref)):
            v = a01[:, blk].reshape(256, 128)
            if l == 0:
                ref[:, 0:128] = v
            else:
                ref[:, 128:172] = v[:, 0:44]
                if blk == 0:
                    loss_ref[...] = v[0:8, :]
        for g in range(4):
            cols = slice(256 * g + 128 * l, 256 * g + 128 * l + 128)
            ogs1_ref[:, cols] = a2[0:4, g].reshape(32, 128)
            ogn1_ref[:, cols] = a2[4:8, g].reshape(32, 128)

    @pl.when(core == 0)
    def _():
        emit(0, fin01[...], fin2[...])

    @pl.when(core == 1)
    def _():
        emit(1, fin01[...], fin2[...])

    wait_bytes(half2, r_h2)
    wait_bytes(half01, r_h)

    @pl.when(core == 0)
    def _():
        emit(1, half01[...], half2[...])

    @pl.when(core == 1)
    def _():
        emit(0, half01[...], half2[...])

    n63, f3, c31 = pl.ds(0, NODES - 1), pl.ds(0, FEATS - 1), pl.ds(0, CHIPS - 1)
    wait_bytes(recv1.at[n63], s_e1)
    wait_bytes(xrecv.at[f3], s_x)
    wait_bytes(w1s_full.at[f3], s_w.at[0])
    wait_bytes(w1n_full.at[f3], s_w.at[1])
    wait_bytes(agg_recv.at[f3], s_agg)
    wait_bytes(yrecv.at[f3], s_y)
    wait_bytes(srecv.at[f3], s_s)
    wait_bytes(recv2.at[n63], s_e2)
    wait_bytes(stat.at[f3], s_st)
    wait_bytes(dlp.at[f3], s_dl)
    wait_bytes(recvb.at[n63], s_eb)
    wait_bytes(gp.at[f3], s_g)
    wait_bytes(dpeer, s_d)
    wait_bytes(rrecv.at[c31], s_rs)
    wait_bytes(fin01.at[c31], s_f)
    wait_bytes(half2, s_h2)
    wait_bytes(half01, s_h)

    @pl.when(jnp.logical_not(mine_keep))
    def _():
        wait_bytes(trecv.at[0], s_t)

    @pl.when(mine_keep)
    def _():
        wait_bytes(ptile.at[pl.ds(0, CHIPS - 1), pl.ds(0, 32)], s_f2)


def tile_table(tile_src):
    src = tile_src.reshape(-1)
    spot = jnp.arange(TILES, dtype=jnp.int32)
    before = (src[None, :] < src[:, None]) | ((src[None, :] == src[:, None]) & (spot[None, :] < spot[:, None]))
    rank = jnp.sum(before.astype(jnp.int32), axis=1)
    at = rank[:, None] == spot[None, :]
    order = jnp.sum(jnp.where(at, spot[:, None], 0), axis=0)
    same = (src[None, :] == src[:, None]) & (spot[None, :] < spot[:, None])
    goes_on_own = jnp.any(same, axis=1).astype(jnp.int32)
    goes_on = jnp.sum(jnp.where(at, goes_on_own[:, None], 0), axis=0)
    block = jnp.arange(TILES, dtype=jnp.int32)
    last = jnp.maximum(jnp.sum((src[None, :] <= block[:, None]).astype(jnp.int32), axis=1) - 1, 0)
    filled = jnp.any(src[None, :] == block[:, None], axis=1).astype(jnp.int32)
    return jnp.concatenate([src, order, goes_on, last, filled])


def shards(features, send_rows, send_count, tile_src, tile_val, labels, w_self1, w_neigh1, w_self2, w_neigh2):
    grad_scale = 1.0 / math.sqrt(ROWS * NODES)
    used = jnp.arange(SLOTS, dtype=jnp.int32)[None, :] < send_count[0][:, None]
    slots = jnp.where(used, send_rows[0], -1)
    slot_col = jnp.pad(slots.T, ((0, 0), (0, 64)))
    slot_row = slots.reshape(NODES, 2, 32).transpose(1, 0, 2).reshape(2, 2048)
    xcat = jnp.stack([jnp.pad(features, ((0, 0), (32 * q, 96 - 32 * q))) for q in range(4)])
    split1 = lambda w: w.reshape(32, FEATS, 256).transpose(1, 0, 2)
    pad2 = lambda w: jnp.pad(w.reshape(256, FEATS, 1, CLS), ((0, 0), (0, 0), (0, 0), (0, 64 - CLS)))
    w2p = jnp.concatenate([pad2(w_self2), pad2(w_neigh2)], axis=2).reshape(256, 512)
    vm = lambda *shape, dt=F32: pltpu.VMEM(shape, dt)
    dma = pltpu.SemaphoreType.DMA
    whole = pl.BlockSpec(memory_space=pltpu.VMEM)
    loss, gs1, gn1, gs2, gn2 = pl.pallas_call(
        functools.partial(step_kernel, grad_scale),
        out_shape=(
            jax.ShapeDtypeStruct((8, 128), F32),
            jax.ShapeDtypeStruct((32, 1024), F32),
            jax.ShapeDtypeStruct((32, 1024), F32),
            jax.ShapeDtypeStruct((256, 172), F32),
            jax.ShapeDtypeStruct((256, 172), F32),
        ),
        in_specs=[pl.BlockSpec(memory_space=pltpu.SMEM)] + [whole] * 8,
        out_specs=(whole,) * 5,
        scratch_shapes=[
            vm(64, 64, 512, dt=BF), vm(2, 512, 2048, dt=BF), vm(64, 128, 128, dt=BF), vm(36, 128, 128, dt=BF),
            vm(64, 128, 128), vm(64, 128, 128),
            vm(64, 16, 128, dt=BF), vm(64, 16, 128, dt=BF), vm(4, 512, 128, dt=BF),
            vm(4, 32, 256, dt=BF), vm(4, 32, 256, dt=BF), vm(128, 128, dt=BF), vm(4, 128, 128, dt=BF),
            vm(512, 128, dt=BF), vm(512, 128, dt=BF),
            vm(512, 256), vm(512, 256, dt=BF), vm(256, 512, dt=BF), vm(256, 512, dt=BF), vm(4, 512, 128),
            vm(2, 512, 128, dt=BF), vm(4, 256, 128, dt=BF), vm(4, 256, 128), vm(4, 256, 128, dt=BF),
            vm(4, 256, 128), vm(4, 256, 128),
            vm(64, 32, 128, dt=BF), vm(64, 32, 128, dt=BF), vm(4, 8, 512), vm(4, 256, 128, dt=BF),
            vm(64, 32, 128, dt=BF), vm(64, 32, 128, dt=BF), vm(4, 256, 128, dt=BF), vm(512, 512, dt=BF),
            vm(2, 32, 3, 8, 128), vm(32, 3, 8, 128), vm(32, 3, 8, 128), vm(32, 3, 8, 128), vm(3, 8, 128),
            vm(4, 8, 128), vm(32, 2, 8, 128), vm(8, 4, 8, 128), vm(32, 2, 8, 128), vm(8, 4, 8, 128),
            dma, dma, dma((2,)), dma((2,)),
        ] + [dma] * 32,
        compiler_params=pltpu.CompilerParams(
            collective_id=0, has_side_effects=True, vmem_limit_bytes=56 * 1024 * 1024
        ),
    )(
        tile_table(tile_src), xcat, slot_col, slot_row, tile_val.reshape(TILES, 128, 128), labels[:, None],
        split1(w_self1), split1(w_neigh1), w2p,
    )
    return (loss[0, 127] / (ROWS * NODES), gs1, gn1, gs2, gn2)


def solution(mesh):
    in_specs = (
        P("node", "feat"),
        P("node", None, None),
        P("node", None),
        P("node", None),
        P("node", None, None, None),
        P("node"),
        P("feat", None),
        P("feat", None),
        P("feat", None),
        P("feat", None),
    )
    out_specs = (P(), P("feat", None), P("feat", None), P("feat", None), P("feat", None))
    return jax.shard_map(shards, mesh=mesh, in_specs=in_specs, out_specs=out_specs, check_vma=False)
```

```python
import functools
import math

import jax
import jax.numpy as jnp
from jax import lax
from jax.experimental import pallas as pl
from jax.experimental.pallas import tpu as pltpu
from jax.sharding import PartitionSpec as P

MESH = pl.DeviceIdType.MESH
F32 = jnp.float32
BF = jnp.bfloat16
I32 = jnp.int32
ROWS = 512
SLOTS = 64
NODES = 64
FEATS = 4
CHIPS = NODES // 2
RINGS = 4
TILES = 64
CLASSES = 172
CLS = 43
TALL = 176
CLS_TILES = TALL // 8
GELU_C = math.sqrt(2.0 / math.pi)


def lane_roll(value, shift):
    shift = shift % value.shape[-1]
    return pltpu.roll(value, shift, value.ndim - 1) if shift else value


def dot(a, b):
    return jnp.dot(a, b, preferred_element_type=F32)


def dot_nt(a, b):
    return lax.dot_general(a, b, (((1,), (1,)), ((), ())), preferred_element_type=F32)


def iota(shape, axis):
    return lax.broadcasted_iota(I32, shape, axis)


def g1_row(chip):
    y, z = chip // 8, chip % 8
    keep = (y + z) % 4
    rt = y * 2 + z // 4
    return (rt // 4) * 128 + 32 * keep + 8 * (rt % 4)


def step_kernel(
    grad_scale,
    tile_src, feat_t, send_rows, send_count, tiles_hbm, labels, w1s, w1n, w2s_t, w2n_t,
    fin_a, half_a, fin_b, half_b, fin_c, half_c,
    tiles, xcat, slot_col, wide, w2p_t, order_v, order,
    hot, hot_t, tiles_t, src, run, ptile,
    out1, recv1, xrecv, w1s_full, w1n_full, aggp, agg_recv, xfull, aggf,
    slope, hid, xa_t, pf, ycat, ypack, yown, yrecv, spack, srecv,
    out2, recv2, stat, dlp, ret, recvb, gp, dlcat, dlcat_t, gcat,
    da, pa, db, pb, dc, pc, ra, rb, rc, ta, tb, tc, trecv,
    s_tiles, s_order, s_x, r_x, s_w, r_w, s_e1, r_e1, s_agg, r_agg, s_y, r_y, s_s, r_s, s_e2, r_e2,
    s_st, r_st, s_dl, r_dl, s_eb, r_eb, s_g, r_g, s_pair, r_pair, s_red, r_red,
    s_t, r_t, s_fin, r_fin, s_half, r_half,
):
    me = lax.axis_index("node")
    f = lax.axis_index("feat")
    chip, core = me // 2, lax.rem(me, 2)
    ring, place = me // 16, lax.rem(me // 2, 8)
    partner = me + 1 - 2 * core

    def wait_bytes(ref, sem):
        pltpu.make_async_copy(ref, ref, sem).wait()

    def send(s, d, ssem, rsem, node, feat):
        pltpu.make_async_remote_copy(
            src_ref=s, dst_ref=d, send_sem=ssem, recv_sem=rsem,
            device_id=(node, feat), device_id_type=MESH,
        ).start()

    def to_feats(s, d, ssem, rsem, same=False):
        for i in (2, 1, 3):
            g = lax.rem(f + i, FEATS)
            send(s if same else s.at[g], d.at[f], ssem, rsem, me, g)

    def place_at(k):
        off = ((k + 1) // 2) * (2 * lax.rem(k, 2) - 1)
        return lax.rem(place + off + 8, 8)

    def ring_at(j):
        return lax.rem(ring + (2, 1, 3, 0)[j], RINGS)

    lane = lambda r, n=128: iota((r, n), 1)
    three = pl.ds(0, FEATS - 1)

    load_tiles = pltpu.make_async_copy(tiles_hbm, tiles, s_tiles)
    load_tiles.start()

    bar = pltpu.get_barrier_semaphore()

    def hello(i, c):
        pl.semaphore_signal(bar, inc=1, device_id=(lax.rem(me + i, NODES), f), device_id_type=MESH)
        return c

    lax.fori_loop(1, NODES, hello, 0)
    for i in range(1, FEATS):
        pl.semaphore_signal(bar, inc=1, device_id=(me, lax.rem(f + i, FEATS)), device_id_type=MESH)

    x0 = jnp.transpose(jnp.concatenate([feat_t[...].astype(F32), jnp.zeros((96, ROWS), F32)], axis=0))
    for q in range(4):
        xcat[q] = lane_roll(x0, 32 * q).astype(BF)

    wide[0, 0:64, 0:64] = send_rows[...].astype(F32)
    turned = jnp.transpose(wide[0, 0:128, 0:128]).astype(I32)[0:64]
    counts = jnp.concatenate([send_count[...], jnp.zeros((1, 64), I32)], axis=1)
    slot_col[...] = jnp.where(iota((64, 128), 0) < counts, turned, -1)

    def build_hot(d, c):
        col = jnp.sum(jnp.where(lane(SLOTS) == d, slot_col[...], 0), axis=1, keepdims=True)
        hot[d] = jnp.where(col == lane(SLOTS, ROWS), 1.0, 0.0).astype(BF)
        return c

    lax.fori_loop(0, NODES, build_hot, 0, unroll=8)
    pl.semaphore_wait(bar, NODES - 1 + FEATS - 1)

    for j in range(RINGS):
        rr = ring_at(j)
        d0 = pl.multiple_of(rr * 16, 16)
        acc = jnp.zeros((256, 128), F32)
        for q in range(4):
            acc = acc + dot(hot[pl.ds(d0, 16), 16 * q:16 * q + 16, :].reshape(256, ROWS), xcat[q])
        out1[pl.ds(d0, 16)] = acc.astype(BF).reshape(16, 16, 128)

        def send1(k, c):
            k = (16 if j < 3 else 15) - 1 - k + (0 if j < 3 else 1)
            p = rr * 16 + place_at(k // 2) * 2 + lax.rem(core + k, 2)
            send(out1.at[p], recv1.at[me], s_e1, r_e1.at[ring], p, f)
            return c

        lax.fori_loop(0, 16 if j < 3 else 15, send1, 0)
    for i in (2, 1, 3):
        g = lax.rem(f + i, FEATS)
        cols = pl.ds(pl.multiple_of(g * 256, 256), 256)
        send(xcat.at[f], xrecv.at[f], s_x, r_x, me, g)
        send(w1s.at[:, cols], w1s_full.at[f], s_w.at[0], r_w.at[0], me, g)
        send(w1n.at[:, cols], w1n_full.at[f], s_w.at[1], r_w.at[1], me, g)

    recv1[me] = out1[me]
    xrecv[f] = xcat[f]
    own_cols = pl.ds(pl.multiple_of(f * 256, 256), 256)
    w1s_full[f] = w1s[:, own_cols]
    w1n_full[f] = w1n[:, own_cols]
    for b in range(4):
        src[b] = xcat[0, 128 * b:128 * b + 128, :]

    for part, ref in enumerate((w2s_t, w2n_t)):
        wide[0, 0:CLASSES, 0:256] = ref[...].astype(F32)
        wide[1] = jnp.zeros((256, 256), F32)
        for g in range(4):
            wide[1, 64 * g:64 * g + CLS, :] = wide[0, CLS * g:CLS * g + CLS, 0:256]
        w2p_t[256 * part:256 * part + 256, :] = wide[1].astype(BF)

    srow = jnp.full((128, 128), 1 << 20, I32)
    for t in range(TILES):
        srow = jnp.where(lane(128) == t, tile_src[t // 16, t % 16], srow)
    scol = jnp.transpose(srow)
    sub = iota((128, 128), 0)
    lane128 = lane(128)
    same = (srow == scol) & (lane128 < sub)
    rank = jnp.sum(jnp.where((srow < scol) | same, 1, 0), axis=1, keepdims=True)
    goes = jnp.minimum(jnp.sum(jnp.where(same, 1, 0), axis=1, keepdims=True), 1)
    at = rank == lane128
    order_v[...] = jnp.zeros((8, 128), I32)
    order_v[0:1, :] = jnp.sum(jnp.where(at, sub, 0), axis=0, keepdims=True)
    order_v[1:2, :] = jnp.sum(jnp.where(at, goes, 0), axis=0, keepdims=True)
    upto = jnp.sum(jnp.where(scol <= lane128, 1, 0), axis=0, keepdims=True)
    order_v[2:3, :] = jnp.maximum(upto - 1, 0)
    order_v[3:4, :] = jnp.minimum(jnp.sum(jnp.where(scol == lane128, 1, 0), axis=0, keepdims=True), 1)
    order_copy = pltpu.make_async_copy(order_v, order, s_order)
    order_copy.start()

    load_tiles.wait()

    def turn(t, c):
        tiles_t[t] = jnp.transpose(tiles[t])
        return c

    lax.fori_loop(0, TILES, turn, 0, unroll=4)
    order_copy.wait()

    def row_bytes(buf, j):
        return buf.at[pl.ds(0, 15 if j == 3 else 16)]

    for j in (3, 1, 2, 0):
        rr = ring_at(j)
        wait_bytes(row_bytes(recv1, j), r_e1.at[rr])

        def unpack1(k, c):
            b = rr * 8 + k
            for p in range(2):
                v = recv1[2 * b + p].astype(F32)
                for q in range(4):
                    src[4 + b, 64 * p + 16 * q:64 * p + 16 * q + 16, :] = lane_roll(v, -32 * q).astype(BF)
            return c

        lax.fori_loop(0, 8, unpack1, 0, unroll=4)

    def tile_product(b):
        lhs = jnp.concatenate([tiles[16 * b + k] for k in range(16)], axis=1)
        rhs = jnp.concatenate([src[tile_src[b, k]] for k in range(16)], axis=0)
        return dot(lhs, rhs)

    packed = jnp.zeros((128, 128), F32)
    group = lane128 // 32
    for b in range(4):
        packed = packed + lane_roll(jnp.where(group == 0, tile_product(b), 0.0), 32 * b)
    aggp[...] = packed.astype(BF)
    to_feats(aggp, agg_recv, s_agg, r_agg, same=True)
    agg_recv[f] = aggp[...]

    wait_bytes(xrecv.at[three], r_x)
    wait_bytes(w1s_full.at[three], r_w.at[0])
    wait_bytes(w1n_full.at[three], r_w.at[1])
    xfull[...] = xrecv[0] + xrecv[1] + xrecv[2] + xrecv[3]
    pre0 = dot(xfull[...], w1s_full[...].reshape(128, 256))
    wait_bytes(agg_recv.at[three], r_agg)
    for b in range(4):
        acc = jnp.zeros((128, 128), F32)
        for g in range(4):
            acc = jnp.where(group == g, lane_roll(agg_recv[g].astype(F32), 32 * (g - b)), acc)
        aggf[128 * b:128 * b + 128, :] = acc.astype(BF)

    pre = pre0 + dot(aggf[...], w1n_full[...].reshape(128, 256))
    th = jnp.tanh(GELU_C * (pre + 0.044715 * (pre * pre * pre)))
    cdf = 0.5 * (1.0 + th)
    slope[...] = cdf + pre * (0.5 * (1.0 - th * th)) * (GELU_C * (1.0 + 3.0 * 0.044715 * (pre * pre)))
    hid[...] = (pre * cdf).astype(BF)

    low256 = lane(256) < 64

    def pack_halves(v, g):
        a, b = v[0:256], v[256:512]
        return jnp.where(low256, a if g % 2 == 0 else lane_roll(a, 64), lane_roll(b, 64) if g % 2 == 0 else b)

    for half in range(2):
        v = dot_nt(hid[...], w2p_t[256 + 128 * half:256 + 128 * half + 128, :])
        for g in (2 * half, 2 * half + 1):
            yv = pack_halves(v, g)
            yown[g] = yv
            ypack[g] = yv.astype(BF)
    to_feats(ypack, yrecv, s_y, r_y)
    for half in range(2):
        v = dot_nt(hid[...], w2p_t[128 * half:128 * half + 128, :])
        for g in (2 * half, 2 * half + 1):
            spack[g] = pack_halves(v, g)
    to_feats(spack, srecv, s_s, r_s)
    yrecv[f] = jnp.zeros((256, 128), BF)
    srecv[f] = spack[f]
    wait_bytes(yrecv.at[three], r_y)
    ys = yown[f]
    for g in range(4):
        ys = ys + yrecv[g].astype(F32)
    yr = lane_roll(ys, 64)
    ycat[0, 0:256, :] = jnp.where(low256, ys, 0.0).astype(BF)
    ycat[0, 256:512, :] = jnp.where(low256, yr, 0.0).astype(BF)
    ycat[1, 0:256, :] = jnp.where(low256, 0.0, yr).astype(BF)
    ycat[1, 256:512, :] = jnp.where(low256, 0.0, ys).astype(BF)

    for j in range(RINGS):
        rr = ring_at(j)
        d0 = pl.multiple_of(rr * 16, 16)
        acc = dot(hot[pl.ds(d0, 16), 0:32, :].reshape(512, ROWS), ycat[0])
        acc = acc + dot(hot[pl.ds(d0, 16), 32:64, :].reshape(512, ROWS), ycat[1])
        out2[pl.ds(d0, 16)] = acc.astype(BF).reshape(16, 32, 128)

        def send2(k, c):
            k = (16 if j < 3 else 15) - 1 - k + (0 if j < 3 else 1)
            p = rr * 16 + place_at(k // 2) * 2 + lax.rem(core + k, 2)
            send(out2.at[p], recv2.at[me], s_e2, r_e2.at[ring], p, f)
            return c

        lax.fori_loop(0, 16 if j < 3 else 15, send2, 0)

    recv2[me] = out2[me]
    for b in range(4):
        src[b] = ycat[0, 128 * b:128 * b + 128, :]
    xa_t[0:128, :] = jnp.transpose(xfull[...])
    xa_t[128:256, :] = jnp.transpose(aggf[...])

    def turn_hot(y, c):
        d0 = pl.multiple_of(y * 16, 16)
        for h in range(2):
            for k in range(4):
                part = hot[pl.ds(d0, 16), 32 * h:32 * h + 32, 128 * k:128 * k + 128].reshape(512, 128)
                hot_t[y, h, 128 * k:128 * k + 128, :] = jnp.transpose(part)
        return c

    lax.fori_loop(0, RINGS, turn_hot, 0)

    for j in (3, 1, 2, 0):
        rr = ring_at(j)
        wait_bytes(row_bytes(recv2, j), r_e2.at[rr])

        def unpack2(k, c):
            b = rr * 8 + k
            for p in range(2):
                v = recv2[2 * b + p]
                src[4 + b, 64 * p:64 * p + 32, :] = v
                src[4 + b, 64 * p + 32:64 * p + 64, :] = lane_roll(v.astype(F32), 64).astype(BF)
            return c

        lax.fori_loop(0, 8, unpack2, 0, unroll=4)

    wait_bytes(srecv.at[three], r_s)
    ss = srecv[0] + srecv[1] + srecv[2] + srecv[3]
    pf[0, 0:256, :] = ss
    pf[0, 256:512, :] = lane_roll(ss, 64)

    mine = lane128 < CLS
    for b in range(4):
        r = slice(128 * b, 128 * b + 128)
        lg = jnp.where(mine, pf[0, r, :] + tile_product(b), -1e30)
        top = jnp.max(lg, axis=1, keepdims=True)
        ex = jnp.exp(lg - top)
        tot = jnp.sum(ex, axis=1, keepdims=True)
        lab = jnp.transpose(jnp.broadcast_to(labels[b:b + 1, :].astype(F32), (128, 128))).astype(I32)
        want = mine & ((lab - CLS * f) == lane128)
        hit = jnp.sum(jnp.where(want, lg, 0.0), axis=1, keepdims=True)
        st = jnp.where(lane128 == 0, top, jnp.where(lane128 == 1, tot, jnp.where(lane128 == 2, hit, 0.0)))
        stat[f, :, r] = jnp.transpose(st)[0:8, :]
        pf[1, r, :] = ex
        pf[2, r, :] = jnp.where(want, 1.0, 0.0)
    to_feats(stat.at[f], stat, s_st, r_st, same=True)
    wait_bytes(stat.at[three], r_st)

    tops = [stat[g, 0:1, :] for g in range(4)]
    best = jnp.maximum(jnp.maximum(tops[0], tops[1]), jnp.maximum(tops[2], tops[3]))
    total = jnp.zeros_like(best)
    hits = jnp.zeros_like(best)
    for g in range(4):
        total = total + stat[g, 1:2, :] * jnp.exp(tops[g] - best)
        hits = hits + stat[g, 2:3, :]
    loss = jnp.sum(jnp.log(total) + best - hits)
    factor = jnp.broadcast_to(jnp.exp(stat[f, 0:1, :] - best) / total, (128, ROWS))
    for b in range(4):
        r = slice(128 * b, 128 * b + 128)
        fac = jnp.transpose(factor[:, 128 * b:128 * b + 128])
        dl = ((pf[1, r, :] * fac - pf[2, r, :]) * grad_scale).astype(BF)
        rows = slice(128 * (b % 2), 128 * (b % 2) + 128)
        if b < 2:
            dlp[f, rows, :] = dl
        else:
            dlp[f, rows, :] = (dlp[f, rows, :].astype(F32) + lane_roll(dl.astype(F32), 64)).astype(BF)
        lhs = tiles_t[16 * b:16 * b + 16].reshape(2048, 128)
        ptile[16 * b:16 * b + 16] = dot(lhs, dl).reshape(16, 128, 128)
    to_feats(dlp.at[f], dlp, s_dl, r_dl, same=True)

    def gather_sum(t, acc):
        acc = acc * order[1, t].astype(F32) + ptile[order[0, t]]
        run[t] = acc
        return acc

    lax.fori_loop(0, TILES, gather_sum, jnp.zeros((128, 128), F32), unroll=4)

    def landed(j):
        return run[order[2, j]] * order[3, j].astype(F32)

    for j in range(RINGS):
        rr = ring_at(j)

        def pack_back(k, c):
            to = rr * 8 + place_at(7 - k)
            blk = landed(4 + to)
            for p in range(2):
                v = blk[64 * p:64 * p + 32, :] + lane_roll(blk[64 * p + 32:64 * p + 64, :], 64)
                ret[2 * to + p] = v.astype(BF)
            return c

        lax.fori_loop(0, 8, pack_back, 0, unroll=4)

        def send_back(k, c):
            k = (16 if j < 3 else 15) - 1 - k + (0 if j < 3 else 1)
            p = rr * 16 + place_at(k // 2) * 2 + lax.rem(core + k, 2)
            send(ret.at[p], recvb.at[me], s_eb, r_eb.at[ring], p, f)
            return c

        lax.fori_loop(0, 16 if j < 3 else 15, send_back, 0)

    recvb[me] = ret[me]
    for b in range(4):
        pf[3, 128 * b:128 * b + 128, :] = landed(b)

    def join(ref, out):
        for pair in range(2):
            c = slice(128 * pair, 128 * pair + 128)
            a, b = ref[2 * pair].astype(F32), ref[2 * pair + 1].astype(F32)
            out[0:256, c] = jnp.where(low256, a, lane_roll(b, 64)).astype(BF)
            out[256:512, c] = jnp.where(low256, lane_roll(a, 64), b).astype(BF)

    def class_rows(v, d):
        for l in range(2):
            d[l, TALL - 8:TALL, :] = jnp.zeros((8, 128), F32)
            for g in range(4):
                d[l, CLS * g:CLS * g + CLS, :] = v[64 * g:64 * g + CLS, 128 * l:128 * l + 128]

    def rows8(t):
        return pl.ds(pl.multiple_of(t * 8, 8), 8)

    def chip_at(i):
        return lax.rem(ring + (i // 8) + 4, RINGS) * 8 + place_at(lax.rem(i, 8))

    def for_chips(body):
        lax.fori_loop(1, CHIPS, lambda i, c: (body(chip_at(CHIPS - i)), c)[1], 0)

    def reduce_class(d, peer, part, k):
        wait_bytes(peer, r_pair.at[k])
        d[core] = d[core] + peer[...]

        def one(p):
            @pl.when(p < CLS_TILES)
            def _():
                send(d.at[core, rows8(p)], part.at[chip], s_red.at[k], r_red.at[k], 2 * p + core, f)

        for_chips(one)

        @pl.when(chip < CLS_TILES)
        def _():
            part[chip] = d[core, rows8(chip), :]

    def spread_class(part, tile, fin, k):
        @pl.when(chip < CLS_TILES)
        def _():
            wait_bytes(part.at[pl.ds(0, CHIPS - 1)], r_red.at[k])
            tile[...] = jnp.sum(part[...], axis=0)
            for_chips(lambda p: send(tile, fin.at[chip], s_fin.at[k], r_fin.at[k], 2 * p + core, f))
            fin[chip] = tile[...]

    def gather_class(fin, half, k):
        @pl.when(chip < CLS_TILES)
        def _():
            wait_bytes(fin.at[pl.ds(0, CLS_TILES - 1)], r_fin.at[k])

        @pl.when(chip >= CLS_TILES)
        def _():
            wait_bytes(fin, r_fin.at[k])

        send(fin, half, s_half.at[k], r_half.at[k], partner, f)

    wait_bytes(dlp.at[three], r_dl)
    join(dlp, dlcat)
    dlcat_t[...] = jnp.transpose(dlcat[...])
    class_rows(dot(dlcat_t[...], hid[...]), da)
    tail = (iota((8, 128), 0) == 7) & (lane(8) == 0)
    for l in range(2):
        da[l, TALL - 8:TALL, :] = da[l, TALL - 8:TALL, :] + jnp.where(tail, loss, 0.0)
    send(da.at[1 - core], pa, s_pair.at[0], r_pair.at[0], partner, f)
    reduce_class(da, pa, ra, 0)

    g_sum = pf[3]
    low = lane(ROWS) < 64
    for j in (3, 1, 2, 0):
        rr = ring_at(j)
        wait_bytes(row_bytes(recvb, j), r_eb.at[rr])
        back = recvb[pl.ds(pl.multiple_of(rr * 16, 16), 16)].reshape(512, 128)
        g_sum = g_sum + jnp.where(low, dot(hot_t[rr, 0], back), 0.0)
        g_sum = g_sum + jnp.where(low, lane_roll(dot(hot_t[rr, 1], back), 64), 0.0)
    gp[f] = (g_sum[0:256] + lane_roll(g_sum[256:512], 64)).astype(BF)
    to_feats(gp.at[f], gp, s_g, r_g, same=True)
    spread_class(ra, ta, fin_a, 0)
    bh0 = dot(dlcat[...], w2p_t[0:256, :])
    wait_bytes(gp.at[three], r_g)
    join(gp, gcat)

    class_rows(dot(jnp.transpose(gcat[...]), hid[...]), db)
    send(db.at[1 - core], pb, s_pair.at[1], r_pair.at[1], partner, f)
    bh = bh0 + dot(gcat[...], w2p_t[256:512, :])
    g1 = dot(xa_t[...], (bh * slope[...]).astype(BF))
    for l in range(2):
        for ch in range(CHIPS):
            dc[l, ch] = g1[g1_row(ch):g1_row(ch) + 8, 128 * l:128 * l + 128]
    send(dc.at[1 - core], pc, s_pair.at[2], r_pair.at[2], partner, f)
    wait_bytes(pc, r_pair.at[2])
    dc[core] = dc[core] + pc[...]
    for_chips(lambda p: send(dc.at[core, p], rc.at[chip], s_red.at[2], r_red.at[2], 2 * p + core, f))
    rc[chip] = dc[core, chip]
    reduce_class(db, pb, rb, 1)

    wait_bytes(rc.at[pl.ds(0, CHIPS - 1)], r_red.at[2])
    tc[...] = jnp.sum(rc[...], axis=0)
    keep = lax.rem(ring + place, 4)
    rt = ring * 2 + place // 4
    kept = keep == f

    @pl.when(jnp.logical_not(kept))
    def _():
        send(tc, trecv.at[f], s_t, r_t, me, keep)

    spread_class(rb, tb, fin_b, 1)

    @pl.when(kept)
    def _():
        trecv[f] = tc[...]
        wait_bytes(trecv.at[three], r_t)
        for_chips(lambda p: send(trecv, fin_c.at[rt], s_fin.at[2], r_fin.at[2], 2 * p + core, f))
        fin_c[rt] = trecv[...]

    gather_class(fin_a, half_a, 0)
    gather_class(fin_b, half_b, 1)

    @pl.when(kept)
    def _():
        wait_bytes(fin_c.at[pl.ds(0, 7)], r_fin.at[2])

    @pl.when(jnp.logical_not(kept))
    def _():
        wait_bytes(fin_c, r_fin.at[2])

    send(fin_c, half_c, s_half.at[2], r_half.at[2], partner, f)

    n63, c31 = pl.ds(0, NODES - 1), pl.ds(0, CHIPS - 1)
    wait_bytes(recv1.at[n63], s_e1)
    wait_bytes(xrecv.at[three], s_x)
    wait_bytes(w1s_full.at[three], s_w.at[0])
    wait_bytes(w1n_full.at[three], s_w.at[1])
    wait_bytes(agg_recv.at[three], s_agg)
    wait_bytes(yrecv.at[three], s_y)
    wait_bytes(srecv.at[three], s_s)
    wait_bytes(recv2.at[n63], s_e2)
    wait_bytes(stat.at[three], s_st)
    wait_bytes(dlp.at[three], s_dl)
    wait_bytes(recvb.at[n63], s_eb)
    wait_bytes(gp.at[three], s_g)
    wait_bytes(pa, s_pair.at[0])
    wait_bytes(pb, s_pair.at[1])
    wait_bytes(pc, s_pair.at[2])
    wait_bytes(rc.at[c31], s_red.at[2])
    for k, part in ((0, ra), (1, rb)):
        @pl.when(chip < CLS_TILES)
        def _():
            wait_bytes(part.at[pl.ds(0, CLS_TILES - 1)], s_red.at[k])
            wait_bytes(part.at[c31], s_fin.at[k])

        @pl.when(chip >= CLS_TILES)
        def _():
            wait_bytes(part.at[pl.ds(0, CLS_TILES)], s_red.at[k])

    @pl.when(jnp.logical_not(kept))
    def _():
        wait_bytes(trecv.at[0], s_t)

    @pl.when(kept)
    def _():
        wait_bytes(ptile.at[c31, pl.ds(0, 32)], s_fin.at[2])

    for k, ref in enumerate((half_a, half_b, half_c)):
        wait_bytes(ref, s_half.at[k])
        wait_bytes(ref, r_half.at[k])


def result_kernel(scale, fin_a, half_a, fin_b, half_b, fin_c, half_c, loss_ref, gs1_ref, gn1_ref, gs2_ref, gn2_ref):
    core = lax.rem(lax.axis_index("node"), 2)
    first = core == 0
    loss_ref[...] = fin_a[CLS_TILES - 1, 7:8, 0:1] * scale
    for l in range(2):
        c = slice(128 * l, 128 * l + 128)
        mine = first if l == 0 else jnp.logical_not(first)
        for fin, half, ref in ((fin_a, half_a, gs2_ref), (fin_b, half_b, gn2_ref)):
            ref[:, c] = jnp.where(mine, fin[...], half[...]).reshape(TALL, 128)[0:CLASSES]
        v = jnp.where(mine, fin_c[...], half_c[...])
        for g in range(4):
            cols = slice(256 * g + 128 * l, 256 * g + 128 * l + 128)
            gs1_ref[:, cols] = v[0:4, g].reshape(32, 128)
            gn1_ref[:, cols] = v[4:8, g].reshape(32, 128)


def shards(features, send_rows, send_count, tile_src, tile_val, labels, w_self1, w_neigh1, w_self2, w_neigh2):
    vm = lambda *shape, dt=F32: pltpu.VMEM(shape, dt)
    dma = pltpu.SemaphoreType.DMA
    whole = pl.BlockSpec(memory_space=pltpu.VMEM)
    half_class = jax.ShapeDtypeStruct((CLS_TILES, 8, 128), F32)
    half_first = jax.ShapeDtypeStruct((8, 4, 8, 128), F32)
    parts = pl.pallas_call(
        functools.partial(step_kernel, 1.0 / math.sqrt(ROWS * NODES)),
        out_shape=(half_class,) * 4 + (half_first,) * 2,
        in_specs=[pl.BlockSpec(memory_space=pltpu.SMEM)] + [whole] * 3 + [pl.BlockSpec(memory_space=pl.ANY)] + [whole] * 5,
        out_specs=(whole,) * 6,
        scratch_shapes=[
            vm(64, 128, 128, dt=BF), vm(4, 512, 128, dt=BF), vm(64, 128, dt=I32), vm(2, 256, 256),
            vm(512, 256, dt=BF), vm(8, 128, dt=I32), pltpu.SMEM((8, 128), I32),
            vm(64, 64, 512, dt=BF), vm(4, 2, 512, 512, dt=BF), vm(64, 128, 128, dt=BF), vm(36, 128, 128, dt=BF),
            vm(64, 128, 128), vm(64, 128, 128),
            vm(64, 16, 128, dt=BF), vm(64, 16, 128, dt=BF), vm(4, 512, 128, dt=BF),
            vm(4, 32, 256, dt=BF), vm(4, 32, 256, dt=BF), vm(128, 128, dt=BF), vm(4, 128, 128, dt=BF),
            vm(512, 128, dt=BF), vm(512, 128, dt=BF),
            vm(512, 256), vm(512, 256, dt=BF), vm(256, 512, dt=BF), vm(4, 512, 128),
            vm(2, 512, 128, dt=BF), vm(4, 256, 128, dt=BF), vm(4, 256, 128), vm(4, 256, 128, dt=BF),
            vm(4, 256, 128), vm(4, 256, 128),
            vm(64, 32, 128, dt=BF), vm(64, 32, 128, dt=BF), vm(4, 8, 512), vm(4, 256, 128, dt=BF),
            vm(64, 32, 128, dt=BF), vm(64, 32, 128, dt=BF), vm(4, 256, 128, dt=BF),
            vm(512, 256, dt=BF), vm(256, 512, dt=BF), vm(512, 256, dt=BF),
            vm(2, TALL, 128), vm(TALL, 128), vm(2, TALL, 128), vm(TALL, 128), vm(2, 32, 8, 128), vm(32, 8, 128),
            vm(32, 8, 128), vm(32, 8, 128), vm(32, 8, 128), vm(8, 128), vm(8, 128), vm(8, 128), vm(4, 8, 128),
            dma, dma, dma, dma, dma((2,)), dma((2,)), dma, dma((4,)), dma, dma, dma, dma, dma, dma, dma, dma((4,)),
            dma, dma, dma, dma, dma, dma((4,)), dma, dma, dma((3,)), dma((3,)), dma((3,)), dma((3,)),
            dma, dma, dma((3,)), dma((3,)), dma((3,)), dma((3,)),
        ],
        compiler_params=pltpu.CompilerParams(
            collective_id=0, has_side_effects=True, vmem_limit_bytes=56 * 1024 * 1024
        ),
    )(
        tile_src, features.T, send_rows[0], send_count, tile_val.reshape(TILES, 128, 128), labels.reshape(4, 128),
        w_self1, w_neigh1, w_self2.T, w_neigh2.T,
    )
    loss, gs1, gn1, gs2, gn2 = pl.pallas_call(
        functools.partial(result_kernel, 1.0 / (ROWS * NODES)),
        out_shape=(
            jax.ShapeDtypeStruct((1, 1), F32),
            jax.ShapeDtypeStruct((32, 1024), F32),
            jax.ShapeDtypeStruct((32, 1024), F32),
            jax.ShapeDtypeStruct((CLASSES, 256), F32),
            jax.ShapeDtypeStruct((CLASSES, 256), F32),
        ),
        in_specs=[whole] * 6,
        out_specs=(whole,) * 5,
    )(*parts)
    return (loss[0, 0], gs1, gn1, gs2.T, gn2.T)


def solution(mesh):
    in_specs = (
        P("node", "feat"),
        P("node", None, None),
        P("node", None),
        P("node", None),
        P("node", None, None, None),
        P("node"),
        P("feat", None),
        P("feat", None),
        P("feat", None),
        P("feat", None),
    )
    out_specs = (P(), P("feat", None), P("feat", None), P("feat", None), P("feat", None))
    return jax.shard_map(shards, mesh=mesh, in_specs=in_specs, out_specs=out_specs, check_vma=False)
```

```python
import functools
import math

import jax
import jax.numpy as jnp
from jax import lax
from jax.experimental import pallas as pl
from jax.experimental.pallas import tpu as pltpu
from jax.sharding import PartitionSpec as P

MESH = pl.DeviceIdType.MESH
F32 = jnp.float32
BF = jnp.bfloat16
I32 = jnp.int32
ROWS = 512
SLOTS = 64
NODES = 64
FEATS = 4
CHIPS = NODES // 2
RINGS = 4
TILES = 64
CLASSES = 172
CLS = 43
TALL = 176
CLS_TILES = TALL // 8
GELU_C = math.sqrt(2.0 / math.pi)


def lane_roll(value, shift):
    shift = shift % value.shape[-1]
    return pltpu.roll(value, shift, value.ndim - 1) if shift else value


def dot(a, b):
    return jnp.dot(a, b, preferred_element_type=F32)


def dot_nt(a, b):
    return lax.dot_general(a, b, (((1,), (1,)), ((), ())), preferred_element_type=F32)


def iota(shape, axis):
    return lax.broadcasted_iota(I32, shape, axis)


def g1_row(chip):
    y, z = chip // 8, chip % 8
    keep = (y + z) % 4
    rt = y * 2 + z // 4
    return (rt // 4) * 128 + 32 * keep + 8 * (rt % 4)


def step_kernel(
    grad_scale,
    tile_src, feat_t, send_rows, send_count, tiles_hbm, labels, w1s, w1n, w2s_t, w2n_t,
    fin_a, half_a, fin_b, half_b, fin_c, half_c,
    tiles, xcat, xsend, slot_col, wide, w2p_t, order_v, order,
    hot, hot_t, tiles_t, src, run, ptile,
    out1, recv1, xrecv, w1s_full, w1n_full, aggp, agg_recv, xfull, aggf,
    slope, hid, xa_t, pf, ycat, ypack, yown, yrecv, spack, srecv,
    out2, recv2, stat, hits, dlp, ret, recvb, gp, dlcat, dlcat_t, gcat,
    da, pa, db, pb, dc, pc, ra, rb, rc, ta, tb, tc, trecv,
    s_tiles, s_order, s_x, r_x, s_w, r_w, s_e1, r_e1, s_agg, r_agg, s_y, r_y, s_s, r_s, s_e2, r_e2,
    s_st, r_st, s_dl, r_dl, s_eb, r_eb, s_g, r_g, s_pair, r_pair, s_red, r_red,
    s_t, r_t, s_fin, r_fin, s_half, r_half, s_hit, r_hit,
):
    me = lax.axis_index("node")
    f = lax.axis_index("feat")
    chip, core = me // 2, lax.rem(me, 2)
    ring, place = me // 16, lax.rem(me // 2, 8)
    partner = me + 1 - 2 * core

    def wait_bytes(ref, sem):
        pltpu.make_async_copy(ref, ref, sem).wait()

    def send(s, d, ssem, rsem, node, feat):
        pltpu.make_async_remote_copy(
            src_ref=s, dst_ref=d, send_sem=ssem, recv_sem=rsem,
            device_id=(node, feat), device_id_type=MESH,
        ).start()

    def to_feats(s, d, ssem, rsem, same=False):
        for i in (2, 1, 3):
            g = lax.rem(f + i, FEATS)
            send(s if same else s.at[g], d.at[f], ssem, rsem, me, g)

    def place_at(k):
        off = ((k + 1) // 2) * (2 * lax.rem(k, 2) - 1)
        return lax.rem(place + off + 8, 8)

    def ring_at(j):
        return lax.rem(ring + (2, 1, 3, 0)[j], RINGS)

    lane = lambda r, n=128: iota((r, n), 1)
    three = pl.ds(0, FEATS - 1)

    load_tiles = pltpu.make_async_copy(tiles_hbm, tiles, s_tiles)
    load_tiles.start()

    bar = pltpu.get_barrier_semaphore()

    def hello(i, c):
        pl.semaphore_signal(bar, inc=1, device_id=(lax.rem(me + i, NODES), f), device_id_type=MESH)
        return c

    for lo, hi in ((25, 40), (1, 25), (40, NODES)):
        lax.fori_loop(lo, hi, hello, 0)
    for i in range(1, FEATS):
        pl.semaphore_signal(bar, inc=1, device_id=(me, lax.rem(f + i, FEATS)), device_id_type=MESH)

    x0 = jnp.transpose(jnp.concatenate([feat_t[...].astype(F32), jnp.zeros((96, ROWS), F32)], axis=0))
    for q in range(4):
        shifted = lane_roll(x0, 32 * q)
        xcat[q] = shifted.astype(BF)
        part = shifted[128 * q:128 * q + 128]
        xpack = part if q == 0 else xpack + part
    xsend[...] = xpack.astype(BF)

    wide[0, 0:64, 0:64] = send_rows[...].astype(F32)
    turned = jnp.transpose(wide[0, 0:128, 0:128]).astype(I32)[0:64]
    counts = jnp.concatenate([send_count[...], jnp.zeros((1, 64), I32)], axis=1)
    slot_col[...] = jnp.where(iota((64, 128), 0) < counts, turned, -1)

    def build_hot(d, c):
        col = jnp.sum(jnp.where(lane(SLOTS) == d, slot_col[...], 0), axis=1, keepdims=True)
        hot[d] = jnp.where(col == lane(SLOTS, ROWS), 1.0, 0.0).astype(BF)
        return c

    lax.fori_loop(0, NODES, build_hot, 0, unroll=8)

    def pack1(m, c):
        d0 = pl.multiple_of(m * 32, 32)
        acc = jnp.zeros((512, 128), F32)
        for q in range(4):
            acc = acc + dot(hot[pl.ds(d0, 32), 16 * q:16 * q + 16, :].reshape(512, ROWS), xcat[q])
        out1[pl.ds(d0, 32)] = acc.astype(BF).reshape(32, 16, 128)
        return c

    lax.fori_loop(0, 2, pack1, 0)
    recv1[me] = out1[me]
    xrecv[f] = xsend[...]
    pl.semaphore_wait(bar, NODES - 1 + FEATS - 1)

    for j in range(RINGS):
        rr = ring_at(j)

        def send1(k, c):
            k = (16 if j < 3 else 15) - 1 - k + (0 if j < 3 else 1)
            p = rr * 16 + place_at(k // 2) * 2 + lax.rem(core + k, 2)
            send(out1.at[p], recv1.at[me], s_e1, r_e1.at[ring], p, f)
            return c

        lax.fori_loop(0, 16 if j < 3 else 15, send1, 0)
    for i in (2, 1, 3):
        g = lax.rem(f + i, FEATS)
        cols = pl.ds(pl.multiple_of(g * 256, 256), 256)
        send(xsend, xrecv.at[f], s_x, r_x, me, g)
        send(w1s.at[:, cols], w1s_full.at[f], s_w.at[0], r_w.at[0], me, g)
        send(w1n.at[:, cols], w1n_full.at[f], s_w.at[1], r_w.at[1], me, g)

    own_cols = pl.ds(pl.multiple_of(f * 256, 256), 256)
    w1s_full[f] = w1s[:, own_cols]
    w1n_full[f] = w1n[:, own_cols]
    for b in range(4):
        src[b] = xcat[0, 128 * b:128 * b + 128, :]

    for part, ref in enumerate((w2s_t, w2n_t)):
        wide[0, 0:CLASSES, 0:256] = ref[...].astype(F32)
        wide[1] = jnp.zeros((256, 256), F32)
        for g in range(4):
            wide[1, 64 * g:64 * g + CLS, :] = wide[0, CLS * g:CLS * g + CLS, 0:256]
        w2p_t[256 * part:256 * part + 256, :] = wide[1].astype(BF)

    srow = jnp.full((128, 128), 1 << 20, I32)
    for t in range(TILES):
        srow = jnp.where(lane(128) == t, tile_src[t // 16, t % 16], srow)
    scol = jnp.transpose(srow)
    sub = iota((128, 128), 0)
    lane128 = lane(128)
    same = (srow == scol) & (lane128 < sub)
    rank = jnp.sum(jnp.where((srow < scol) | same, 1, 0), axis=1, keepdims=True)
    goes = jnp.minimum(jnp.sum(jnp.where(same, 1, 0), axis=1, keepdims=True), 1)
    at = rank == lane128
    order_v[...] = jnp.zeros((8, 128), I32)
    order_v[0:1, :] = jnp.sum(jnp.where(at, sub, 0), axis=0, keepdims=True)
    order_v[1:2, :] = jnp.sum(jnp.where(at, goes, 0), axis=0, keepdims=True)
    upto = jnp.sum(jnp.where(scol <= lane128, 1, 0), axis=0, keepdims=True)
    order_v[2:3, :] = jnp.maximum(upto - 1, 0)
    order_v[3:4, :] = jnp.minimum(jnp.sum(jnp.where(scol == lane128, 1, 0), axis=0, keepdims=True), 1)
    order_copy = pltpu.make_async_copy(order_v, order, s_order)
    order_copy.start()

    load_tiles.wait()

    def turn(t, c):
        tiles_t[t] = jnp.transpose(tiles[t])
        return c

    lax.fori_loop(0, TILES, turn, 0, unroll=4)
    order_copy.wait()

    def row_bytes(buf, j):
        return buf.at[pl.ds(0, 15 if j == 3 else 16)]

    group = lane128 // 32

    def unpack_feats(ref, out):
        for b in range(4):
            acc = jnp.zeros((128, 128), F32)
            for g in range(4):
                acc = jnp.where(group == g, lane_roll(ref[g].astype(F32), 32 * (g - b)), acc)
            out[128 * b:128 * b + 128, :] = acc.astype(BF)

    wait_bytes(xrecv.at[three], r_x)
    wait_bytes(w1s_full.at[three], r_w.at[0])
    unpack_feats(xrecv, xfull)
    slope[...] = dot(xfull[...], w1s_full[...].reshape(128, 256))
    xa_t[0:128, :] = jnp.transpose(xfull[...])

    for j in (3, 1, 2, 0):
        rr = ring_at(j)
        wait_bytes(row_bytes(recv1, j), r_e1.at[rr])

        def unpack1(k, c):
            b = rr * 8 + k
            for p in range(2):
                v = recv1[2 * b + p].astype(F32)
                for q in range(4):
                    src[4 + b, 64 * p + 16 * q:64 * p + 16 * q + 16, :] = lane_roll(v, -32 * q).astype(BF)
            return c

        lax.fori_loop(0, 8, unpack1, 0, unroll=4)

    def tile_product(b):
        lhs = jnp.concatenate([tiles[16 * b + k] for k in range(16)], axis=1)
        rhs = jnp.concatenate([src[tile_src[b, k]] for k in range(16)], axis=0)
        return dot(lhs, rhs)

    packed = jnp.zeros((128, 128), F32)
    for b in range(4):
        packed = packed + lane_roll(jnp.where(group == 0, tile_product(b), 0.0), 32 * b)
    aggp[...] = packed.astype(BF)
    to_feats(aggp, agg_recv, s_agg, r_agg, same=True)
    agg_recv[f] = aggp[...]

    wait_bytes(w1n_full.at[three], r_w.at[1])
    wait_bytes(agg_recv.at[three], r_agg)
    unpack_feats(agg_recv, aggf)

    pre = slope[...] + dot(aggf[...], w1n_full[...].reshape(128, 256))
    th = jnp.tanh(GELU_C * (pre + 0.044715 * (pre * pre * pre)))
    cdf = 0.5 * (1.0 + th)
    slope[...] = cdf + pre * (0.5 * (1.0 - th * th)) * (GELU_C * (1.0 + 3.0 * 0.044715 * (pre * pre)))
    hid[...] = (pre * cdf).astype(BF)

    low256 = lane(256) < 64

    def pack_halves(v, g):
        a, b = v[0:256], v[256:512]
        return jnp.where(low256, a if g % 2 == 0 else lane_roll(a, 64), lane_roll(b, 64) if g % 2 == 0 else b)

    for half in range(2):
        v = dot_nt(hid[...], w2p_t[256 + 128 * half:256 + 128 * half + 128, :])
        for g in (2 * half, 2 * half + 1):
            yv = pack_halves(v, g)
            yown[g] = yv
            ypack[g] = yv.astype(BF)
    to_feats(ypack, yrecv, s_y, r_y)
    for half in range(2):
        v = dot_nt(hid[...], w2p_t[128 * half:128 * half + 128, :])
        for g in (2 * half, 2 * half + 1):
            spack[g] = pack_halves(v, g)
    to_feats(spack, srecv, s_s, r_s)
    yrecv[f] = jnp.zeros((256, 128), BF)
    srecv[f] = spack[f]
    wait_bytes(yrecv.at[three], r_y)
    ys = yown[f]
    for g in range(4):
        ys = ys + yrecv[g].astype(F32)
    yr = lane_roll(ys, 64)
    ycat[0, 0:256, :] = jnp.where(low256, ys, 0.0).astype(BF)
    ycat[0, 256:512, :] = jnp.where(low256, yr, 0.0).astype(BF)
    ycat[1, 0:256, :] = jnp.where(low256, 0.0, yr).astype(BF)
    ycat[1, 256:512, :] = jnp.where(low256, 0.0, ys).astype(BF)

    for j in range(RINGS):
        rr = ring_at(j)
        d0 = pl.multiple_of(rr * 16, 16)
        acc = dot(hot[pl.ds(d0, 16), 0:32, :].reshape(512, ROWS), ycat[0])
        acc = acc + dot(hot[pl.ds(d0, 16), 32:64, :].reshape(512, ROWS), ycat[1])
        out2[pl.ds(d0, 16)] = acc.astype(BF).reshape(16, 32, 128)

        def send2(k, c):
            k = (16 if j < 3 else 15) - 1 - k + (0 if j < 3 else 1)
            p = rr * 16 + place_at(k // 2) * 2 + lax.rem(core + k, 2)
            send(out2.at[p], recv2.at[me], s_e2, r_e2.at[ring], p, f)
            return c

        lax.fori_loop(0, 16 if j < 3 else 15, send2, 0)

    recv2[me] = out2[me]
    for b in range(4):
        src[b] = ycat[0, 128 * b:128 * b + 128, :]
    xa_t[128:256, :] = jnp.transpose(aggf[...])

    def turn_hot(y, c):
        d0 = pl.multiple_of(y * 16, 16)
        for h in range(2):
            for k in range(4):
                part = hot[pl.ds(d0, 16), 32 * h:32 * h + 32, 128 * k:128 * k + 128].reshape(512, 128)
                hot_t[y, h, 128 * k:128 * k + 128, :] = jnp.transpose(part)
        return c

    lax.fori_loop(0, RINGS, turn_hot, 0)

    for j in (3, 1, 2, 0):
        rr = ring_at(j)
        wait_bytes(row_bytes(recv2, j), r_e2.at[rr])

        def unpack2(k, c):
            b = rr * 8 + k
            for p in range(2):
                v = recv2[2 * b + p]
                src[4 + b, 64 * p:64 * p + 32, :] = v
                src[4 + b, 64 * p + 32:64 * p + 64, :] = lane_roll(v.astype(F32), 64).astype(BF)
            return c

        lax.fori_loop(0, 8, unpack2, 0, unroll=4)

    wait_bytes(srecv.at[three], r_s)
    ss = srecv[0] + srecv[1] + srecv[2] + srecv[3]
    pf[0, 0:256, :] = ss
    pf[0, 256:512, :] = lane_roll(ss, 64)

    mine = lane128 < CLS
    for b in range(4):
        r = slice(128 * b, 128 * b + 128)
        lg = jnp.where(mine, pf[0, r, :] + tile_product(b), -1e30)
        top = jnp.max(lg, axis=1, keepdims=True)
        ex = jnp.exp(lg - top)
        tot = jnp.sum(ex, axis=1, keepdims=True)
        lab = jnp.transpose(jnp.broadcast_to(labels[b:b + 1, :].astype(F32), (128, 128))).astype(I32)
        want = mine & ((lab - CLS * f) == lane128)
        hit = jnp.sum(jnp.where(want, lg, 0.0), axis=1, keepdims=True)
        st = jnp.where(lane128 == 0, top, jnp.where(lane128 == 1, tot, jnp.where(lane128 == 2, hit, 0.0)))
        st_t = jnp.transpose(st)
        stat[f, b:b + 1, :] = st_t[0:1]
        stat[f, 4 + b:5 + b, :] = st_t[1:2]
        hits[f, b:b + 1, :] = st_t[2:3]
        pf[1, r, :] = ex
        pf[2, r, :] = jnp.where(want, 1.0, 0.0)
    to_feats(stat.at[f], stat, s_st, r_st, same=True)
    wait_bytes(stat.at[three], r_st)

    tops = [stat[g, 0:4, :] for g in range(4)]
    best = jnp.maximum(jnp.maximum(tops[0], tops[1]), jnp.maximum(tops[2], tops[3]))
    total = jnp.zeros_like(best)
    for g in range(4):
        total = total + stat[g, 4:8, :] * jnp.exp(tops[g] - best)
    factor = jnp.exp(stat[f, 0:4, :] - best) / total
    for b in range(4):
        r = slice(128 * b, 128 * b + 128)
        fac = jnp.transpose(jnp.broadcast_to(factor[b:b + 1, :], (128, 128)))
        dl = ((pf[1, r, :] * fac - pf[2, r, :]) * grad_scale).astype(BF)
        rows = slice(128 * (b % 2), 128 * (b % 2) + 128)
        if b < 2:
            dlp[f, rows, :] = dl
        else:
            dlp[f, rows, :] = (dlp[f, rows, :].astype(F32) + lane_roll(dl.astype(F32), 64)).astype(BF)
        lhs = tiles_t[16 * b:16 * b + 16].reshape(2048, 128)
        ptile[16 * b:16 * b + 16] = dot(lhs, dl).reshape(16, 128, 128)
    to_feats(dlp.at[f], dlp, s_dl, r_dl, same=True)
    to_feats(hits.at[f], hits, s_hit, r_hit, same=True)

    def gather_sum(t, acc):
        acc = acc * order[1, t].astype(F32) + ptile[order[0, t]]
        run[t] = acc
        return acc

    lax.fori_loop(0, TILES, gather_sum, jnp.zeros((128, 128), F32), unroll=4)

    def landed(j):
        return run[order[2, j]] * order[3, j].astype(F32)

    for j in range(RINGS):
        rr = ring_at(j)

        def pack_back(k, c):
            to = rr * 8 + place_at(7 - k)
            blk = landed(4 + to)
            for p in range(2):
                v = blk[64 * p:64 * p + 32, :] + lane_roll(blk[64 * p + 32:64 * p + 64, :], 64)
                ret[2 * to + p] = v.astype(BF)
            return c

        lax.fori_loop(0, 8, pack_back, 0, unroll=4)

        def send_back(k, c):
            k = (16 if j < 3 else 15) - 1 - k + (0 if j < 3 else 1)
            p = rr * 16 + place_at(k // 2) * 2 + lax.rem(core + k, 2)
            send(ret.at[p], recvb.at[me], s_eb, r_eb.at[ring], p, f)
            return c

        lax.fori_loop(0, 16 if j < 3 else 15, send_back, 0)

    recvb[me] = ret[me]
    for b in range(4):
        pf[3, 128 * b:128 * b + 128, :] = landed(b)

    def join(ref, out):
        for pair in range(2):
            c = slice(128 * pair, 128 * pair + 128)
            a, b = ref[2 * pair].astype(F32), ref[2 * pair + 1].astype(F32)
            out[0:256, c] = jnp.where(low256, a, lane_roll(b, 64)).astype(BF)
            out[256:512, c] = jnp.where(low256, lane_roll(a, 64), b).astype(BF)

    def class_rows(v, d):
        for l in range(2):
            d[l, TALL - 8:TALL, :] = jnp.zeros((8, 128), F32)
            for g in range(4):
                d[l, CLS * g:CLS * g + CLS, :] = v[64 * g:64 * g + CLS, 128 * l:128 * l + 128]

    def rows8(t):
        return pl.ds(pl.multiple_of(t * 8, 8), 8)

    def chip_at(i):
        return lax.rem(ring + (i // 8) + 4, RINGS) * 8 + place_at(lax.rem(i, 8))

    def for_chips(body):
        lax.fori_loop(1, CHIPS, lambda i, c: (body(chip_at(CHIPS - i)), c)[1], 0)

    def reduce_class(d, peer, part, k):
        wait_bytes(peer, r_pair.at[k])
        d[core] = d[core] + peer[...]

        def one(p):
            @pl.when(p < CLS_TILES)
            def _():
                send(d.at[core, rows8(p)], part.at[chip], s_red.at[k], r_red.at[k], 2 * p + core, f)

        for_chips(one)

        @pl.when(chip < CLS_TILES)
        def _():
            part[chip] = d[core, rows8(chip), :]

    def spread_class(part, tile, fin, k):
        @pl.when(chip < CLS_TILES)
        def _():
            wait_bytes(part.at[pl.ds(0, CHIPS - 1)], r_red.at[k])
            tile[...] = jnp.sum(part[...], axis=0)
            for_chips(lambda p: send(tile, fin.at[chip], s_fin.at[k], r_fin.at[k], 2 * p + core, f))
            fin[chip] = tile[...]

    def gather_class(fin, half, k):
        @pl.when(chip < CLS_TILES)
        def _():
            wait_bytes(fin.at[pl.ds(0, CLS_TILES - 1)], r_fin.at[k])

        @pl.when(chip >= CLS_TILES)
        def _():
            wait_bytes(fin, r_fin.at[k])

        send(fin, half, s_half.at[k], r_half.at[k], partner, f)

    wait_bytes(hits.at[three], r_hit)
    hit_sum = hits[0, 0:4, :] + hits[1, 0:4, :] + hits[2, 0:4, :] + hits[3, 0:4, :]
    loss = jnp.sum(jnp.log(total) + best - hit_sum)
    wait_bytes(dlp.at[three], r_dl)
    join(dlp, dlcat)
    dlcat_t[...] = jnp.transpose(dlcat[...])
    class_rows(dot(dlcat_t[...], hid[...]), da)
    tail = (iota((8, 128), 0) == 7) & (lane(8) == 0)
    for l in range(2):
        da[l, TALL - 8:TALL, :] = da[l, TALL - 8:TALL, :] + jnp.where(tail, loss, 0.0)
    send(da.at[1 - core], pa, s_pair.at[0], r_pair.at[0], partner, f)
    reduce_class(da, pa, ra, 0)

    g_sum = pf[3]
    low = lane(ROWS) < 64
    for j in (3, 1, 2, 0):
        rr = ring_at(j)
        wait_bytes(row_bytes(recvb, j), r_eb.at[rr])
        back = recvb[pl.ds(pl.multiple_of(rr * 16, 16), 16)].reshape(512, 128)
        g_sum = g_sum + jnp.where(low, dot(hot_t[rr, 0], back), 0.0)
        g_sum = g_sum + jnp.where(low, lane_roll(dot(hot_t[rr, 1], back), 64), 0.0)
    gp[f] = (g_sum[0:256] + lane_roll(g_sum[256:512], 64)).astype(BF)
    to_feats(gp.at[f], gp, s_g, r_g, same=True)
    spread_class(ra, ta, fin_a, 0)
    bh0 = dot(dlcat[...], w2p_t[0:256, :])
    wait_bytes(gp.at[three], r_g)
    join(gp, gcat)

    bh = bh0 + dot(gcat[...], w2p_t[256:512, :])
    g1 = dot(xa_t[...], (bh * slope[...]).astype(BF))
    for l in range(2):
        for ch in range(CHIPS):
            dc[l, ch] = g1[g1_row(ch):g1_row(ch) + 8, 128 * l:128 * l + 128]
    send(dc.at[1 - core], pc, s_pair.at[2], r_pair.at[2], partner, f)
    class_rows(dot(jnp.transpose(gcat[...]), hid[...]), db)
    send(db.at[1 - core], pb, s_pair.at[1], r_pair.at[1], partner, f)
    wait_bytes(pc, r_pair.at[2])
    dc[core] = dc[core] + pc[...]
    for_chips(lambda p: send(dc.at[core, p], rc.at[chip], s_red.at[2], r_red.at[2], 2 * p + core, f))
    rc[chip] = dc[core, chip]
    reduce_class(db, pb, rb, 1)

    wait_bytes(rc.at[pl.ds(0, CHIPS - 1)], r_red.at[2])
    tc[...] = jnp.sum(rc[...], axis=0)
    keep = lax.rem(ring + place, 4)
    rt = ring * 2 + place // 4
    kept = keep == f

    @pl.when(jnp.logical_not(kept))
    def _():
        send(tc, trecv.at[f], s_t, r_t, me, keep)

    spread_class(rb, tb, fin_b, 1)

    @pl.when(kept)
    def _():
        trecv[f] = tc[...]
        wait_bytes(trecv.at[three], r_t)
        for_chips(lambda p: send(trecv, fin_c.at[rt], s_fin.at[2], r_fin.at[2], 2 * p + core, f))
        fin_c[rt] = trecv[...]

    gather_class(fin_a, half_a, 0)
    gather_class(fin_b, half_b, 1)

    @pl.when(kept)
    def _():
        wait_bytes(fin_c.at[pl.ds(0, 7)], r_fin.at[2])

    @pl.when(jnp.logical_not(kept))
    def _():
        wait_bytes(fin_c, r_fin.at[2])

    send(fin_c, half_c, s_half.at[2], r_half.at[2], partner, f)

    n63, c31 = pl.ds(0, NODES - 1), pl.ds(0, CHIPS - 1)
    wait_bytes(recv1.at[n63], s_e1)
    wait_bytes(xrecv.at[three], s_x)
    wait_bytes(w1s_full.at[three], s_w.at[0])
    wait_bytes(w1n_full.at[three], s_w.at[1])
    wait_bytes(agg_recv.at[three], s_agg)
    wait_bytes(yrecv.at[three], s_y)
    wait_bytes(srecv.at[three], s_s)
    wait_bytes(recv2.at[n63], s_e2)
    wait_bytes(stat.at[three], s_st)
    wait_bytes(dlp.at[three], s_dl)
    wait_bytes(hits.at[three], s_hit)
    wait_bytes(recvb.at[n63], s_eb)
    wait_bytes(gp.at[three], s_g)
    wait_bytes(pa, s_pair.at[0])
    wait_bytes(pb, s_pair.at[1])
    wait_bytes(pc, s_pair.at[2])
    wait_bytes(rc.at[c31], s_red.at[2])
    for k, part in ((0, ra), (1, rb)):
        @pl.when(chip < CLS_TILES)
        def _():
            wait_bytes(part.at[pl.ds(0, CLS_TILES - 1)], s_red.at[k])
            wait_bytes(part.at[c31], s_fin.at[k])

        @pl.when(chip >= CLS_TILES)
        def _():
            wait_bytes(part.at[pl.ds(0, CLS_TILES)], s_red.at[k])

    @pl.when(jnp.logical_not(kept))
    def _():
        wait_bytes(trecv.at[0], s_t)

    @pl.when(kept)
    def _():
        wait_bytes(ptile.at[c31, pl.ds(0, 32)], s_fin.at[2])

    for k, ref in enumerate((half_a, half_b, half_c)):
        wait_bytes(ref, s_half.at[k])
        wait_bytes(ref, r_half.at[k])


def result_kernel(scale, fin_a, half_a, fin_b, half_b, fin_c, half_c, loss_ref, gs1_ref, gn1_ref, gs2_ref, gn2_ref):
    core = lax.rem(lax.axis_index("node"), 2)
    first = core == 0
    loss_ref[...] = fin_a[CLS_TILES - 1, 7:8, 0:1] * scale
    for l in range(2):
        c = slice(128 * l, 128 * l + 128)
        mine = first if l == 0 else jnp.logical_not(first)
        for fin, half, ref in ((fin_a, half_a, gs2_ref), (fin_b, half_b, gn2_ref)):
            ref[:, c] = jnp.where(mine, fin[...], half[...]).reshape(TALL, 128)[0:CLASSES]
        v = jnp.where(mine, fin_c[...], half_c[...])
        for g in range(4):
            cols = slice(256 * g + 128 * l, 256 * g + 128 * l + 128)
            gs1_ref[:, cols] = v[0:4, g].reshape(32, 128)
            gn1_ref[:, cols] = v[4:8, g].reshape(32, 128)


def shards(features, send_rows, send_count, tile_src, tile_val, labels, w_self1, w_neigh1, w_self2, w_neigh2):
    vm = lambda *shape, dt=F32: pltpu.VMEM(shape, dt)
    dma = pltpu.SemaphoreType.DMA
    whole = pl.BlockSpec(memory_space=pltpu.VMEM)
    half_class = jax.ShapeDtypeStruct((CLS_TILES, 8, 128), F32)
    half_first = jax.ShapeDtypeStruct((8, 4, 8, 128), F32)
    parts = pl.pallas_call(
        functools.partial(step_kernel, 1.0 / math.sqrt(ROWS * NODES)),
        out_shape=(half_class,) * 4 + (half_first,) * 2,
        in_specs=[pl.BlockSpec(memory_space=pltpu.SMEM)] + [whole] * 3 + [pl.BlockSpec(memory_space=pl.ANY)] + [whole] * 5,
        out_specs=(whole,) * 6,
        scratch_shapes=[
            vm(64, 128, 128, dt=BF), vm(4, 512, 128, dt=BF), vm(128, 128, dt=BF), vm(64, 128, dt=I32), vm(2, 256, 256),
            vm(512, 256, dt=BF), vm(8, 128, dt=I32), pltpu.SMEM((8, 128), I32),
            vm(64, 64, 512, dt=BF), vm(4, 2, 512, 512, dt=BF), vm(64, 128, 128, dt=BF), vm(36, 128, 128, dt=BF),
            vm(64, 128, 128), vm(64, 128, 128),
            vm(64, 16, 128, dt=BF), vm(64, 16, 128, dt=BF), vm(4, 128, 128, dt=BF),
            vm(4, 32, 256, dt=BF), vm(4, 32, 256, dt=BF), vm(128, 128, dt=BF), vm(4, 128, 128, dt=BF),
            vm(512, 128, dt=BF), vm(512, 128, dt=BF),
            vm(512, 256), vm(512, 256, dt=BF), vm(256, 512, dt=BF), vm(4, 512, 128),
            vm(2, 512, 128, dt=BF), vm(4, 256, 128, dt=BF), vm(4, 256, 128), vm(4, 256, 128, dt=BF),
            vm(4, 256, 128), vm(4, 256, 128),
            vm(64, 32, 128, dt=BF), vm(64, 32, 128, dt=BF), vm(4, 8, 128), vm(4, 8, 128), vm(4, 256, 128, dt=BF),
            vm(64, 32, 128, dt=BF), vm(64, 32, 128, dt=BF), vm(4, 256, 128, dt=BF),
            vm(512, 256, dt=BF), vm(256, 512, dt=BF), vm(512, 256, dt=BF),
            vm(2, TALL, 128), vm(TALL, 128), vm(2, TALL, 128), vm(TALL, 128), vm(2, 32, 8, 128), vm(32, 8, 128),
            vm(32, 8, 128), vm(32, 8, 128), vm(32, 8, 128), vm(8, 128), vm(8, 128), vm(8, 128), vm(4, 8, 128),
            dma, dma, dma, dma, dma((2,)), dma((2,)), dma, dma((4,)), dma, dma, dma, dma, dma, dma, dma, dma((4,)),
            dma, dma, dma, dma, dma, dma((4,)), dma, dma, dma((3,)), dma((3,)), dma((3,)), dma((3,)),
            dma, dma, dma((3,)), dma((3,)), dma((3,)), dma((3,)), dma, dma,
        ],
        compiler_params=pltpu.CompilerParams(
            collective_id=0, has_side_effects=True, vmem_limit_bytes=56 * 1024 * 1024
        ),
    )(
        tile_src, features.T, send_rows[0], send_count, tile_val.reshape(TILES, 128, 128), labels.reshape(4, 128),
        w_self1, w_neigh1, w_self2.T, w_neigh2.T,
    )
    loss, gs1, gn1, gs2, gn2 = pl.pallas_call(
        functools.partial(result_kernel, 1.0 / (ROWS * NODES)),
        out_shape=(
            jax.ShapeDtypeStruct((1, 1), F32),
            jax.ShapeDtypeStruct((32, 1024), F32),
            jax.ShapeDtypeStruct((32, 1024), F32),
            jax.ShapeDtypeStruct((CLASSES, 256), F32),
            jax.ShapeDtypeStruct((CLASSES, 256), F32),
        ),
        in_specs=[whole] * 6,
        out_specs=(whole,) * 5,
    )(*parts)
    return (loss[0, 0], gs1, gn1, gs2.T, gn2.T)


def solution(mesh):
    in_specs = (
        P("node", "feat"),
        P("node", None, None),
        P("node", None),
        P("node", None),
        P("node", None, None, None),
        P("node"),
        P("feat", None),
        P("feat", None),
        P("feat", None),
        P("feat", None),
    )
    out_specs = (P(), P("feat", None), P("feat", None), P("feat", None), P("feat", None))
    return jax.shard_map(shards, mesh=mesh, in_specs=in_specs, out_specs=out_specs, check_vma=False)
```

```python
import functools
import math

import jax
import jax.numpy as jnp
from jax import lax
from jax.experimental import pallas as pl
from jax.experimental.pallas import tpu as pltpu
from jax.sharding import PartitionSpec as P

MESH = pl.DeviceIdType.MESH
F32 = jnp.float32
BF = jnp.bfloat16
I32 = jnp.int32
ROWS = 512
SLOTS = 64
NODES = 64
FEATS = 4
CHIPS = NODES // 2
RINGS = 4
TILES = 64
CLASSES = 172
CLS = 43
TALL = 176
CLS_TILES = TALL // 8
MSG = 24
RING_ROWS = 16 * MSG
GELU_C = math.sqrt(2.0 / math.pi)


def lane_roll(value, shift):
    shift = shift % value.shape[-1]
    return pltpu.roll(value, shift, value.ndim - 1) if shift else value


def dot(a, b):
    return jnp.dot(a, b, preferred_element_type=F32)


def dot_nt(a, b):
    return lax.dot_general(a, b, (((1,), (1,)), ((), ())), preferred_element_type=F32)


def iota(shape, axis):
    return lax.broadcasted_iota(I32, shape, axis)


def split_third(w):
    n = w.shape[0]
    at = iota((n, 16, 128), 2)
    last = jnp.sum(jnp.where(at == iota((n, 16, 128), 1), w[:, 16:17, :], 0.0), axis=2, keepdims=True)
    return jnp.where(at == CLS - 1, last, w[:, 0:16, :])


def third_rest(col):
    shape = col.shape
    pick = (iota(shape, 2) == iota(shape, 1) + 2 * CLS) & (iota(shape, 1) < 16)
    return jnp.sum(jnp.where(pick, col, 0.0), axis=1, keepdims=True)


def g1_row(chip):
    y, z = chip // 8, chip % 8
    keep = (y + z) % 4
    rt = y * 2 + z // 4
    return (rt // 4) * 128 + 32 * keep + 8 * (rt % 4)


def step_kernel(
    grad_scale,
    tile_src, feat_t, send_rows, send_count, tiles_hbm, labels, w1s, w1n, w2s_t, w2n_t,
    fin_a, half_a, fin_b, half_b, fin_c, half_c,
    tiles, xcat, xsend, slot_col, wide, w2p_t, order_v, order,
    hot, hot3, hot_t, tiles_t, src, run, ptile,
    out1, recv1, xrecv, w1s_full, w1n_full, aggp, agg_recv, xfull, aggf,
    slope, hid, xa_t, pf, ycat, ypack, yown, yrecv, spack, srecv,
    out2, recv2, stat, hits, dlp, ret, recvb, gp, dlcat, dlcat_t, gcat,
    da, pa, db, pb, dc, pc, ra, rb, rc, ta, tb, tc, trecv,
    s_tiles, s_order, s_x, r_x, s_w, r_w, s_e1, r_e1, s_agg, r_agg, s_y, r_y, s_s, r_s, s_e2, r_e2,
    s_st, r_st, s_dl, r_dl, s_eb, r_eb, s_g, r_g, s_pair, r_pair, s_red, r_red,
    s_t, r_t, s_fin, r_fin, s_half, r_half, s_hit, r_hit,
):
    me = lax.axis_index("node")
    f = lax.axis_index("feat")
    chip, core = me // 2, lax.rem(me, 2)
    ring, place = me // 16, lax.rem(me // 2, 8)
    partner = me + 1 - 2 * core

    def wait_bytes(ref, sem):
        pltpu.make_async_copy(ref, ref, sem).wait()

    def send(s, d, ssem, rsem, node, feat):
        pltpu.make_async_remote_copy(
            src_ref=s, dst_ref=d, send_sem=ssem, recv_sem=rsem,
            device_id=(node, feat), device_id_type=MESH,
        ).start()

    def to_feats(s, d, ssem, rsem, same=False):
        for i in (2, 1, 3):
            g = lax.rem(f + i, FEATS)
            send(s if same else s.at[g], d.at[f], ssem, rsem, me, g)

    def place_at(k):
        off = ((k + 1) // 2) * (2 * lax.rem(k, 2) - 1)
        return lax.rem(place + off + 8, 8)

    def ring_at(j):
        return lax.rem(ring + (2, 1, 3, 0)[j], RINGS)

    lane = lambda r, n=128: iota((r, n), 1)
    three = pl.ds(0, FEATS - 1)

    load_tiles = pltpu.make_async_copy(tiles_hbm, tiles, s_tiles)
    load_tiles.start()

    bar = pltpu.get_barrier_semaphore()

    def hello(i, c):
        pl.semaphore_signal(bar, inc=1, device_id=(lax.rem(me + i, NODES), f), device_id_type=MESH)
        return c

    for lo, hi in ((25, 40), (1, 25), (40, NODES)):
        lax.fori_loop(lo, hi, hello, 0)
    for i in range(1, FEATS):
        pl.semaphore_signal(bar, inc=1, device_id=(me, lax.rem(f + i, FEATS)), device_id_type=MESH)

    x0 = jnp.transpose(jnp.concatenate([feat_t[...].astype(F32), jnp.zeros((96, ROWS), F32)], axis=0))
    for q in range(4):
        shifted = lane_roll(x0, 32 * q)
        xcat[q] = shifted.astype(BF)
        part = shifted[128 * q:128 * q + 128]
        xpack = part if q == 0 else xpack + part
    xsend[...] = xpack.astype(BF)

    wide[0, 0:64, 0:64] = send_rows[...].astype(F32)
    turned = jnp.transpose(wide[0, 0:128, 0:128]).astype(I32)[0:64]
    counts = jnp.concatenate([send_count[...], jnp.zeros((1, 64), I32)], axis=1)
    slot_col[...] = jnp.where(iota((64, 128), 0) < counts, turned, -1)

    def build_hot(d, c):
        col = jnp.sum(jnp.where(lane(SLOTS) == d, slot_col[...], 0), axis=1, keepdims=True)
        hot[d] = jnp.where(col == lane(SLOTS, ROWS), 1.0, 0.0).astype(BF)
        return c

    lax.fori_loop(0, NODES, build_hot, 0, unroll=8)

    def pack1(m, c):
        d0 = pl.multiple_of(m * 32, 32)
        acc = jnp.zeros((512, 128), F32)
        for q in range(4):
            acc = acc + dot(hot[pl.ds(d0, 32), 16 * q:16 * q + 16, :].reshape(512, ROWS), xcat[q])
        out1[pl.ds(d0, 32)] = acc.astype(BF).reshape(32, 16, 128)
        return c

    lax.fori_loop(0, 2, pack1, 0)
    recv1[me] = out1[me]
    xrecv[f] = xsend[...]
    pl.semaphore_wait(bar, NODES - 1 + FEATS - 1)

    for j in range(RINGS):
        rr = ring_at(j)

        def send1(k, c):
            k = (16 if j < 3 else 15) - 1 - k + (0 if j < 3 else 1)
            p = rr * 16 + place_at(k // 2) * 2 + lax.rem(core + k, 2)
            send(out1.at[p], recv1.at[me], s_e1, r_e1.at[ring], p, f)
            return c

        lax.fori_loop(0, 16 if j < 3 else 15, send1, 0)
    for i in (2, 1, 3):
        g = lax.rem(f + i, FEATS)
        cols = pl.ds(pl.multiple_of(g * 256, 256), 256)
        send(xsend, xrecv.at[f], s_x, r_x, me, g)
        send(w1s.at[:, cols], w1s_full.at[f], s_w.at[0], r_w.at[0], me, g)
        send(w1n.at[:, cols], w1n_full.at[f], s_w.at[1], r_w.at[1], me, g)

    own_cols = pl.ds(pl.multiple_of(f * 256, 256), 256)
    w1s_full[f] = w1s[:, own_cols]
    w1n_full[f] = w1n[:, own_cols]
    for b in range(4):
        src[b] = xcat[0, 128 * b:128 * b + 128, :]

    for part, ref in enumerate((w2s_t, w2n_t)):
        wide[0, 0:CLASSES, 0:256] = ref[...].astype(F32)
        wide[1] = jnp.zeros((256, 256), F32)
        for g in range(4):
            wide[1, 64 * g:64 * g + CLS, :] = wide[0, CLS * g:CLS * g + CLS, 0:256]
        w2p_t[256 * part:256 * part + 256, :] = wide[1].astype(BF)

    srow = jnp.full((128, 128), 1 << 20, I32)
    for t in range(TILES):
        srow = jnp.where(lane(128) == t, tile_src[t // 16, t % 16], srow)
    scol = jnp.transpose(srow)
    sub = iota((128, 128), 0)
    lane128 = lane(128)
    same = (srow == scol) & (lane128 < sub)
    rank = jnp.sum(jnp.where((srow < scol) | same, 1, 0), axis=1, keepdims=True)
    goes = jnp.minimum(jnp.sum(jnp.where(same, 1, 0), axis=1, keepdims=True), 1)
    at = rank == lane128
    order_v[...] = jnp.zeros((8, 128), I32)
    order_v[0:1, :] = jnp.sum(jnp.where(at, sub, 0), axis=0, keepdims=True)
    order_v[1:2, :] = jnp.sum(jnp.where(at, goes, 0), axis=0, keepdims=True)
    upto = jnp.sum(jnp.where(scol <= lane128, 1, 0), axis=0, keepdims=True)
    order_v[2:3, :] = jnp.maximum(upto - 1, 0)
    order_v[3:4, :] = jnp.minimum(jnp.sum(jnp.where(scol == lane128, 1, 0), axis=0, keepdims=True), 1)
    order_copy = pltpu.make_async_copy(order_v, order, s_order)
    order_copy.start()

    def build_hot3(m, c):
        cols = []
        for d in (2 * m, 2 * m + 1):
            cols.append(jnp.sum(jnp.where(lane(SLOTS) == d, slot_col[...], 0), axis=1, keepdims=True))
        none = jnp.full((8, 1), -1, I32)
        at = pl.ds(pl.multiple_of(m * 48, 48), 48)
        for k, rows in enumerate((
            [cols[0][0:24], cols[1][0:24]],
            [cols[0][24:48], cols[1][24:48]],
            [cols[0][48:64], none, cols[1][48:64], none],
        )):
            col = jnp.concatenate(rows, axis=0)
            hot3[k, at, :] = jnp.where(col == lane(48, ROWS), 1.0, 0.0).astype(BF)
        return c

    lax.fori_loop(0, NODES // 2, build_hot3, 0, unroll=4)
    load_tiles.wait()

    def turn(t, c):
        tiles_t[t] = jnp.transpose(tiles[t])
        return c

    lax.fori_loop(0, TILES, turn, 0, unroll=4)
    order_copy.wait()

    def row_bytes(buf, j):
        return buf.at[pl.ds(0, 15 if j == 3 else 16)]

    group = lane128 // 32

    def unpack_feats(ref, out):
        for b in range(4):
            acc = jnp.zeros((128, 128), F32)
            for g in range(4):
                acc = jnp.where(group == g, lane_roll(ref[g].astype(F32), 32 * (g - b)), acc)
            out[128 * b:128 * b + 128, :] = acc.astype(BF)

    wait_bytes(xrecv.at[three], r_x)
    wait_bytes(w1s_full.at[three], r_w.at[0])
    unpack_feats(xrecv, xfull)
    slope[...] = dot(xfull[...], w1s_full[...].reshape(128, 256))
    xa_t[0:128, :] = jnp.transpose(xfull[...])

    for j in (3, 1, 2, 0):
        rr = ring_at(j)
        wait_bytes(row_bytes(recv1, j), r_e1.at[rr])

        def unpack1(k, c):
            b = rr * 8 + k
            for p in range(2):
                v = recv1[2 * b + p].astype(F32)
                for q in range(4):
                    src[4 + b, 64 * p + 16 * q:64 * p + 16 * q + 16, :] = lane_roll(v, -32 * q).astype(BF)
            return c

        lax.fori_loop(0, 8, unpack1, 0, unroll=4)

    def tile_product(b):
        lhs = jnp.concatenate([tiles[16 * b + k] for k in range(16)], axis=1)
        rhs = jnp.concatenate([src[tile_src[b, k]] for k in range(16)], axis=0)
        return dot(lhs, rhs)

    packed = jnp.zeros((128, 128), F32)
    for b in range(4):
        packed = packed + lane_roll(jnp.where(group == 0, tile_product(b), 0.0), 32 * b)
    aggp[...] = packed.astype(BF)
    to_feats(aggp, agg_recv, s_agg, r_agg, same=True)
    agg_recv[f] = aggp[...]

    wait_bytes(w1n_full.at[three], r_w.at[1])
    wait_bytes(agg_recv.at[three], r_agg)
    unpack_feats(agg_recv, aggf)

    pre = slope[...] + dot(aggf[...], w1n_full[...].reshape(128, 256))
    th = jnp.tanh(GELU_C * (pre + 0.044715 * (pre * pre * pre)))
    cdf = 0.5 * (1.0 + th)
    slope[...] = cdf + pre * (0.5 * (1.0 - th * th)) * (GELU_C * (1.0 + 3.0 * 0.044715 * (pre * pre)))
    hid[...] = (pre * cdf).astype(BF)

    low256 = lane(256) < 64

    def pack_halves(v, g):
        a, b = v[0:256], v[256:512]
        return jnp.where(low256, a if g % 2 == 0 else lane_roll(a, 64), lane_roll(b, 64) if g % 2 == 0 else b)

    for half in range(2):
        v = dot_nt(hid[...], w2p_t[256 + 128 * half:256 + 128 * half + 128, :])
        for g in (2 * half, 2 * half + 1):
            yv = pack_halves(v, g)
            yown[g] = yv
            ypack[g] = yv.astype(BF)
    to_feats(ypack, yrecv, s_y, r_y)
    for half in range(2):
        v = dot_nt(hid[...], w2p_t[128 * half:128 * half + 128, :])
        for g in (2 * half, 2 * half + 1):
            spack[g] = pack_halves(v, g)
    to_feats(spack, srecv, s_s, r_s)
    yrecv[f] = jnp.zeros((256, 128), BF)
    srecv[f] = spack[f]
    wait_bytes(yrecv.at[three], r_y)
    ys = yown[f]
    for g in range(4):
        ys = ys + yrecv[g].astype(F32)
    yr = lane_roll(ys, 64)
    y_lo = jnp.concatenate([jnp.where(low256, ys, 0.0), jnp.where(low256, yr, 0.0)], axis=0)
    ycat[0] = y_lo.astype(BF)
    ycat[1] = lane_roll(y_lo, CLS).astype(BF)
    ycat[2] = lane_roll(jnp.where(lane(ROWS) < CLS - 1, y_lo, 0.0), 2 * CLS).astype(BF)
    ycat[3] = jnp.broadcast_to(y_lo[:, CLS - 1:CLS], (ROWS, 128)).astype(BF)

    for j in range(RINGS):
        rr = ring_at(j)
        d0 = pl.multiple_of(rr * 16, 16)
        at = pl.ds(pl.multiple_of(rr * RING_ROWS, RING_ROWS), RING_ROWS)
        third = hot3[2, at, :]
        acc = dot(hot3[0, at, :], ycat[0]) + dot(hot3[1, at, :], ycat[1]) + dot(third, ycat[2])
        acc = acc.reshape(16, MSG, 128)
        rest = third_rest(dot(third, ycat[3]).reshape(16, MSG, 128))
        acc = jnp.where((iota((16, MSG, 128), 1) == 16) & (iota((16, MSG, 128), 2) >= 2 * CLS), rest, acc)
        out2[pl.ds(d0, 16)] = acc.astype(BF)

        def send2(k, c):
            k = (16 if j < 3 else 15) - 1 - k + (0 if j < 3 else 1)
            p = rr * 16 + place_at(k // 2) * 2 + lax.rem(core + k, 2)
            send(out2.at[p], recv2.at[me], s_e2, r_e2.at[ring], p, f)
            return c

        lax.fori_loop(0, 16 if j < 3 else 15, send2, 0)

    recv2[me] = out2[me]
    for b in range(4):
        src[b] = ycat[0, 128 * b:128 * b + 128, :]
    xa_t[128:256, :] = jnp.transpose(aggf[...])

    def turn_hot(y, c):
        for h in range(3):
            for k in range(4):
                part = hot3[h, pl.ds(pl.multiple_of(y * RING_ROWS, RING_ROWS), RING_ROWS), 128 * k:128 * k + 128]
                hot_t[y, h, 128 * k:128 * k + 128, :] = jnp.transpose(part)
        return c

    lax.fori_loop(0, RINGS, turn_hot, 0)

    for j in (3, 1, 2, 0):
        rr = ring_at(j)
        wait_bytes(row_bytes(recv2, j), r_e2.at[rr])

        def unpack2(k, c):
            b = rr * 8 + k
            v = recv2[pl.ds(2 * b, 2)].astype(F32)
            both = jnp.concatenate([v, lane_roll(v, -CLS), split_third(lane_roll(v, -2 * CLS))], axis=1)
            src[4 + b] = both.reshape(128, 128).astype(BF)
            return c

        lax.fori_loop(0, 8, unpack2, 0, unroll=4)

    wait_bytes(srecv.at[three], r_s)
    ss = srecv[0] + srecv[1] + srecv[2] + srecv[3]
    pf[0, 0:256, :] = ss
    pf[0, 256:512, :] = lane_roll(ss, 64)

    mine = lane128 < CLS
    for b in range(4):
        r = slice(128 * b, 128 * b + 128)
        lg = jnp.where(mine, pf[0, r, :] + tile_product(b), -1e30)
        top = jnp.max(lg, axis=1, keepdims=True)
        ex = jnp.exp(lg - top)
        tot = jnp.sum(ex, axis=1, keepdims=True)
        lab = jnp.transpose(jnp.broadcast_to(labels[b:b + 1, :].astype(F32), (128, 128))).astype(I32)
        want = mine & ((lab - CLS * f) == lane128)
        hit = jnp.sum(jnp.where(want, lg, 0.0), axis=1, keepdims=True)
        st = jnp.where(lane128 == 0, top, jnp.where(lane128 == 1, tot, jnp.where(lane128 == 2, hit, 0.0)))
        st_t = jnp.transpose(st)
        stat[f, b:b + 1, :] = st_t[0:1]
        stat[f, 4 + b:5 + b, :] = st_t[1:2]
        hits[f, b:b + 1, :] = st_t[2:3]
        pf[1, r, :] = ex
        pf[2, r, :] = jnp.where(want, 1.0, 0.0)
    to_feats(stat.at[f], stat, s_st, r_st, same=True)
    wait_bytes(stat.at[three], r_st)

    tops = [stat[g, 0:4, :] for g in range(4)]
    best = jnp.maximum(jnp.maximum(tops[0], tops[1]), jnp.maximum(tops[2], tops[3]))
    total = jnp.zeros_like(best)
    for g in range(4):
        total = total + stat[g, 4:8, :] * jnp.exp(tops[g] - best)
    factor = jnp.exp(stat[f, 0:4, :] - best) / total
    for b in range(4):
        r = slice(128 * b, 128 * b + 128)
        fac = jnp.transpose(jnp.broadcast_to(factor[b:b + 1, :], (128, 128)))
        dl = ((pf[1, r, :] * fac - pf[2, r, :]) * grad_scale).astype(BF)
        rows = slice(128 * (b % 2), 128 * (b % 2) + 128)
        if b < 2:
            dlp[f, rows, :] = dl
        else:
            dlp[f, rows, :] = (dlp[f, rows, :].astype(F32) + lane_roll(dl.astype(F32), 64)).astype(BF)
        lhs = tiles_t[16 * b:16 * b + 16].reshape(2048, 128)
        ptile[16 * b:16 * b + 16] = dot(lhs, dl).reshape(16, 128, 128)
    to_feats(dlp.at[f], dlp, s_dl, r_dl, same=True)
    to_feats(hits.at[f], hits, s_hit, r_hit, same=True)

    def gather_sum(t, acc):
        acc = acc * order[1, t].astype(F32) + ptile[order[0, t]]
        run[t] = acc
        return acc

    lax.fori_loop(0, TILES, gather_sum, jnp.zeros((128, 128), F32), unroll=4)

    def landed(j):
        return run[order[2, j]] * order[3, j].astype(F32)

    for j in range(RINGS):
        rr = ring_at(j)

        def pack_back(k, c):
            to = rr * 8 + place_at(7 - k)
            blk = landed(4 + to)
            blk = blk.reshape(2, 64, 128)
            third = blk[:, 48:64, :]
            rest = third_rest(jnp.broadcast_to(third[:, :, CLS - 1:CLS], (2, 16, 128)))
            rest = jnp.where(iota((2, 8, 128), 1) == 0, rest, 0.0)
            turned3 = lane_roll(jnp.where(iota((2, 16, 128), 2) < CLS - 1, third, 0.0), 2 * CLS)
            v = blk[:, 0:24, :] + lane_roll(blk[:, 24:48, :], CLS) + jnp.concatenate([turned3, rest], axis=1)
            ret[pl.ds(2 * to, 2)] = v.astype(BF)
            return c

        lax.fori_loop(0, 8, pack_back, 0, unroll=4)

        def send_back(k, c):
            k = (16 if j < 3 else 15) - 1 - k + (0 if j < 3 else 1)
            p = rr * 16 + place_at(k // 2) * 2 + lax.rem(core + k, 2)
            send(ret.at[p], recvb.at[me], s_eb, r_eb.at[ring], p, f)
            return c

        lax.fori_loop(0, 16 if j < 3 else 15, send_back, 0)

    recvb[me] = ret[me]
    for b in range(4):
        pf[3, 128 * b:128 * b + 128, :] = landed(b)

    def join(ref, out):
        for pair in range(2):
            c = slice(128 * pair, 128 * pair + 128)
            a, b = ref[2 * pair].astype(F32), ref[2 * pair + 1].astype(F32)
            out[0:256, c] = jnp.where(low256, a, lane_roll(b, 64)).astype(BF)
            out[256:512, c] = jnp.where(low256, lane_roll(a, 64), b).astype(BF)

    def class_rows(v, d):
        for l in range(2):
            d[l, TALL - 8:TALL, :] = jnp.zeros((8, 128), F32)
            for g in range(4):
                d[l, CLS * g:CLS * g + CLS, :] = v[64 * g:64 * g + CLS, 128 * l:128 * l + 128]

    def rows8(t):
        return pl.ds(pl.multiple_of(t * 8, 8), 8)

    def chip_at(i):
        return lax.rem(ring + (i // 8) + 4, RINGS) * 8 + place_at(lax.rem(i, 8))

    def for_chips(body):
        lax.fori_loop(1, CHIPS, lambda i, c: (body(chip_at(CHIPS - i)), c)[1], 0)

    def reduce_class(d, peer, part, k):
        wait_bytes(peer, r_pair.at[k])
        d[core] = d[core] + peer[...]

        def one(p):
            @pl.when(p < CLS_TILES)
            def _():
                send(d.at[core, rows8(p)], part.at[chip], s_red.at[k], r_red.at[k], 2 * p + core, f)

        for_chips(one)

        @pl.when(chip < CLS_TILES)
        def _():
            part[chip] = d[core, rows8(chip), :]

    def spread_class(part, tile, fin, k):
        @pl.when(chip < CLS_TILES)
        def _():
            wait_bytes(part.at[pl.ds(0, CHIPS - 1)], r_red.at[k])
            tile[...] = jnp.sum(part[...], axis=0)
            for_chips(lambda p: send(tile, fin.at[chip], s_fin.at[k], r_fin.at[k], 2 * p + core, f))
            fin[chip] = tile[...]

    def gather_class(fin, half, k):
        @pl.when(chip < CLS_TILES)
        def _():
            wait_bytes(fin.at[pl.ds(0, CLS_TILES - 1)], r_fin.at[k])

        @pl.when(chip >= CLS_TILES)
        def _():
            wait_bytes(fin, r_fin.at[k])

        send(fin, half, s_half.at[k], r_half.at[k], partner, f)

    wait_bytes(hits.at[three], r_hit)
    hit_sum = hits[0, 0:4, :] + hits[1, 0:4, :] + hits[2, 0:4, :] + hits[3, 0:4, :]
    loss = jnp.sum(jnp.log(total) + best - hit_sum)
    wait_bytes(dlp.at[three], r_dl)
    join(dlp, dlcat)
    dlcat_t[...] = jnp.transpose(dlcat[...])
    class_rows(dot(dlcat_t[...], hid[...]), da)
    tail = (iota((8, 128), 0) == 7) & (lane(8) == 0)
    for l in range(2):
        da[l, TALL - 8:TALL, :] = da[l, TALL - 8:TALL, :] + jnp.where(tail, loss, 0.0)
    send(da.at[1 - core], pa, s_pair.at[0], r_pair.at[0], partner, f)
    reduce_class(da, pa, ra, 0)

    g_sum = pf[3]
    valid = lane(ROWS) < CLS
    for j in (3, 1, 2, 0):
        rr = ring_at(j)
        wait_bytes(row_bytes(recvb, j), r_eb.at[rr])
        back = recvb[pl.ds(pl.multiple_of(rr * 16, 16), 16)].astype(F32)
        third = split_third(lane_roll(back, -2 * CLS))
        third = jnp.concatenate([third, jnp.zeros((16, 8, 128), F32)], axis=1).reshape(RING_ROWS, 128).astype(BF)
        back = back.reshape(RING_ROWS, 128).astype(BF)
        g_sum = g_sum + jnp.where(valid, dot(hot_t[rr, 0], back) + dot(hot_t[rr, 2], third), 0.0)
        g_sum = g_sum + jnp.where(valid, lane_roll(dot(hot_t[rr, 1], back), -CLS), 0.0)
    gp[f] = (g_sum[0:256] + lane_roll(g_sum[256:512], 64)).astype(BF)
    to_feats(gp.at[f], gp, s_g, r_g, same=True)
    spread_class(ra, ta, fin_a, 0)
    bh0 = dot(dlcat[...], w2p_t[0:256, :])
    wait_bytes(gp.at[three], r_g)
    join(gp, gcat)

    bh = bh0 + dot(gcat[...], w2p_t[256:512, :])
    g1 = dot(xa_t[...], (bh * slope[...]).astype(BF))
    for l in range(2):
        for ch in range(CHIPS):
            dc[l, ch] = g1[g1_row(ch):g1_row(ch) + 8, 128 * l:128 * l + 128]
    send(dc.at[1 - core], pc, s_pair.at[2], r_pair.at[2], partner, f)
    class_rows(dot(jnp.transpose(gcat[...]), hid[...]), db)
    send(db.at[1 - core], pb, s_pair.at[1], r_pair.at[1], partner, f)
    wait_bytes(pc, r_pair.at[2])
    dc[core] = dc[core] + pc[...]
    for_chips(lambda p: send(dc.at[core, p], rc.at[chip], s_red.at[2], r_red.at[2], 2 * p + core, f))
    rc[chip] = dc[core, chip]
    reduce_class(db, pb, rb, 1)

    wait_bytes(rc.at[pl.ds(0, CHIPS - 1)], r_red.at[2])
    tc[...] = jnp.sum(rc[...], axis=0)
    keep = lax.rem(ring + place, 4)
    rt = ring * 2 + place // 4
    kept = keep == f

    @pl.when(jnp.logical_not(kept))
    def _():
        send(tc, trecv.at[f], s_t, r_t, me, keep)

    spread_class(rb, tb, fin_b, 1)

    @pl.when(kept)
    def _():
        trecv[f] = tc[...]
        wait_bytes(trecv.at[three], r_t)
        for_chips(lambda p: send(trecv, fin_c.at[rt], s_fin.at[2], r_fin.at[2], 2 * p + core, f))
        fin_c[rt] = trecv[...]

    gather_class(fin_a, half_a, 0)
    gather_class(fin_b, half_b, 1)

    @pl.when(kept)
    def _():
        wait_bytes(fin_c.at[pl.ds(0, 7)], r_fin.at[2])

    @pl.when(jnp.logical_not(kept))
    def _():
        wait_bytes(fin_c, r_fin.at[2])

    send(fin_c, half_c, s_half.at[2], r_half.at[2], partner, f)

    n63, c31 = pl.ds(0, NODES - 1), pl.ds(0, CHIPS - 1)
    wait_bytes(recv1.at[n63], s_e1)
    wait_bytes(xrecv.at[three], s_x)
    wait_bytes(w1s_full.at[three], s_w.at[0])
    wait_bytes(w1n_full.at[three], s_w.at[1])
    wait_bytes(agg_recv.at[three], s_agg)
    wait_bytes(yrecv.at[three], s_y)
    wait_bytes(srecv.at[three], s_s)
    wait_bytes(recv2.at[n63], s_e2)
    wait_bytes(stat.at[three], s_st)
    wait_bytes(dlp.at[three], s_dl)
    wait_bytes(hits.at[three], s_hit)
    wait_bytes(recvb.at[n63], s_eb)
    wait_bytes(gp.at[three], s_g)
    wait_bytes(pa, s_pair.at[0])
    wait_bytes(pb, s_pair.at[1])
    wait_bytes(pc, s_pair.at[2])
    wait_bytes(rc.at[c31], s_red.at[2])
    for k, part in ((0, ra), (1, rb)):
        @pl.when(chip < CLS_TILES)
        def _():
            wait_bytes(part.at[pl.ds(0, CLS_TILES - 1)], s_red.at[k])
            wait_bytes(part.at[c31], s_fin.at[k])

        @pl.when(chip >= CLS_TILES)
        def _():
            wait_bytes(part.at[pl.ds(0, CLS_TILES)], s_red.at[k])

    @pl.when(jnp.logical_not(kept))
    def _():
        wait_bytes(trecv.at[0], s_t)

    @pl.when(kept)
    def _():
        wait_bytes(ptile.at[c31, pl.ds(0, 32)], s_fin.at[2])

    for k, ref in enumerate((half_a, half_b, half_c)):
        wait_bytes(ref, s_half.at[k])
        wait_bytes(ref, r_half.at[k])


def result_kernel(scale, fin_a, half_a, fin_b, half_b, fin_c, half_c, loss_ref, gs1_ref, gn1_ref, gs2_ref, gn2_ref):
    core = lax.rem(lax.axis_index("node"), 2)
    first = core == 0
    loss_ref[...] = fin_a[CLS_TILES - 1, 7:8, 0:1] * scale
    for l in range(2):
        c = slice(128 * l, 128 * l + 128)
        mine = first if l == 0 else jnp.logical_not(first)
        for fin, half, ref in ((fin_a, half_a, gs2_ref), (fin_b, half_b, gn2_ref)):
            ref[:, c] = jnp.where(mine, fin[...], half[...]).reshape(TALL, 128)[0:CLASSES]
        v = jnp.where(mine, fin_c[...], half_c[...])
        for g in range(4):
            cols = slice(256 * g + 128 * l, 256 * g + 128 * l + 128)
            gs1_ref[:, cols] = v[0:4, g].reshape(32, 128)
            gn1_ref[:, cols] = v[4:8, g].reshape(32, 128)


def shards(features, send_rows, send_count, tile_src, tile_val, labels, w_self1, w_neigh1, w_self2, w_neigh2):
    vm = lambda *shape, dt=F32: pltpu.VMEM(shape, dt)
    dma = pltpu.SemaphoreType.DMA
    whole = pl.BlockSpec(memory_space=pltpu.VMEM)
    half_class = jax.ShapeDtypeStruct((CLS_TILES, 8, 128), F32)
    half_first = jax.ShapeDtypeStruct((8, 4, 8, 128), F32)
    parts = pl.pallas_call(
        functools.partial(step_kernel, 1.0 / math.sqrt(ROWS * NODES)),
        out_shape=(half_class,) * 4 + (half_first,) * 2,
        in_specs=[pl.BlockSpec(memory_space=pltpu.SMEM)] + [whole] * 3 + [pl.BlockSpec(memory_space=pl.ANY)] + [whole] * 5,
        out_specs=(whole,) * 6,
        scratch_shapes=[
            vm(64, 128, 128, dt=BF), vm(4, 512, 128, dt=BF), vm(128, 128, dt=BF), vm(64, 128, dt=I32), vm(2, 256, 256),
            vm(512, 256, dt=BF), vm(8, 128, dt=I32), pltpu.SMEM((8, 128), I32),
            vm(64, 64, 512, dt=BF), vm(3, 1536, 512, dt=BF), vm(4, 3, 512, 384, dt=BF), vm(64, 128, 128, dt=BF), vm(36, 128, 128, dt=BF),
            vm(64, 128, 128), vm(64, 128, 128),
            vm(64, 16, 128, dt=BF), vm(64, 16, 128, dt=BF), vm(4, 128, 128, dt=BF),
            vm(4, 32, 256, dt=BF), vm(4, 32, 256, dt=BF), vm(128, 128, dt=BF), vm(4, 128, 128, dt=BF),
            vm(512, 128, dt=BF), vm(512, 128, dt=BF),
            vm(512, 256), vm(512, 256, dt=BF), vm(256, 512, dt=BF), vm(4, 512, 128),
            vm(4, 512, 128, dt=BF), vm(4, 256, 128, dt=BF), vm(4, 256, 128), vm(4, 256, 128, dt=BF),
            vm(4, 256, 128), vm(4, 256, 128),
            vm(64, MSG, 128, dt=BF), vm(64, MSG, 128, dt=BF), vm(4, 8, 128), vm(4, 8, 128), vm(4, 256, 128, dt=BF),
            vm(64, MSG, 128, dt=BF), vm(64, MSG, 128, dt=BF), vm(4, 256, 128, dt=BF),
            vm(512, 256, dt=BF), vm(256, 512, dt=BF), vm(512, 256, dt=BF),
            vm(2, TALL, 128), vm(TALL, 128), vm(2, TALL, 128), vm(TALL, 128), vm(2, 32, 8, 128), vm(32, 8, 128),
            vm(32, 8, 128), vm(32, 8, 128), vm(32, 8, 128), vm(8, 128), vm(8, 128), vm(8, 128), vm(4, 8, 128),
            dma, dma, dma, dma, dma((2,)), dma((2,)), dma, dma((4,)), dma, dma, dma, dma, dma, dma, dma, dma((4,)),
            dma, dma, dma, dma, dma, dma((4,)), dma, dma, dma((3,)), dma((3,)), dma((3,)), dma((3,)),
            dma, dma, dma((3,)), dma((3,)), dma((3,)), dma((3,)), dma, dma,
        ],
        compiler_params=pltpu.CompilerParams(
            collective_id=0, has_side_effects=True, vmem_limit_bytes=56 * 1024 * 1024
        ),
    )(
        tile_src, features.T, send_rows[0], send_count, tile_val.reshape(TILES, 128, 128), labels.reshape(4, 128),
        w_self1, w_neigh1, w_self2.T, w_neigh2.T,
    )
    loss, gs1, gn1, gs2, gn2 = pl.pallas_call(
        functools.partial(result_kernel, 1.0 / (ROWS * NODES)),
        out_shape=(
            jax.ShapeDtypeStruct((1, 1), F32),
            jax.ShapeDtypeStruct((32, 1024), F32),
            jax.ShapeDtypeStruct((32, 1024), F32),
            jax.ShapeDtypeStruct((CLASSES, 256), F32),
            jax.ShapeDtypeStruct((CLASSES, 256), F32),
        ),
        in_specs=[whole] * 6,
        out_specs=(whole,) * 5,
    )(*parts)
    return (loss[0, 0], gs1, gn1, gs2.T, gn2.T)


def solution(mesh):
    in_specs = (
        P("node", "feat"),
        P("node", None, None),
        P("node", None),
        P("node", None),
        P("node", None, None, None),
        P("node"),
        P("feat", None),
        P("feat", None),
        P("feat", None),
        P("feat", None),
    )
    out_specs = (P(), P("feat", None), P("feat", None), P("feat", None), P("feat", None))
    return jax.shard_map(shards, mesh=mesh, in_specs=in_specs, out_specs=out_specs, check_vma=False)
```

```python
import functools
import math

import jax
import jax.numpy as jnp
from jax import lax
from jax.experimental import pallas as pl
from jax.experimental.pallas import tpu as pltpu
from jax.sharding import PartitionSpec as P

MESH = pl.DeviceIdType.MESH
F32 = jnp.float32
BF = jnp.bfloat16
I32 = jnp.int32
ROWS = 512
SLOTS = 64
NODES = 64
FEATS = 4
CHIPS = NODES // 2
RINGS = 4
TILES = 64
CLASSES = 172
CLS = 43
TALL = 176
CLS_TILES = TALL // 8
MSG = 24
RING_ROWS = 16 * MSG
GELU_C = math.sqrt(2.0 / math.pi)


def lane_roll(value, shift):
    shift = shift % value.shape[-1]
    return pltpu.roll(value, shift, value.ndim - 1) if shift else value


def dot(a, b):
    return jnp.dot(a, b, preferred_element_type=F32)


def dot_nt(a, b):
    return lax.dot_general(a, b, (((1,), (1,)), ((), ())), preferred_element_type=F32)


def iota(shape, axis):
    return lax.broadcasted_iota(I32, shape, axis)


def split_third(w):
    n = w.shape[0]
    at = iota((n, 16, 128), 2)
    last = jnp.sum(jnp.where(at == iota((n, 16, 128), 1), w[:, 16:17, :], 0.0), axis=2, keepdims=True)
    return jnp.where(at == CLS - 1, last, w[:, 0:16, :])


def third_rest(col):
    shape = col.shape
    pick = (iota(shape, 2) == iota(shape, 1) + 2 * CLS) & (iota(shape, 1) < 16)
    return jnp.sum(jnp.where(pick, col, 0.0), axis=1, keepdims=True)


def step_kernel(
    grad_scale,
    tile_src_in, feat_in, rows_in, count_in, tiles_in, labels_in, w1s_in, w1n_in, w2s_in, w2n_in,
    fin_a, half_a, fin_b, half_b, fin_c, half_c,
    tile_src, feat_t, send_rows, send_count, labels, w1s, w1n, w2s_t, w2n_t, tiles, xcat, xsend, slot_col, wide, w2p_t, order_v, order,
    hot, hot3, hot_t, tiles_t, src, run, ptile,
    out1, recv1, xrecv, w1s_full, w1n_full, aggp, agg_recv, xfull, aggf,
    slope, hid, xa_t, pf, ycat, ypack, yown, yrecv, spack, srecv,
    out2, recv2, stat, hits, dlp, ret, recvb, gp, dlcat, dlcat_t, gcat,
    da, pa, db, pb, dc, pc, ra, rb, rc, ta, tb, tc, trecv,
    s_load, s_order, s_x, r_x, s_w, r_w, s_e1, r_e1, s_agg, r_agg, s_y, r_y, s_s, r_s, s_e2, r_e2,
    s_st, r_st, s_dl, r_dl, s_eb, r_eb, s_g, r_g, s_pair, r_pair, s_red, r_red,
    s_t, r_t, s_fin, r_fin, s_half, r_half, s_hit, r_hit,
):
    me = lax.axis_index("node")
    f = lax.axis_index("feat")
    chip, core = me // 2, lax.rem(me, 2)
    ring, place = me // 16, lax.rem(me // 2, 8)
    partner = me + 1 - 2 * core

    def wait_bytes(ref, sem):
        pltpu.make_async_copy(ref, ref, sem).wait()

    def send(s, d, ssem, rsem, node, feat):
        pltpu.make_async_remote_copy(
            src_ref=s, dst_ref=d, send_sem=ssem, recv_sem=rsem,
            device_id=(node, feat), device_id_type=MESH,
        ).start()

    def to_feats(s, d, ssem, rsem, same=False):
        for i in (2, 1, 3):
            g = lax.rem(f + i, FEATS)
            send(s if same else s.at[g], d.at[f], ssem, rsem, me, g)

    def place_at(k):
        off = ((k + 1) // 2) * (2 * lax.rem(k, 2) - 1)
        return lax.rem(place + off + 8, 8)

    def ring_at(j):
        return lax.rem(ring + (2, 1, 3, 0)[j], RINGS)

    lane = lambda r, n=128: iota((r, n), 1)
    three = pl.ds(0, FEATS - 1)

    loads = [
        pltpu.make_async_copy(a, b, s_load.at[k])
        for k, (a, b) in enumerate((
            (rows_in, send_rows), (count_in, send_count), (feat_in, feat_t), (w1s_in, w1s), (w1n_in, w1n),
            (tile_src_in, tile_src), (w2s_in, w2s_t), (w2n_in, w2n_t), (labels_in, labels), (tiles_in, tiles),
        ))
    ]
    for load in loads:
        load.start()

    bar = pltpu.get_barrier_semaphore()

    def hello(i, c):
        pl.semaphore_signal(bar, inc=1, device_id=(lax.rem(me + i, NODES), f), device_id_type=MESH)
        return c

    for lo, hi in ((25, 40), (1, 25), (40, NODES)):
        lax.fori_loop(lo, hi, hello, 0)
    for i in range(1, FEATS):
        pl.semaphore_signal(bar, inc=1, device_id=(me, lax.rem(f + i, FEATS)), device_id_type=MESH)

    for load in loads[0:3]:
        load.wait()

    x0 = jnp.transpose(jnp.concatenate([feat_t[...].astype(F32), jnp.zeros((96, ROWS), F32)], axis=0))
    for q in range(4):
        shifted = lane_roll(x0, 32 * q)
        xcat[q] = shifted.astype(BF)
        part = shifted[128 * q:128 * q + 128]
        xpack = part if q == 0 else xpack + part
    xsend[...] = xpack.astype(BF)

    wide[0, 0:64, 0:64] = send_rows[...].astype(F32)
    turned = jnp.transpose(wide[0, 0:128, 0:128]).astype(I32)[0:64]
    counts = jnp.concatenate([send_count[...], jnp.zeros((1, 64), I32)], axis=1)
    slot_col[...] = jnp.where(iota((64, 128), 0) < counts, turned, -1)

    def build_hot(d, c):
        col = jnp.sum(jnp.where(lane(SLOTS) == d, slot_col[...], 0), axis=1, keepdims=True)
        hot[d] = jnp.where(col == lane(SLOTS, ROWS), 1.0, 0.0).astype(BF)
        return c

    lax.fori_loop(0, NODES, build_hot, 0, unroll=8)

    def pack1(m, c):
        d0 = pl.multiple_of(m * 32, 32)
        acc = jnp.zeros((512, 128), F32)
        for q in range(4):
            acc = acc + dot(hot[pl.ds(d0, 32), 16 * q:16 * q + 16, :].reshape(512, ROWS), xcat[q])
        out1[pl.ds(d0, 32)] = acc.astype(BF).reshape(32, 16, 128)
        return c

    lax.fori_loop(0, 2, pack1, 0)
    recv1[me] = out1[me]
    xrecv[f] = xsend[...]
    for load in loads[3:9]:
        load.wait()
    pl.semaphore_wait(bar, NODES - 1 + FEATS - 1)

    for j in range(RINGS):
        rr = ring_at(j)

        def send1(k, c):
            k = (16 if j < 3 else 15) - 1 - k + (0 if j < 3 else 1)
            p = rr * 16 + place_at(k // 2) * 2 + lax.rem(core + k, 2)
            send(out1.at[p], recv1.at[me], s_e1, r_e1.at[ring], p, f)
            return c

        lax.fori_loop(0, 16 if j < 3 else 15, send1, 0)
    for i in (2, 1, 3):
        g = lax.rem(f + i, FEATS)
        cols = pl.ds(pl.multiple_of(g * 256, 256), 256)
        send(xsend, xrecv.at[f], s_x, r_x, me, g)
        send(w1s.at[:, cols], w1s_full.at[f], s_w.at[0], r_w.at[0], me, g)
        send(w1n.at[:, cols], w1n_full.at[f], s_w.at[1], r_w.at[1], me, g)

    own_cols = pl.ds(pl.multiple_of(f * 256, 256), 256)
    w1s_full[f] = w1s[:, own_cols]
    w1n_full[f] = w1n[:, own_cols]
    for b in range(4):
        src[b] = xcat[0, 128 * b:128 * b + 128, :]

    for part, ref in enumerate((w2s_t, w2n_t)):
        wide[0, 0:CLASSES, 0:256] = ref[...].astype(F32)
        wide[1] = jnp.zeros((256, 256), F32)
        for g in range(4):
            wide[1, 64 * g:64 * g + CLS, :] = wide[0, CLS * g:CLS * g + CLS, 0:256]
        w2p_t[256 * part:256 * part + 256, :] = wide[1].astype(BF)

    srow = jnp.full((128, 128), 1 << 20, I32)
    for t in range(TILES):
        srow = jnp.where(lane(128) == t, tile_src[t // 16, t % 16], srow)
    scol = jnp.transpose(srow)
    sub = iota((128, 128), 0)
    lane128 = lane(128)
    same = (srow == scol) & (lane128 < sub)
    rank = jnp.sum(jnp.where((srow < scol) | same, 1, 0), axis=1, keepdims=True)
    goes = jnp.minimum(jnp.sum(jnp.where(same, 1, 0), axis=1, keepdims=True), 1)
    at = rank == lane128
    order_v[...] = jnp.zeros((8, 128), I32)
    order_v[0:1, :] = jnp.sum(jnp.where(at, sub, 0), axis=0, keepdims=True)
    order_v[1:2, :] = jnp.sum(jnp.where(at, goes, 0), axis=0, keepdims=True)
    upto = jnp.sum(jnp.where(scol <= lane128, 1, 0), axis=0, keepdims=True)
    order_v[2:3, :] = jnp.maximum(upto - 1, 0)
    order_v[3:4, :] = jnp.minimum(jnp.sum(jnp.where(scol == lane128, 1, 0), axis=0, keepdims=True), 1)
    order_copy = pltpu.make_async_copy(order_v, order, s_order)
    order_copy.start()

    def build_hot3(m, c):
        cols = []
        for d in (2 * m, 2 * m + 1):
            cols.append(jnp.sum(jnp.where(lane(SLOTS) == d, slot_col[...], 0), axis=1, keepdims=True))
        none = jnp.full((8, 1), -1, I32)
        at = pl.ds(pl.multiple_of(m * 48, 48), 48)
        for k, rows in enumerate((
            [cols[0][0:24], cols[1][0:24]],
            [cols[0][24:48], cols[1][24:48]],
            [cols[0][48:64], none, cols[1][48:64], none],
        )):
            col = jnp.concatenate(rows, axis=0)
            hot3[k, at, :] = jnp.where(col == lane(48, ROWS), 1.0, 0.0).astype(BF)
        return c

    lax.fori_loop(0, NODES // 2, build_hot3, 0, unroll=4)
    loads[9].wait()

    def turn(t, c):
        tiles_t[t] = jnp.transpose(tiles[t])
        return c

    lax.fori_loop(0, TILES, turn, 0, unroll=4)
    order_copy.wait()

    def row_bytes(buf, j):
        return buf.at[pl.ds(0, 15 if j == 3 else 16)]

    group = lane128 // 32

    def unpack_feats(ref, out):
        for b in range(4):
            acc = jnp.zeros((128, 128), F32)
            for g in range(4):
                acc = jnp.where(group == g, lane_roll(ref[g].astype(F32), 32 * (g - b)), acc)
            out[128 * b:128 * b + 128, :] = acc.astype(BF)

    wait_bytes(xrecv.at[three], r_x)
    wait_bytes(w1s_full.at[three], r_w.at[0])
    unpack_feats(xrecv, xfull)
    slope[...] = dot(xfull[...], w1s_full[...].reshape(128, 256))
    xa_t[0:128, :] = jnp.transpose(xfull[...])

    for j in (3, 1, 2, 0):
        rr = ring_at(j)
        wait_bytes(row_bytes(recv1, j), r_e1.at[rr])

        def unpack1(k, c):
            b = rr * 8 + k
            for p in range(2):
                v = recv1[2 * b + p].astype(F32)
                for q in range(4):
                    src[4 + b, 64 * p + 16 * q:64 * p + 16 * q + 16, :] = lane_roll(v, -32 * q).astype(BF)
            return c

        lax.fori_loop(0, 8, unpack1, 0, unroll=4)

    def tile_product(b):
        lhs = jnp.concatenate([tiles[16 * b + k] for k in range(16)], axis=1)
        rhs = jnp.concatenate([src[tile_src[b, k]] for k in range(16)], axis=0)
        return dot(lhs, rhs)

    packed = jnp.zeros((128, 128), F32)
    for b in range(4):
        packed = packed + lane_roll(jnp.where(group == 0, tile_product(b), 0.0), 32 * b)
    aggp[...] = packed.astype(BF)
    to_feats(aggp, agg_recv, s_agg, r_agg, same=True)
    agg_recv[f] = aggp[...]

    wait_bytes(w1n_full.at[three], r_w.at[1])
    wait_bytes(agg_recv.at[three], r_agg)
    unpack_feats(agg_recv, aggf)

    pre = slope[...] + dot(aggf[...], w1n_full[...].reshape(128, 256))
    th = jnp.tanh(GELU_C * (pre + 0.044715 * (pre * pre * pre)))
    cdf = 0.5 * (1.0 + th)
    slope[...] = cdf + pre * (0.5 * (1.0 - th * th)) * (GELU_C * (1.0 + 3.0 * 0.044715 * (pre * pre)))
    hid[...] = (pre * cdf).astype(BF)

    low256 = lane(256) < 64

    def pack_halves(v, g):
        a, b = v[0:256], v[256:512]
        return jnp.where(low256, a if g % 2 == 0 else lane_roll(a, 64), lane_roll(b, 64) if g % 2 == 0 else b)

    for half in range(2):
        v = dot_nt(hid[...], w2p_t[256 + 128 * half:256 + 128 * half + 128, :])
        for g in (2 * half, 2 * half + 1):
            yv = pack_halves(v, g)
            yown[g] = yv
            ypack[g] = yv.astype(BF)
    to_feats(ypack, yrecv, s_y, r_y)
    for half in range(2):
        v = dot_nt(hid[...], w2p_t[128 * half:128 * half + 128, :])
        for g in (2 * half, 2 * half + 1):
            spack[g] = pack_halves(v, g)
    to_feats(spack, srecv, s_s, r_s)
    yrecv[f] = jnp.zeros((256, 128), BF)
    srecv[f] = spack[f]
    wait_bytes(yrecv.at[three], r_y)
    ys = yown[f]
    for g in range(4):
        ys = ys + yrecv[g].astype(F32)
    yr = lane_roll(ys, 64)
    y_lo = jnp.concatenate([jnp.where(low256, ys, 0.0), jnp.where(low256, yr, 0.0)], axis=0)
    ycat[0] = y_lo.astype(BF)
    ycat[1] = lane_roll(y_lo, CLS).astype(BF)
    ycat[2] = lane_roll(jnp.where(lane(ROWS) < CLS - 1, y_lo, 0.0), 2 * CLS).astype(BF)
    ycat[3] = jnp.broadcast_to(y_lo[:, CLS - 1:CLS], (ROWS, 128)).astype(BF)

    for j in range(RINGS):
        rr = ring_at(j)
        d0 = pl.multiple_of(rr * 16, 16)
        at = pl.ds(pl.multiple_of(rr * RING_ROWS, RING_ROWS), RING_ROWS)
        third = hot3[2, at, :]
        acc = dot(hot3[0, at, :], ycat[0]) + dot(hot3[1, at, :], ycat[1]) + dot(third, ycat[2])
        acc = acc.reshape(16, MSG, 128)
        rest = third_rest(dot(third, ycat[3]).reshape(16, MSG, 128))
        acc = jnp.where((iota((16, MSG, 128), 1) == 16) & (iota((16, MSG, 128), 2) >= 2 * CLS), rest, acc)
        out2[pl.ds(d0, 16)] = acc.astype(BF)

        def send2(k, c):
            k = (16 if j < 3 else 15) - 1 - k + (0 if j < 3 else 1)
            p = rr * 16 + place_at(k // 2) * 2 + lax.rem(core + k, 2)
            send(out2.at[p], recv2.at[me], s_e2, r_e2.at[ring], p, f)
            return c

        lax.fori_loop(0, 16 if j < 3 else 15, send2, 0)

    recv2[me] = out2[me]
    for b in range(4):
        src[b] = ycat[0, 128 * b:128 * b + 128, :]
    xa_t[128:256, :] = jnp.transpose(aggf[...])

    def turn_hot(y, c):
        for h in range(3):
            for k in range(4):
                part = hot3[h, pl.ds(pl.multiple_of(y * RING_ROWS, RING_ROWS), RING_ROWS), 128 * k:128 * k + 128]
                hot_t[y, h, 128 * k:128 * k + 128, :] = jnp.transpose(part)
        return c

    lax.fori_loop(0, RINGS, turn_hot, 0)

    for j in (3, 1, 2, 0):
        rr = ring_at(j)
        wait_bytes(row_bytes(recv2, j), r_e2.at[rr])

        def unpack2(k, c):
            b = rr * 8 + k
            v = recv2[pl.ds(2 * b, 2)].astype(F32)
            both = jnp.concatenate([v, lane_roll(v, -CLS), split_third(lane_roll(v, -2 * CLS))], axis=1)
            src[4 + b] = both.reshape(128, 128).astype(BF)
            return c

        lax.fori_loop(0, 8, unpack2, 0, unroll=4)

    wait_bytes(srecv.at[three], r_s)
    ss = srecv[0] + srecv[1] + srecv[2] + srecv[3]
    pf[0, 0:256, :] = ss
    pf[0, 256:512, :] = lane_roll(ss, 64)

    mine = lane128 < CLS
    for b in range(4):
        r = slice(128 * b, 128 * b + 128)
        lg = jnp.where(mine, pf[0, r, :] + tile_product(b), -1e30)
        top = jnp.max(lg, axis=1, keepdims=True)
        ex = jnp.exp(lg - top)
        tot = jnp.sum(ex, axis=1, keepdims=True)
        lab = jnp.transpose(jnp.broadcast_to(labels[b:b + 1, :].astype(F32), (128, 128))).astype(I32)
        want = mine & ((lab - CLS * f) == lane128)
        hit = jnp.sum(jnp.where(want, lg, 0.0), axis=1, keepdims=True)
        st = jnp.where(lane128 == 0, top, jnp.where(lane128 == 1, tot, jnp.where(lane128 == 2, hit, 0.0)))
        st_t = jnp.transpose(st)
        stat[f, b:b + 1, :] = st_t[0:1]
        stat[f, 4 + b:5 + b, :] = st_t[1:2]
        hits[f, b:b + 1, :] = st_t[2:3]
        pf[1, r, :] = ex
        pf[2, r, :] = jnp.where(want, 1.0, 0.0)
    to_feats(stat.at[f], stat, s_st, r_st, same=True)
    wait_bytes(stat.at[three], r_st)

    tops = [stat[g, 0:4, :] for g in range(4)]
    best = jnp.maximum(jnp.maximum(tops[0], tops[1]), jnp.maximum(tops[2], tops[3]))
    total = jnp.zeros_like(best)
    for g in range(4):
        total = total + stat[g, 4:8, :] * jnp.exp(tops[g] - best)
    factor = jnp.exp(stat[f, 0:4, :] - best) / total
    for b in range(4):
        r = slice(128 * b, 128 * b + 128)
        fac = jnp.transpose(jnp.broadcast_to(factor[b:b + 1, :], (128, 128)))
        dl = ((pf[1, r, :] * fac - pf[2, r, :]) * grad_scale).astype(BF)
        rows = slice(128 * (b % 2), 128 * (b % 2) + 128)
        if b < 2:
            dlp[f, rows, :] = dl
        else:
            dlp[f, rows, :] = (dlp[f, rows, :].astype(F32) + lane_roll(dl.astype(F32), 64)).astype(BF)
        lhs = tiles_t[16 * b:16 * b + 16].reshape(2048, 128)
        ptile[16 * b:16 * b + 16] = dot(lhs, dl).reshape(16, 128, 128)
    to_feats(dlp.at[f], dlp, s_dl, r_dl, same=True)
    to_feats(hits.at[f], hits, s_hit, r_hit, same=True)

    def gather_sum(t, acc):
        acc = acc * order[1, t].astype(F32) + ptile[order[0, t]]
        run[t] = acc
        return acc

    lax.fori_loop(0, TILES, gather_sum, jnp.zeros((128, 128), F32), unroll=4)

    def landed(j):
        return run[order[2, j]] * order[3, j].astype(F32)

    for j in range(RINGS):
        rr = ring_at(j)

        def pack_back(k, c):
            to = rr * 8 + place_at(7 - k)
            blk = landed(4 + to)
            blk = blk.reshape(2, 64, 128)
            third = blk[:, 48:64, :]
            rest = third_rest(jnp.broadcast_to(third[:, :, CLS - 1:CLS], (2, 16, 128)))
            rest = jnp.where(iota((2, 8, 128), 1) == 0, rest, 0.0)
            turned3 = lane_roll(jnp.where(iota((2, 16, 128), 2) < CLS - 1, third, 0.0), 2 * CLS)
            v = blk[:, 0:24, :] + lane_roll(blk[:, 24:48, :], CLS) + jnp.concatenate([turned3, rest], axis=1)
            ret[pl.ds(2 * to, 2)] = v.astype(BF)
            return c

        lax.fori_loop(0, 8, pack_back, 0, unroll=4)

        def send_back(k, c):
            k = (16 if j < 3 else 15) - 1 - k + (0 if j < 3 else 1)
            p = rr * 16 + place_at(k // 2) * 2 + lax.rem(core + k, 2)
            send(ret.at[p], recvb.at[me], s_eb, r_eb.at[ring], p, f)
            return c

        lax.fori_loop(0, 16 if j < 3 else 15, send_back, 0)

    recvb[me] = ret[me]
    for b in range(4):
        pf[3, 128 * b:128 * b + 128, :] = landed(b)

    def join(ref, out):
        for pair in range(2):
            c = slice(128 * pair, 128 * pair + 128)
            a, b = ref[2 * pair].astype(F32), ref[2 * pair + 1].astype(F32)
            out[0:256, c] = jnp.where(low256, a, lane_roll(b, 64)).astype(BF)
            out[256:512, c] = jnp.where(low256, lane_roll(a, 64), b).astype(BF)

    def class_rows(v, d):
        for l in range(2):
            d[l, TALL - 8:TALL, :] = jnp.zeros((8, 128), F32)
            for g in range(4):
                d[l, CLS * g:CLS * g + CLS, :] = v[64 * g:64 * g + CLS, 128 * l:128 * l + 128]

    def rows8(t):
        return pl.ds(pl.multiple_of(t * 8, 8), 8)

    def chip_at(i):
        return lax.rem(ring + (i // 8) + 4, RINGS) * 8 + place_at(lax.rem(i, 8))

    def for_chips(body):
        lax.fori_loop(1, CHIPS, lambda i, c: (body(chip_at(CHIPS - i)), c)[1], 0)

    def reduce_class(d, peer, part, k):
        wait_bytes(peer, r_pair.at[k])
        d[core] = d[core] + peer[...]

        def one(p):
            @pl.when(p < CLS_TILES)
            def _():
                send(d.at[core, rows8(p)], part.at[chip], s_red.at[k], r_red.at[k], 2 * p + core, f)

        for_chips(one)

        @pl.when(chip < CLS_TILES)
        def _():
            part[chip] = d[core, rows8(chip), :]

    def spread_class(part, tile, fin, k):
        @pl.when(chip < CLS_TILES)
        def _():
            wait_bytes(part.at[pl.ds(0, CHIPS - 1)], r_red.at[k])
            tile[...] = jnp.sum(part[...], axis=0)
            for_chips(lambda p: send(tile, fin.at[chip], s_fin.at[k], r_fin.at[k], 2 * p + core, f))
            fin[chip] = tile[...]

    def gather_class(fin, half, k):
        @pl.when(chip < CLS_TILES)
        def _():
            wait_bytes(fin.at[pl.ds(0, CLS_TILES - 1)], r_fin.at[k])

        @pl.when(chip >= CLS_TILES)
        def _():
            wait_bytes(fin, r_fin.at[k])

        send(fin, half, s_half.at[k], r_half.at[k], partner, f)

    wait_bytes(hits.at[three], r_hit)
    hit_sum = hits[0, 0:4, :] + hits[1, 0:4, :] + hits[2, 0:4, :] + hits[3, 0:4, :]
    loss = jnp.sum(jnp.log(total) + best - hit_sum)
    wait_bytes(dlp.at[three], r_dl)
    join(dlp, dlcat)
    dlcat_t[...] = jnp.transpose(dlcat[...])
    class_rows(dot(dlcat_t[...], hid[...]), da)
    tail = (iota((8, 128), 0) == 7) & (lane(8) == 0)
    for l in range(2):
        da[l, TALL - 8:TALL, :] = da[l, TALL - 8:TALL, :] + jnp.where(tail, loss, 0.0)
    send(da.at[1 - core], pa, s_pair.at[0], r_pair.at[0], partner, f)
    reduce_class(da, pa, ra, 0)

    g_sum = pf[3]
    valid = lane(ROWS) < CLS
    for j in (3, 1, 2, 0):
        rr = ring_at(j)
        wait_bytes(row_bytes(recvb, j), r_eb.at[rr])
        back = recvb[pl.ds(pl.multiple_of(rr * 16, 16), 16)].astype(F32)
        third = split_third(lane_roll(back, -2 * CLS))
        third = jnp.concatenate([third, jnp.zeros((16, 8, 128), F32)], axis=1).reshape(RING_ROWS, 128).astype(BF)
        back = back.reshape(RING_ROWS, 128).astype(BF)
        g_sum = g_sum + jnp.where(valid, dot(hot_t[rr, 0], back) + dot(hot_t[rr, 2], third), 0.0)
        g_sum = g_sum + jnp.where(valid, lane_roll(dot(hot_t[rr, 1], back), -CLS), 0.0)
    gp[f] = (g_sum[0:256] + lane_roll(g_sum[256:512], 64)).astype(BF)
    to_feats(gp.at[f], gp, s_g, r_g, same=True)
    spread_class(ra, ta, fin_a, 0)
    bh0 = dot(dlcat[...], w2p_t[0:256, :])
    wait_bytes(gp.at[three], r_g)
    join(gp, gcat)

    bh = bh0 + dot(gcat[...], w2p_t[256:512, :])
    g1 = dot(xa_t[...], (bh * slope[...]).astype(BF))
    for l in range(2):
        dc[l] = g1[:, 128 * l:128 * l + 128]
    send(dc.at[1 - core], pc, s_pair.at[2], r_pair.at[2], partner, f)
    class_rows(dot(jnp.transpose(gcat[...]), hid[...]), db)
    send(db.at[1 - core], pb, s_pair.at[1], r_pair.at[1], partner, f)
    wait_bytes(pc, r_pair.at[2])
    dc[core] = dc[core] + pc[...]

    def rows1(p):
        m = p // 4
        return pl.ds(pl.multiple_of((m // 4) * 128 + 32 * lax.rem(f + lax.rem(p, 4), 4) + 8 * lax.rem(m, 4), 8), 8)

    for_chips(lambda p: send(dc.at[core, rows1(p)], rc.at[chip], s_red.at[2], r_red.at[2], 2 * p + core, f))
    rc[chip] = dc[core, rows1(chip), :]
    reduce_class(db, pb, rb, 1)

    wait_bytes(rc.at[pl.ds(0, CHIPS - 1)], r_red.at[2])
    tc[...] = jnp.sum(rc[...], axis=0)
    turn_by = lax.rem(chip, 4)
    came_from = lax.rem(f - turn_by + 4, 4)

    @pl.when(turn_by > 0)
    def _():
        send(tc, trecv, s_t, r_t, me, lax.rem(f + turn_by, 4))

    spread_class(rb, tb, fin_b, 1)

    @pl.when(turn_by > 0)
    def _():
        wait_bytes(trecv, r_t)

    @pl.when(turn_by == 0)
    def _():
        trecv[...] = tc[...]

    for_chips(lambda p: send(trecv, fin_c.at[chip // 4, came_from], s_fin.at[2], r_fin.at[2], 2 * p + core, f))
    fin_c[chip // 4, came_from] = trecv[...]

    gather_class(fin_a, half_a, 0)
    gather_class(fin_b, half_b, 1)

    wait_bytes(rc.at[pl.ds(0, CHIPS - 1)], r_fin.at[2])
    send(fin_c, half_c, s_half.at[2], r_half.at[2], partner, f)

    n63, c31 = pl.ds(0, NODES - 1), pl.ds(0, CHIPS - 1)
    wait_bytes(recv1.at[n63], s_e1)
    wait_bytes(xrecv.at[three], s_x)
    wait_bytes(w1s_full.at[three], s_w.at[0])
    wait_bytes(w1n_full.at[three], s_w.at[1])
    wait_bytes(agg_recv.at[three], s_agg)
    wait_bytes(yrecv.at[three], s_y)
    wait_bytes(srecv.at[three], s_s)
    wait_bytes(recv2.at[n63], s_e2)
    wait_bytes(stat.at[three], s_st)
    wait_bytes(dlp.at[three], s_dl)
    wait_bytes(hits.at[three], s_hit)
    wait_bytes(recvb.at[n63], s_eb)
    wait_bytes(gp.at[three], s_g)
    wait_bytes(pa, s_pair.at[0])
    wait_bytes(pb, s_pair.at[1])
    wait_bytes(pc, s_pair.at[2])
    wait_bytes(rc.at[c31], s_red.at[2])
    for k, part in ((0, ra), (1, rb)):
        @pl.when(chip < CLS_TILES)
        def _():
            wait_bytes(part.at[pl.ds(0, CLS_TILES - 1)], s_red.at[k])
            wait_bytes(part.at[c31], s_fin.at[k])

        @pl.when(chip >= CLS_TILES)
        def _():
            wait_bytes(part.at[pl.ds(0, CLS_TILES)], s_red.at[k])

    wait_bytes(rc.at[c31], s_fin.at[2])

    @pl.when(turn_by > 0)
    def _():
        wait_bytes(trecv, s_t)

    for k, ref in enumerate((half_a, half_b, half_c)):
        wait_bytes(ref, s_half.at[k])
        wait_bytes(ref, r_half.at[k])


def result_kernel(scale, fin_a, half_a, fin_b, half_b, fin_c, half_c, loss_ref, gs1_ref, gn1_ref, gs2_ref, gn2_ref):
    core = lax.rem(lax.axis_index("node"), 2)
    first = core == 0
    loss_ref[...] = fin_a[CLS_TILES - 1, 7:8, 0:1] * scale
    for l in range(2):
        c = slice(128 * l, 128 * l + 128)
        mine = first if l == 0 else jnp.logical_not(first)
        for fin, half, ref in ((fin_a, half_a, gs2_ref), (fin_b, half_b, gn2_ref)):
            ref[:, c] = jnp.where(mine, fin[...], half[...]).reshape(TALL, 128)[0:CLASSES]
        v = jnp.where(mine, fin_c[...], half_c[...])
        for g in range(4):
            cols = slice(256 * g + 128 * l, 256 * g + 128 * l + 128)
            gs1_ref[:, cols] = v[0:4, g].reshape(32, 128)
            gn1_ref[:, cols] = v[4:8, g].reshape(32, 128)


def shards(features, send_rows, send_count, tile_src, tile_val, labels, w_self1, w_neigh1, w_self2, w_neigh2):
    vm = lambda *shape, dt=F32: pltpu.VMEM(shape, dt)
    dma = pltpu.SemaphoreType.DMA
    whole = pl.BlockSpec(memory_space=pltpu.VMEM)
    half_class = jax.ShapeDtypeStruct((CLS_TILES, 8, 128), F32)
    half_first = jax.ShapeDtypeStruct((8, 4, 8, 128), F32)
    parts = pl.pallas_call(
        functools.partial(step_kernel, 1.0 / math.sqrt(ROWS * NODES)),
        out_shape=(half_class,) * 4 + (half_first,) * 2,
        in_specs=[pl.BlockSpec(memory_space=pltpu.HBM)] * 10,
        out_specs=(whole,) * 6,
        scratch_shapes=[
            pltpu.SMEM((4, 16), I32), vm(32, 512, dt=BF), vm(64, 64, dt=I32), vm(1, 64, dt=I32), vm(4, 128, dt=I32),
            vm(32, 1024, dt=BF), vm(32, 1024, dt=BF), vm(CLASSES, 256, dt=BF), vm(CLASSES, 256, dt=BF),
            vm(64, 128, 128, dt=BF), vm(4, 512, 128, dt=BF), vm(128, 128, dt=BF), vm(64, 128, dt=I32), vm(2, 256, 256),
            vm(512, 256, dt=BF), vm(8, 128, dt=I32), pltpu.SMEM((8, 128), I32),
            vm(64, 64, 512, dt=BF), vm(3, 1536, 512, dt=BF), vm(4, 3, 512, 384, dt=BF), vm(64, 128, 128, dt=BF), vm(36, 128, 128, dt=BF),
            vm(64, 128, 128), vm(64, 128, 128),
            vm(64, 16, 128, dt=BF), vm(64, 16, 128, dt=BF), vm(4, 128, 128, dt=BF),
            vm(4, 32, 256, dt=BF), vm(4, 32, 256, dt=BF), vm(128, 128, dt=BF), vm(4, 128, 128, dt=BF),
            vm(512, 128, dt=BF), vm(512, 128, dt=BF),
            vm(512, 256), vm(512, 256, dt=BF), vm(256, 512, dt=BF), vm(4, 512, 128),
            vm(4, 512, 128, dt=BF), vm(4, 256, 128, dt=BF), vm(4, 256, 128), vm(4, 256, 128, dt=BF),
            vm(4, 256, 128), vm(4, 256, 128),
            vm(64, MSG, 128, dt=BF), vm(64, MSG, 128, dt=BF), vm(4, 8, 128), vm(4, 8, 128), vm(4, 256, 128, dt=BF),
            vm(64, MSG, 128, dt=BF), vm(64, MSG, 128, dt=BF), vm(4, 256, 128, dt=BF),
            vm(512, 256, dt=BF), vm(256, 512, dt=BF), vm(512, 256, dt=BF),
            vm(2, TALL, 128), vm(TALL, 128), vm(2, TALL, 128), vm(TALL, 128), vm(2, 256, 128), vm(256, 128),
            vm(32, 8, 128), vm(32, 8, 128), vm(32, 8, 128), vm(8, 128), vm(8, 128), vm(8, 128), vm(8, 128),
            dma((10,)), dma, dma, dma, dma((2,)), dma((2,)), dma, dma((4,)), dma, dma, dma, dma, dma, dma, dma, dma((4,)),
            dma, dma, dma, dma, dma, dma((4,)), dma, dma, dma((3,)), dma((3,)), dma((3,)), dma((3,)),
            dma, dma, dma((3,)), dma((3,)), dma((3,)), dma((3,)), dma, dma,
        ],
        compiler_params=pltpu.CompilerParams(
            collective_id=0, has_side_effects=True, vmem_limit_bytes=56 * 1024 * 1024
        ),
    )(
        tile_src, features.T, send_rows[0], send_count, tile_val.reshape(TILES, 128, 128), labels.reshape(4, 128),
        w_self1, w_neigh1, w_self2.T, w_neigh2.T,
    )
    loss, gs1, gn1, gs2, gn2 = pl.pallas_call(
        functools.partial(result_kernel, 1.0 / (ROWS * NODES)),
        out_shape=(
            jax.ShapeDtypeStruct((1, 1), F32),
            jax.ShapeDtypeStruct((32, 1024), F32),
            jax.ShapeDtypeStruct((32, 1024), F32),
            jax.ShapeDtypeStruct((CLASSES, 256), F32),
            jax.ShapeDtypeStruct((CLASSES, 256), F32),
        ),
        in_specs=[whole] * 6,
        out_specs=(whole,) * 5,
    )(*parts)
    return (loss[0, 0], gs1, gn1, gs2.T, gn2.T)


def solution(mesh):
    in_specs = (
        P("node", "feat"),
        P("node", None, None),
        P("node", None),
        P("node", None),
        P("node", None, None, None),
        P("node"),
        P("feat", None),
        P("feat", None),
        P("feat", None),
        P("feat", None),
    )
    out_specs = (P(), P("feat", None), P("feat", None), P("feat", None), P("feat", None))
    return jax.shard_map(shards, mesh=mesh, in_specs=in_specs, out_specs=out_specs, check_vma=False)
```

```python
import functools
import math

import jax
import jax.numpy as jnp
from jax import lax
from jax.experimental import pallas as pl
from jax.experimental.pallas import tpu as pltpu
from jax.sharding import PartitionSpec as P

MESH = pl.DeviceIdType.MESH
F32 = jnp.float32
BF = jnp.bfloat16
I32 = jnp.int32
ROWS = 512
SLOTS = 64
NODES = 64
FEATS = 4
CHIPS = NODES // 2
RINGS = 4
TILES = 64
CLASSES = 172
CLS = 43
TALL = 176
CLS_TILES = TALL // 8
MSG = 24
RING_ROWS = 16 * MSG
GELU_C = math.sqrt(2.0 / math.pi)


def lane_roll(value, shift):
    shift = shift % value.shape[-1]
    return pltpu.roll(value, shift, value.ndim - 1) if shift else value


def dot(a, b):
    return jnp.dot(a, b, preferred_element_type=F32)


def dot_nt(a, b):
    return lax.dot_general(a, b, (((1,), (1,)), ((), ())), preferred_element_type=F32)


def iota(shape, axis):
    return lax.broadcasted_iota(I32, shape, axis)


def split_third(w):
    n = w.shape[0]
    at = iota((n, 16, 128), 2)
    last = jnp.sum(jnp.where(at == iota((n, 16, 128), 1), w[:, 16:17, :], 0.0), axis=2, keepdims=True)
    return jnp.where(at == CLS - 1, last, w[:, 0:16, :])


def third_rest(col):
    shape = col.shape
    pick = (iota(shape, 2) == iota(shape, 1) + 2 * CLS) & (iota(shape, 1) < 16)
    return jnp.sum(jnp.where(pick, col, 0.0), axis=1, keepdims=True)


def step_kernel(
    grad_scale,
    tile_src_in, feat_in, rows_in, count_in, tiles_in, labels_in, w1s_in, w1n_in, w2s_in, w2n_in,
    fin_a, half_a, fin_b, half_b, fin_c, half_c,
    tile_src, feat_t, send_rows, send_count, labels, w1s, w1n, w2s_t, w2n_t, tiles, xcat, xsend, slot_col, wide, w2p_t, order_v, order,
    hot, hot3, hot_t, tiles_t, src, run, ptile,
    out1, recv1, xrecv, w1s_full, w1n_full, aggp, agg_recv, xfull, aggf,
    slope, hid, xa_t, pf, ycat, ypack, yown, yrecv, spack, srecv,
    out2, recv2, stat, hits, dlp, ret, recvb, gp, dlcat, dlcat_t, gcat,
    da, pa, db, pb, dc, pc, ra, rb, rc, ta, tb, tc, trecv,
    s_load, s_order, s_x, r_x, s_w, r_w, s_e1, r_e1, s_agg, r_agg, s_y, r_y, s_s, r_s, s_e2, r_e2,
    s_st, r_st, s_dl, r_dl, s_eb, r_eb, s_g, r_g, s_pair, r_pair, s_red, r_red,
    s_t, r_t, s_fin, r_fin, s_half, r_half, s_hit, r_hit,
):
    me = lax.axis_index("node")
    f = lax.axis_index("feat")
    chip, core = me // 2, lax.rem(me, 2)
    ring, place = me // 16, lax.rem(me // 2, 8)
    partner = me + 1 - 2 * core

    def wait_bytes(ref, sem):
        pltpu.make_async_copy(ref, ref, sem).wait()

    def send(s, d, ssem, rsem, node, feat):
        pltpu.make_async_remote_copy(
            src_ref=s, dst_ref=d, send_sem=ssem, recv_sem=rsem,
            device_id=(node, feat), device_id_type=MESH,
        ).start()

    def to_feats(s, d, ssem, rsem, same=False):
        for i in (2, 1, 3):
            g = lax.rem(f + i, FEATS)
            send(s if same else s.at[g], d.at[f], ssem, rsem, me, g)

    def place_at(k):
        off = ((k + 1) // 2) * (2 * lax.rem(k, 2) - 1)
        return lax.rem(place + off + 8, 8)

    def ring_at(j):
        return lax.rem(ring + (2, 1, 3, 0)[j], RINGS)

    lane = lambda r, n=128: iota((r, n), 1)
    three = pl.ds(0, FEATS - 1)

    loads = [
        pltpu.make_async_copy(a, b, s_load.at[k])
        for k, (a, b) in enumerate((
            (rows_in, send_rows), (count_in, send_count), (feat_in, feat_t), (w1s_in, w1s), (w1n_in, w1n),
            (tile_src_in, tile_src), (w2s_in, w2s_t), (w2n_in, w2n_t), (labels_in, labels), (tiles_in, tiles),
        ))
    ]
    for load in loads:
        load.start()

    bar = pltpu.get_barrier_semaphore()

    def hello(i, c):
        pl.semaphore_signal(bar, inc=1, device_id=(lax.rem(me + i, NODES), f), device_id_type=MESH)
        return c

    for lo, hi in ((25, 40), (1, 25), (40, NODES)):
        lax.fori_loop(lo, hi, hello, 0)
    for i in range(1, FEATS):
        pl.semaphore_signal(bar, inc=1, device_id=(me, lax.rem(f + i, FEATS)), device_id_type=MESH)

    for load in loads[0:3]:
        load.wait()

    x0 = jnp.transpose(jnp.concatenate([feat_t[...].astype(F32), jnp.zeros((96, ROWS), F32)], axis=0))
    for q in range(4):
        shifted = lane_roll(x0, 32 * q)
        xcat[q] = shifted.astype(BF)
        part = shifted[128 * q:128 * q + 128]
        xpack = part if q == 0 else xpack + part
    xsend[...] = xpack.astype(BF)

    wide[0, 0:64, 0:64] = send_rows[...].astype(F32)
    turned = jnp.transpose(wide[0, 0:128, 0:128]).astype(I32)[0:64]
    counts = jnp.concatenate([send_count[...], jnp.zeros((1, 64), I32)], axis=1)
    slot_col[...] = jnp.where(iota((64, 128), 0) < counts, turned, -1)

    def build_hot(d, c):
        col = jnp.sum(jnp.where(lane(SLOTS) == d, slot_col[...], 0), axis=1, keepdims=True)
        hot[d] = jnp.where(col == lane(SLOTS, ROWS), 1.0, 0.0).astype(BF)
        return c

    lax.fori_loop(0, NODES, build_hot, 0, unroll=8)

    def pack1(m, c):
        d0 = pl.multiple_of(m * 32, 32)
        acc = jnp.zeros((512, 128), F32)
        for q in range(4):
            acc = acc + dot(hot[pl.ds(d0, 32), 16 * q:16 * q + 16, :].reshape(512, ROWS), xcat[q])
        out1[pl.ds(d0, 32)] = acc.astype(BF).reshape(32, 16, 128)
        return c

    lax.fori_loop(0, 2, pack1, 0)
    recv1[me] = out1[me]
    xrecv[f] = xsend[...]
    for load in loads[3:9]:
        load.wait()
    pl.semaphore_wait(bar, NODES - 1 + FEATS - 1)

    for j in range(RINGS):
        rr = ring_at(j)

        def send1(k, c):
            k = (16 if j < 3 else 15) - 1 - k + (0 if j < 3 else 1)
            p = rr * 16 + place_at(k // 2) * 2 + lax.rem(core + k, 2)
            send(out1.at[p], recv1.at[me], s_e1, r_e1.at[ring], p, f)
            return c

        lax.fori_loop(0, 16 if j < 3 else 15, send1, 0)
    for i in (2, 1, 3):
        g = lax.rem(f + i, FEATS)
        cols = pl.ds(pl.multiple_of(g * 256, 256), 256)
        send(xsend, xrecv.at[f], s_x, r_x, me, g)
        send(w1s.at[:, cols], w1s_full.at[f], s_w.at[0], r_w.at[0], me, g)
        send(w1n.at[:, cols], w1n_full.at[f], s_w.at[1], r_w.at[1], me, g)

    own_cols = pl.ds(pl.multiple_of(f * 256, 256), 256)
    w1s_full[f] = w1s[:, own_cols]
    w1n_full[f] = w1n[:, own_cols]
    for b in range(4):
        src[b] = xcat[0, 128 * b:128 * b + 128, :]

    for part, ref in enumerate((w2s_t, w2n_t)):
        wide[0, 0:CLASSES, 0:256] = ref[...].astype(F32)
        wide[1] = jnp.zeros((256, 256), F32)
        for g in range(4):
            wide[1, 64 * g:64 * g + CLS, :] = wide[0, CLS * g:CLS * g + CLS, 0:256]
        w2p_t[256 * part:256 * part + 256, :] = wide[1].astype(BF)

    srow = jnp.full((128, 128), 1 << 20, I32)
    for t in range(TILES):
        srow = jnp.where(lane(128) == t, tile_src[t // 16, t % 16], srow)
    scol = jnp.transpose(srow)
    sub = iota((128, 128), 0)
    lane128 = lane(128)
    same = (srow == scol) & (lane128 < sub)
    rank = jnp.sum(jnp.where((srow < scol) | same, 1, 0), axis=1, keepdims=True)
    goes = jnp.minimum(jnp.sum(jnp.where(same, 1, 0), axis=1, keepdims=True), 1)
    at = rank == lane128
    order_v[...] = jnp.zeros((8, 128), I32)
    order_v[0:1, :] = jnp.sum(jnp.where(at, sub, 0), axis=0, keepdims=True)
    order_v[1:2, :] = jnp.sum(jnp.where(at, goes, 0), axis=0, keepdims=True)
    upto = jnp.sum(jnp.where(scol <= lane128, 1, 0), axis=0, keepdims=True)
    order_v[2:3, :] = jnp.maximum(upto - 1, 0)
    order_v[3:4, :] = jnp.minimum(jnp.sum(jnp.where(scol == lane128, 1, 0), axis=0, keepdims=True), 1)
    order_copy = pltpu.make_async_copy(order_v, order, s_order)
    order_copy.start()

    def build_hot3(m, c):
        cols = []
        for d in (2 * m, 2 * m + 1):
            cols.append(jnp.sum(jnp.where(lane(SLOTS) == d, slot_col[...], 0), axis=1, keepdims=True))
        none = jnp.full((8, 1), -1, I32)
        at = pl.ds(pl.multiple_of(m * 48, 48), 48)
        for k, rows in enumerate((
            [cols[0][0:24], cols[1][0:24]],
            [cols[0][24:48], cols[1][24:48]],
            [cols[0][48:64], none, cols[1][48:64], none],
        )):
            col = jnp.concatenate(rows, axis=0)
            hot3[k, at, :] = jnp.where(col == lane(48, ROWS), 1.0, 0.0).astype(BF)
        return c

    lax.fori_loop(0, NODES // 2, build_hot3, 0, unroll=4)
    loads[9].wait()

    def turn(t, c):
        tiles_t[t] = jnp.transpose(tiles[t])
        return c

    lax.fori_loop(0, TILES, turn, 0, unroll=4)
    order_copy.wait()

    def row_bytes(buf, j):
        return buf.at[pl.ds(0, 15 if j == 3 else 16)]

    group = lane128 // 32

    def unpack_feats(ref, out):
        for b in range(4):
            acc = jnp.zeros((128, 128), F32)
            for g in range(4):
                acc = jnp.where(group == g, lane_roll(ref[g].astype(F32), 32 * (g - b)), acc)
            out[128 * b:128 * b + 128, :] = acc.astype(BF)

    wait_bytes(xrecv.at[three], r_x)
    wait_bytes(w1s_full.at[three], r_w.at[0])
    unpack_feats(xrecv, xfull)
    slope[...] = dot(xfull[...], w1s_full[...].reshape(128, 256))
    xa_t[0:128, :] = jnp.transpose(xfull[...])

    for j in (3, 1, 2, 0):
        rr = ring_at(j)
        wait_bytes(row_bytes(recv1, j), r_e1.at[rr])

        def unpack1(k, c):
            b = rr * 8 + k
            for p in range(2):
                v = recv1[2 * b + p].astype(F32)
                for q in range(4):
                    src[4 + b, 64 * p + 16 * q:64 * p + 16 * q + 16, :] = lane_roll(v, -32 * q).astype(BF)
            return c

        lax.fori_loop(0, 8, unpack1, 0, unroll=4)

    def tile_product(b):
        lhs = jnp.concatenate([tiles[16 * b + k] for k in range(16)], axis=1)
        rhs = jnp.concatenate([src[tile_src[b, k]] for k in range(16)], axis=0)
        return dot(lhs, rhs)

    packed = jnp.zeros((128, 128), F32)
    for b in range(4):
        packed = packed + lane_roll(jnp.where(group == 0, tile_product(b), 0.0), 32 * b)
    aggp[...] = packed.astype(BF)
    to_feats(aggp, agg_recv, s_agg, r_agg, same=True)
    agg_recv[f] = aggp[...]

    wait_bytes(w1n_full.at[three], r_w.at[1])
    wait_bytes(agg_recv.at[three], r_agg)
    unpack_feats(agg_recv, aggf)

    pre = slope[...] + dot(aggf[...], w1n_full[...].reshape(128, 256))
    th = jnp.tanh(GELU_C * (pre + 0.044715 * (pre * pre * pre)))
    cdf = 0.5 * (1.0 + th)
    slope[...] = cdf + pre * (0.5 * (1.0 - th * th)) * (GELU_C * (1.0 + 3.0 * 0.044715 * (pre * pre)))
    hid[...] = (pre * cdf).astype(BF)

    low256 = lane(256) < 64

    def pack_halves(v, g):
        a, b = v[0:256], v[256:512]
        return jnp.where(low256, a if g % 2 == 0 else lane_roll(a, 64), lane_roll(b, 64) if g % 2 == 0 else b)

    for half in range(2):
        v = dot_nt(hid[...], w2p_t[256 + 128 * half:256 + 128 * half + 128, :])
        for g in (2 * half, 2 * half + 1):
            yv = pack_halves(v, g)
            yown[g] = yv
            ypack[g] = yv.astype(BF)
    to_feats(ypack, yrecv, s_y, r_y)
    for half in range(2):
        v = dot_nt(hid[...], w2p_t[128 * half:128 * half + 128, :])
        for g in (2 * half, 2 * half + 1):
            spack[g] = pack_halves(v, g)
    to_feats(spack, srecv, s_s, r_s)
    yrecv[f] = jnp.zeros((256, 128), BF)
    srecv[f] = spack[f]
    wait_bytes(yrecv.at[three], r_y)
    ys = yown[f]
    for g in range(4):
        ys = ys + yrecv[g].astype(F32)
    yr = lane_roll(ys, 64)
    y_lo = jnp.concatenate([jnp.where(low256, ys, 0.0), jnp.where(low256, yr, 0.0)], axis=0)
    ycat[0] = y_lo.astype(BF)
    ycat[1] = lane_roll(y_lo, CLS).astype(BF)
    ycat[2] = lane_roll(jnp.where(lane(ROWS) < CLS - 1, y_lo, 0.0), 2 * CLS).astype(BF)
    ycat[3] = jnp.broadcast_to(y_lo[:, CLS - 1:CLS], (ROWS, 128)).astype(BF)

    for j in range(RINGS):
        rr = ring_at(j)
        d0 = pl.multiple_of(rr * 16, 16)
        at = pl.ds(pl.multiple_of(rr * RING_ROWS, RING_ROWS), RING_ROWS)
        third = hot3[2, at, :]
        acc = dot(hot3[0, at, :], ycat[0]) + dot(hot3[1, at, :], ycat[1]) + dot(third, ycat[2])
        acc = acc.reshape(16, MSG, 128)
        rest = third_rest(dot(third, ycat[3]).reshape(16, MSG, 128))
        acc = jnp.where((iota((16, MSG, 128), 1) == 16) & (iota((16, MSG, 128), 2) >= 2 * CLS), rest, acc)
        out2[pl.ds(d0, 16)] = acc.astype(BF)

        def send2(k, c):
            k = (16 if j < 3 else 15) - 1 - k + (0 if j < 3 else 1)
            p = rr * 16 + place_at(k // 2) * 2 + lax.rem(core + k, 2)
            send(out2.at[p], recv2.at[me], s_e2, r_e2.at[ring], p, f)
            return c

        lax.fori_loop(0, 16 if j < 3 else 15, send2, 0)

    recv2[me] = out2[me]
    for b in range(4):
        src[b] = ycat[0, 128 * b:128 * b + 128, :]
    xa_t[128:256, :] = jnp.transpose(aggf[...])

    def turn_hot(y, c):
        for h in range(3):
            for k in range(4):
                part = hot3[h, pl.ds(pl.multiple_of(y * RING_ROWS, RING_ROWS), RING_ROWS), 128 * k:128 * k + 128]
                hot_t[y, h, 128 * k:128 * k + 128, :] = jnp.transpose(part)
        return c

    lax.fori_loop(0, RINGS, turn_hot, 0)

    for j in (3, 1, 2, 0):
        rr = ring_at(j)
        wait_bytes(row_bytes(recv2, j), r_e2.at[rr])

        def unpack2(k, c):
            b = rr * 8 + k
            v = recv2[pl.ds(2 * b, 2)].astype(F32)
            both = jnp.concatenate([v, lane_roll(v, -CLS), split_third(lane_roll(v, -2 * CLS))], axis=1)
            src[4 + b] = both.reshape(128, 128).astype(BF)
            return c

        lax.fori_loop(0, 8, unpack2, 0, unroll=4)

    wait_bytes(srecv.at[three], r_s)
    ss = srecv[0] + srecv[1] + srecv[2] + srecv[3]
    pf[0, 0:256, :] = ss
    pf[0, 256:512, :] = lane_roll(ss, 64)

    mine = lane128 < CLS
    for b in range(4):
        r = slice(128 * b, 128 * b + 128)
        lg = jnp.where(mine, pf[0, r, :] + tile_product(b), -1e30)
        top = jnp.max(lg, axis=1, keepdims=True)
        ex = jnp.exp(lg - top)
        tot = jnp.sum(ex, axis=1, keepdims=True)
        lab = jnp.transpose(jnp.broadcast_to(labels[b:b + 1, :].astype(F32), (128, 128))).astype(I32)
        want = mine & ((lab - CLS * f) == lane128)
        hit = jnp.sum(jnp.where(want, lg, 0.0), axis=1, keepdims=True)
        st = jnp.where(lane128 == 0, top, jnp.where(lane128 == 1, tot, jnp.where(lane128 == 2, hit, 0.0)))
        st_t = jnp.transpose(st)
        stat[f, b:b + 1, :] = st_t[0:1]
        stat[f, 4 + b:5 + b, :] = st_t[1:2]
        hits[f, b:b + 1, :] = st_t[2:3]
        pf[1, r, :] = ex
        pf[2, r, :] = jnp.where(want, 1.0, 0.0)
    to_feats(stat.at[f], stat, s_st, r_st, same=True)
    wait_bytes(stat.at[three], r_st)

    tops = [stat[g, 0:4, :] for g in range(4)]
    best = jnp.maximum(jnp.maximum(tops[0], tops[1]), jnp.maximum(tops[2], tops[3]))
    total = jnp.zeros_like(best)
    for g in range(4):
        total = total + stat[g, 4:8, :] * jnp.exp(tops[g] - best)
    factor = jnp.exp(stat[f, 0:4, :] - best) / total
    for b in range(4):
        r = slice(128 * b, 128 * b + 128)
        fac = jnp.transpose(jnp.broadcast_to(factor[b:b + 1, :], (128, 128)))
        dl = ((pf[1, r, :] * fac - pf[2, r, :]) * grad_scale).astype(BF)
        rows = slice(128 * (b % 2), 128 * (b % 2) + 128)
        if b < 2:
            dlp[f, rows, :] = dl
        else:
            dlp[f, rows, :] = (dlp[f, rows, :].astype(F32) + lane_roll(dl.astype(F32), 64)).astype(BF)
        lhs = tiles_t[16 * b:16 * b + 16].reshape(2048, 128)
        ptile[16 * b:16 * b + 16] = dot(lhs, dl).reshape(16, 128, 128)
    to_feats(dlp.at[f], dlp, s_dl, r_dl, same=True)
    to_feats(hits.at[f], hits, s_hit, r_hit, same=True)

    def gather_sum(t, acc):
        acc = acc * order[1, t].astype(F32) + ptile[order[0, t]]
        run[t] = acc
        return acc

    lax.fori_loop(0, TILES, gather_sum, jnp.zeros((128, 128), F32), unroll=4)

    def landed(j):
        return run[order[2, j]] * order[3, j].astype(F32)

    for j in range(RINGS):
        rr = ring_at(j)

        def pack_back(k, c):
            to = rr * 8 + place_at(7 - k)
            blk = landed(4 + to)
            blk = blk.reshape(2, 64, 128)
            third = blk[:, 48:64, :]
            rest = third_rest(jnp.broadcast_to(third[:, :, CLS - 1:CLS], (2, 16, 128)))
            rest = jnp.where(iota((2, 8, 128), 1) == 0, rest, 0.0)
            turned3 = lane_roll(jnp.where(iota((2, 16, 128), 2) < CLS - 1, third, 0.0), 2 * CLS)
            v = blk[:, 0:24, :] + lane_roll(blk[:, 24:48, :], CLS) + jnp.concatenate([turned3, rest], axis=1)
            ret[pl.ds(2 * to, 2)] = v.astype(BF)
            return c

        lax.fori_loop(0, 8, pack_back, 0, unroll=4)

        def send_back(k, c):
            k = (16 if j < 3 else 15) - 1 - k + (0 if j < 3 else 1)
            p = rr * 16 + place_at(k // 2) * 2 + lax.rem(core + k, 2)
            send(ret.at[p], recvb.at[me], s_eb, r_eb.at[ring], p, f)
            return c

        lax.fori_loop(0, 16 if j < 3 else 15, send_back, 0)

    recvb[me] = ret[me]
    for b in range(4):
        pf[3, 128 * b:128 * b + 128, :] = landed(b)

    def join(ref, out):
        for pair in range(2):
            c = slice(128 * pair, 128 * pair + 128)
            a, b = ref[2 * pair].astype(F32), ref[2 * pair + 1].astype(F32)
            out[0:256, c] = jnp.where(low256, a, lane_roll(b, 64)).astype(BF)
            out[256:512, c] = jnp.where(low256, lane_roll(a, 64), b).astype(BF)

    def class_rows(v, d):
        for l in range(2):
            d[l, TALL - 8:TALL, :] = jnp.zeros((8, 128), F32)
            for g in range(4):
                d[l, CLS * g:CLS * g + CLS, :] = v[64 * g:64 * g + CLS, 128 * l:128 * l + 128]

    def rows8(t):
        return pl.ds(pl.multiple_of(t * 8, 8), 8)

    def chip_at(i):
        return lax.rem(ring + (i // 8) + 4, RINGS) * 8 + place_at(lax.rem(i, 8))

    def for_chips(body):
        lax.fori_loop(1, CHIPS, lambda i, c: (body(chip_at(CHIPS - i)), c)[1], 0)

    def reduce_class(d, peer, part, k):
        wait_bytes(peer, r_pair.at[k])
        d[core] = d[core] + peer[...]

        def one(p):
            @pl.when(p < CLS_TILES)
            def _():
                send(d.at[core, rows8(p)], part.at[chip], s_red.at[k], r_red.at[k], 2 * p + core, f)

        for_chips(one)

        @pl.when(chip < CLS_TILES)
        def _():
            part[chip] = d[core, rows8(chip), :]

    def spread_class(part, tile, fin, k):
        @pl.when(chip < CLS_TILES)
        def _():
            wait_bytes(part.at[pl.ds(0, CHIPS - 1)], r_red.at[k])
            tile[...] = jnp.sum(part[...], axis=0)
            for_chips(lambda p: send(tile, fin.at[chip], s_fin.at[k], r_fin.at[k], 2 * p + core, f))
            fin[chip] = tile[...]

    def gather_class(fin, half, k):
        @pl.when(chip < CLS_TILES)
        def _():
            wait_bytes(fin.at[pl.ds(0, CLS_TILES - 1)], r_fin.at[k])

        @pl.when(chip >= CLS_TILES)
        def _():
            wait_bytes(fin, r_fin.at[k])

        send(fin, half, s_half.at[k], r_half.at[k], partner, f)

    wait_bytes(hits.at[three], r_hit)
    hit_sum = hits[0, 0:4, :] + hits[1, 0:4, :] + hits[2, 0:4, :] + hits[3, 0:4, :]
    loss = jnp.sum(jnp.log(total) + best - hit_sum)
    wait_bytes(dlp.at[three], r_dl)
    join(dlp, dlcat)
    dlcat_t[...] = jnp.transpose(dlcat[...])
    class_rows(dot(dlcat_t[...], hid[...]), da)
    tail = (iota((8, 128), 0) == 7) & (lane(8) == 0)
    for l in range(2):
        da[l, TALL - 8:TALL, :] = da[l, TALL - 8:TALL, :] + jnp.where(tail, loss, 0.0)
    send(da.at[1 - core], pa, s_pair.at[0], r_pair.at[0], partner, f)

    g_sum = pf[3]
    valid = lane(ROWS) < CLS
    for j in (3, 1, 2, 0):
        rr = ring_at(j)
        wait_bytes(row_bytes(recvb, j), r_eb.at[rr])
        back = recvb[pl.ds(pl.multiple_of(rr * 16, 16), 16)].astype(F32)
        third = split_third(lane_roll(back, -2 * CLS))
        third = jnp.concatenate([third, jnp.zeros((16, 8, 128), F32)], axis=1).reshape(RING_ROWS, 128).astype(BF)
        back = back.reshape(RING_ROWS, 128).astype(BF)
        g_sum = g_sum + jnp.where(valid, dot(hot_t[rr, 0], back) + dot(hot_t[rr, 2], third), 0.0)
        g_sum = g_sum + jnp.where(valid, lane_roll(dot(hot_t[rr, 1], back), -CLS), 0.0)
    gp[f] = (g_sum[0:256] + lane_roll(g_sum[256:512], 64)).astype(BF)
    to_feats(gp.at[f], gp, s_g, r_g, same=True)
    reduce_class(da, pa, ra, 0)
    bh0 = dot(dlcat[...], w2p_t[0:256, :])
    wait_bytes(gp.at[three], r_g)
    join(gp, gcat)

    bh = bh0 + dot(gcat[...], w2p_t[256:512, :])
    g1 = dot(xa_t[...], (bh * slope[...]).astype(BF))
    for l in range(2):
        dc[l] = g1[:, 128 * l:128 * l + 128]
    send(dc.at[1 - core], pc, s_pair.at[2], r_pair.at[2], partner, f)
    class_rows(dot(jnp.transpose(gcat[...]), hid[...]), db)
    send(db.at[1 - core], pb, s_pair.at[1], r_pair.at[1], partner, f)
    wait_bytes(pc, r_pair.at[2])
    dc[core] = dc[core] + pc[...]

    def rows1(p):
        m = p // 4
        return pl.ds(pl.multiple_of((m // 4) * 128 + 32 * lax.rem(f + lax.rem(p, 4), 4) + 8 * lax.rem(m, 4), 8), 8)

    for_chips(lambda p: send(dc.at[core, rows1(p)], rc.at[chip], s_red.at[2], r_red.at[2], 2 * p + core, f))
    rc[chip] = dc[core, rows1(chip), :]
    reduce_class(db, pb, rb, 1)
    spread_class(ra, ta, fin_a, 0)

    wait_bytes(rc.at[pl.ds(0, CHIPS - 1)], r_red.at[2])
    tc[...] = jnp.sum(rc[...], axis=0)
    turn_by = lax.rem(chip, 4)
    came_from = lax.rem(f - turn_by + 4, 4)

    @pl.when(turn_by > 0)
    def _():
        send(tc, trecv, s_t, r_t, me, lax.rem(f + turn_by, 4))

    spread_class(rb, tb, fin_b, 1)

    @pl.when(turn_by > 0)
    def _():
        wait_bytes(trecv, r_t)

    @pl.when(turn_by == 0)
    def _():
        trecv[...] = tc[...]

    for_chips(lambda p: send(trecv, fin_c.at[chip // 4, came_from], s_fin.at[2], r_fin.at[2], 2 * p + core, f))
    fin_c[chip // 4, came_from] = trecv[...]

    gather_class(fin_a, half_a, 0)
    gather_class(fin_b, half_b, 1)

    wait_bytes(rc.at[pl.ds(0, CHIPS - 1)], r_fin.at[2])
    send(fin_c, half_c, s_half.at[2], r_half.at[2], partner, f)

    n63, c31 = pl.ds(0, NODES - 1), pl.ds(0, CHIPS - 1)
    wait_bytes(recv1.at[n63], s_e1)
    wait_bytes(xrecv.at[three], s_x)
    wait_bytes(w1s_full.at[three], s_w.at[0])
    wait_bytes(w1n_full.at[three], s_w.at[1])
    wait_bytes(agg_recv.at[three], s_agg)
    wait_bytes(yrecv.at[three], s_y)
    wait_bytes(srecv.at[three], s_s)
    wait_bytes(recv2.at[n63], s_e2)
    wait_bytes(stat.at[three], s_st)
    wait_bytes(dlp.at[three], s_dl)
    wait_bytes(hits.at[three], s_hit)
    wait_bytes(recvb.at[n63], s_eb)
    wait_bytes(gp.at[three], s_g)
    wait_bytes(pa, s_pair.at[0])
    wait_bytes(pb, s_pair.at[1])
    wait_bytes(pc, s_pair.at[2])
    wait_bytes(rc.at[c31], s_red.at[2])
    for k, part in ((0, ra), (1, rb)):
        @pl.when(chip < CLS_TILES)
        def _():
            wait_bytes(part.at[pl.ds(0, CLS_TILES - 1)], s_red.at[k])
            wait_bytes(part.at[c31], s_fin.at[k])

        @pl.when(chip >= CLS_TILES)
        def _():
            wait_bytes(part.at[pl.ds(0, CLS_TILES)], s_red.at[k])

    wait_bytes(rc.at[c31], s_fin.at[2])

    @pl.when(turn_by > 0)
    def _():
        wait_bytes(trecv, s_t)

    for k, ref in enumerate((half_a, half_b, half_c)):
        wait_bytes(ref, s_half.at[k])
        wait_bytes(ref, r_half.at[k])


def result_kernel(scale, fin_a, half_a, fin_b, half_b, fin_c, half_c, loss_ref, gs1_ref, gn1_ref, gs2_ref, gn2_ref):
    core = lax.rem(lax.axis_index("node"), 2)
    first = core == 0
    loss_ref[...] = fin_a[CLS_TILES - 1, 7:8, 0:1] * scale
    for l in range(2):
        c = slice(128 * l, 128 * l + 128)
        mine = first if l == 0 else jnp.logical_not(first)
        for fin, half, ref in ((fin_a, half_a, gs2_ref), (fin_b, half_b, gn2_ref)):
            ref[:, c] = jnp.where(mine, fin[...], half[...]).reshape(TALL, 128)[0:CLASSES]
        v = jnp.where(mine, fin_c[...], half_c[...])
        for g in range(4):
            cols = slice(256 * g + 128 * l, 256 * g + 128 * l + 128)
            gs1_ref[:, cols] = v[0:4, g].reshape(32, 128)
            gn1_ref[:, cols] = v[4:8, g].reshape(32, 128)


def shards(features, send_rows, send_count, tile_src, tile_val, labels, w_self1, w_neigh1, w_self2, w_neigh2):
    vm = lambda *shape, dt=F32: pltpu.VMEM(shape, dt)
    dma = pltpu.SemaphoreType.DMA
    whole = pl.BlockSpec(memory_space=pltpu.VMEM)
    half_class = jax.ShapeDtypeStruct((CLS_TILES, 8, 128), F32)
    half_first = jax.ShapeDtypeStruct((8, 4, 8, 128), F32)
    parts = pl.pallas_call(
        functools.partial(step_kernel, 1.0 / math.sqrt(ROWS * NODES)),
        out_shape=(half_class,) * 4 + (half_first,) * 2,
        in_specs=[pl.BlockSpec(memory_space=pltpu.HBM)] * 10,
        out_specs=(whole,) * 6,
        scratch_shapes=[
            pltpu.SMEM((4, 16), I32), vm(32, 512, dt=BF), vm(64, 64, dt=I32), vm(1, 64, dt=I32), vm(4, 128, dt=I32),
            vm(32, 1024, dt=BF), vm(32, 1024, dt=BF), vm(CLASSES, 256, dt=BF), vm(CLASSES, 256, dt=BF),
            vm(64, 128, 128, dt=BF), vm(4, 512, 128, dt=BF), vm(128, 128, dt=BF), vm(64, 128, dt=I32), vm(2, 256, 256),
            vm(512, 256, dt=BF), vm(8, 128, dt=I32), pltpu.SMEM((8, 128), I32),
            vm(64, 64, 512, dt=BF), vm(3, 1536, 512, dt=BF), vm(4, 3, 512, 384, dt=BF), vm(64, 128, 128, dt=BF), vm(36, 128, 128, dt=BF),
            vm(64, 128, 128), vm(64, 128, 128),
            vm(64, 16, 128, dt=BF), vm(64, 16, 128, dt=BF), vm(4, 128, 128, dt=BF),
            vm(4, 32, 256, dt=BF), vm(4, 32, 256, dt=BF), vm(128, 128, dt=BF), vm(4, 128, 128, dt=BF),
            vm(512, 128, dt=BF), vm(512, 128, dt=BF),
            vm(512, 256), vm(512, 256, dt=BF), vm(256, 512, dt=BF), vm(4, 512, 128),
            vm(4, 512, 128, dt=BF), vm(4, 256, 128, dt=BF), vm(4, 256, 128), vm(4, 256, 128, dt=BF),
            vm(4, 256, 128), vm(4, 256, 128),
            vm(64, MSG, 128, dt=BF), vm(64, MSG, 128, dt=BF), vm(4, 8, 128), vm(4, 8, 128), vm(4, 256, 128, dt=BF),
            vm(64, MSG, 128, dt=BF), vm(64, MSG, 128, dt=BF), vm(4, 256, 128, dt=BF),
            vm(512, 256, dt=BF), vm(256, 512, dt=BF), vm(512, 256, dt=BF),
            vm(2, TALL, 128), vm(TALL, 128), vm(2, TALL, 128), vm(TALL, 128), vm(2, 256, 128), vm(256, 128),
            vm(32, 8, 128), vm(32, 8, 128), vm(32, 8, 128), vm(8, 128), vm(8, 128), vm(8, 128), vm(8, 128),
            dma((10,)), dma, dma, dma, dma((2,)), dma((2,)), dma, dma((4,)), dma, dma, dma, dma, dma, dma, dma, dma((4,)),
            dma, dma, dma, dma, dma, dma((4,)), dma, dma, dma((3,)), dma((3,)), dma((3,)), dma((3,)),
            dma, dma, dma((3,)), dma((3,)), dma((3,)), dma((3,)), dma, dma,
        ],
        compiler_params=pltpu.CompilerParams(
            collective_id=0, has_side_effects=True, vmem_limit_bytes=44 * 1024 * 1024
        ),
    )(*[
        pltpu.with_memory_space_constraint(a, pltpu.HBM)
        for a in (
            tile_src, features.T, send_rows[0], send_count, tile_val.reshape(TILES, 128, 128), labels.reshape(4, 128),
            w_self1, w_neigh1, w_self2.T, w_neigh2.T,
        )
    ])
    loss, gs1, gn1, gs2, gn2 = pl.pallas_call(
        functools.partial(result_kernel, 1.0 / (ROWS * NODES)),
        out_shape=(
            jax.ShapeDtypeStruct((1, 1), F32),
            jax.ShapeDtypeStruct((32, 1024), F32),
            jax.ShapeDtypeStruct((32, 1024), F32),
            jax.ShapeDtypeStruct((CLASSES, 256), F32),
            jax.ShapeDtypeStruct((CLASSES, 256), F32),
        ),
        in_specs=[whole] * 6,
        out_specs=(whole,) * 5,
        compiler_params=pltpu.CompilerParams(vmem_limit_bytes=8 * 1024 * 1024),
    )(*parts)
    return (loss[0, 0], gs1, gn1, gs2.T, gn2.T)


def solution(mesh):
    in_specs = (
        P("node", "feat"),
        P("node", None, None),
        P("node", None),
        P("node", None),
        P("node", None, None, None),
        P("node"),
        P("feat", None),
        P("feat", None),
        P("feat", None),
        P("feat", None),
    )
    out_specs = (P(), P("feat", None), P("feat", None), P("feat", None), P("feat", None))
    return jax.shard_map(shards, mesh=mesh, in_specs=in_specs, out_specs=out_specs, check_vma=False)
```

```python
import functools
import math

import jax
import jax.numpy as jnp
from jax import lax
from jax.experimental import pallas as pl
from jax.experimental.pallas import tpu as pltpu
from jax.sharding import PartitionSpec as P

MESH = pl.DeviceIdType.MESH
F32 = jnp.float32
BF = jnp.bfloat16
I32 = jnp.int32
ROWS = 512
SLOTS = 64
NODES = 64
FEATS = 4
CHIPS = NODES // 2
RINGS = 4
TILES = 64
CLASSES = 172
CLS = 43
TALL = 176
CLS_TILES = TALL // 8
MSG = 24
RING_ROWS = 16 * MSG
GELU_C = math.sqrt(2.0 / math.pi)


def lane_roll(value, shift):
    shift = shift % value.shape[-1]
    return pltpu.roll(value, shift, value.ndim - 1) if shift else value


def dot(a, b):
    return jnp.dot(a, b, preferred_element_type=F32)


def dot_nt(a, b):
    return lax.dot_general(a, b, (((1,), (1,)), ((), ())), preferred_element_type=F32)


def iota(shape, axis):
    return lax.broadcasted_iota(I32, shape, axis)


def split_third(w):
    n = w.shape[0]
    at = iota((n, 16, 128), 2)
    last = jnp.sum(jnp.where(at == iota((n, 16, 128), 1), w[:, 16:17, :], 0.0), axis=2, keepdims=True)
    return jnp.where(at == CLS - 1, last, w[:, 0:16, :])


def third_rest(col):
    shape = col.shape
    pick = (iota(shape, 2) == iota(shape, 1) + 2 * CLS) & (iota(shape, 1) < 16)
    return jnp.sum(jnp.where(pick, col, 0.0), axis=1, keepdims=True)


def pack_slots(blk):
    n = blk.shape[0]
    third = blk[:, 48:64, :]
    rest = third_rest(jnp.broadcast_to(third[:, :, CLS - 1:CLS], (n, 16, 128)))
    rest = jnp.where(iota((n, 8, 128), 1) == 0, rest, 0.0)
    turned = lane_roll(jnp.where(iota((n, 16, 128), 2) < CLS - 1, third, 0.0), 2 * CLS)
    return blk[:, 0:24, :] + lane_roll(blk[:, 24:48, :], CLS) + jnp.concatenate([turned, rest], axis=1)


def unpack_slots(v):
    return jnp.concatenate([v, lane_roll(v, -CLS), split_third(lane_roll(v, -2 * CLS))], axis=1)


def step_kernel(
    grad_scale,
    tile_src_in, feat_in, rows_in, count_in, tiles_in, labels_in, w1s_in, w1n_in, w2s_in, w2n_in,
    fin_a, half_a, fin_b, half_b, fin_c, half_c,
    tile_src, feat_t, send_rows, send_count, labels, w1s, w1n, w2s_t, w2n_t, tiles, xcat, xsend, slot_col, wide, w2p_t, order_v, order,
    hot, hot3, hot_t, tiles_t, src, run, ptile,
    out1, recv1, xrecv, w1s_full, w1n_full, aggp, agg_recv, xfull, aggf,
    slope, hid, xa_t, pf, ycat, ypack, yown, yrecv, spack, srecv,
    out2, recv2, stat, hits, dlp, ret, recvb, gp, dlcat, dlcat_t, gcat,
    da, pa, db, pb, dc, pc, ra, rb, rc, ta, tb, tc, trecv,
    s_load, s_order, s_x, r_x, s_w, r_w, s_e1, r_e1, s_agg, r_agg, s_y, r_y, s_s, r_s, s_e2, r_e2,
    s_st, r_st, s_dl, r_dl, s_eb, r_eb, s_g, r_g, s_pair, r_pair, s_red, r_red,
    s_t, r_t, s_fin, r_fin, s_half, r_half, s_hit, r_hit, r_fin_c,
):
    me = lax.axis_index("node")
    f = lax.axis_index("feat")
    chip, core = me // 2, lax.rem(me, 2)
    ring, place = me // 16, lax.rem(me // 2, 8)
    partner = me + 1 - 2 * core

    def wait_bytes(ref, sem):
        pltpu.make_async_copy(ref, ref, sem).wait()

    def send(s, d, ssem, rsem, node, feat):
        pltpu.make_async_remote_copy(
            src_ref=s, dst_ref=d, send_sem=ssem, recv_sem=rsem,
            device_id=(node, feat), device_id_type=MESH,
        ).start()

    def to_feats(s, d, ssem, rsem, same=False):
        for i in (2, 1, 3):
            g = lax.rem(f + i, FEATS)
            send(s if same else s.at[g], d.at[f], ssem, rsem, me, g)

    def place_at(k):
        off = ((k + 1) // 2) * (2 * lax.rem(k, 2) - 1)
        return lax.rem(place + off + 8, 8)

    def ring_at(j):
        return lax.rem(ring + (2, 1, 3, 0)[j], RINGS)

    lane = lambda r, n=128: iota((r, n), 1)
    three = pl.ds(0, FEATS - 1)

    loads = [
        pltpu.make_async_copy(a, b, s_load.at[k])
        for k, (a, b) in enumerate((
            (rows_in, send_rows), (count_in, send_count), (feat_in, feat_t), (w1s_in, w1s), (w1n_in, w1n),
            (tile_src_in, tile_src), (w2s_in, w2s_t), (w2n_in, w2n_t), (labels_in, labels), (tiles_in, tiles),
        ))
    ]
    for load in loads:
        load.start()

    bar = pltpu.get_barrier_semaphore()

    def hello(i, c):
        pl.semaphore_signal(bar, inc=1, device_id=(lax.rem(me + i, NODES), f), device_id_type=MESH)
        return c

    for lo, hi in ((25, 40), (1, 25), (40, NODES)):
        lax.fori_loop(lo, hi, hello, 0)
    for i in range(1, FEATS):
        pl.semaphore_signal(bar, inc=1, device_id=(me, lax.rem(f + i, FEATS)), device_id_type=MESH)

    for load in loads[0:3]:
        load.wait()

    x0 = jnp.transpose(jnp.concatenate([feat_t[...].astype(F32), jnp.zeros((96, ROWS), F32)], axis=0))
    for q in range(4):
        shifted = lane_roll(x0, 32 * q)
        xcat[q] = shifted.astype(BF)
        part = shifted[128 * q:128 * q + 128]
        xpack = part if q == 0 else xpack + part
    xsend[...] = xpack.astype(BF)

    wide[0, 0:64, 0:64] = send_rows[...].astype(F32)
    turned = jnp.transpose(wide[0, 0:128, 0:128]).astype(I32)[0:64]
    counts = jnp.concatenate([send_count[...], jnp.zeros((1, 64), I32)], axis=1)
    slot_col[...] = jnp.where(iota((64, 128), 0) < counts, turned, -1)

    def build_hot(d, c):
        col = jnp.sum(jnp.where(lane(SLOTS) == d, slot_col[...], 0), axis=1, keepdims=True)
        hot[d] = jnp.where(col == lane(SLOTS, ROWS), 1.0, 0.0).astype(BF)
        return c

    lax.fori_loop(0, NODES, build_hot, 0, unroll=8)

    def pack1(m, c):
        d0 = pl.multiple_of(m * 32, 32)
        acc = jnp.zeros((512, 128), F32)
        for q in range(4):
            acc = acc + dot(hot[pl.ds(d0, 32), 16 * q:16 * q + 16, :].reshape(512, ROWS), xcat[q])
        out1[pl.ds(d0, 32)] = acc.astype(BF).reshape(32, 16, 128)
        return c

    lax.fori_loop(0, 2, pack1, 0)
    recv1[me] = out1[me]
    xrecv[f] = xsend[...]
    for load in loads[3:9]:
        load.wait()
    pl.semaphore_wait(bar, NODES - 1 + FEATS - 1)

    for j in range(RINGS):
        rr = ring_at(j)

        def send1(k, c):
            k = (16 if j < 3 else 15) - 1 - k + (0 if j < 3 else 1)
            p = rr * 16 + place_at(k // 2) * 2 + lax.rem(core + k, 2)
            send(out1.at[p], recv1.at[me], s_e1, r_e1.at[ring], p, f)
            return c

        lax.fori_loop(0, 16 if j < 3 else 15, send1, 0)
    for i in (2, 1, 3):
        g = lax.rem(f + i, FEATS)
        cols = pl.ds(pl.multiple_of(g * 256, 256), 256)
        send(xsend, xrecv.at[f], s_x, r_x, me, g)
        send(w1s.at[:, cols], w1s_full.at[f], s_w.at[0], r_w.at[0], me, g)
        send(w1n.at[:, cols], w1n_full.at[f], s_w.at[1], r_w.at[1], me, g)

    own_cols = pl.ds(pl.multiple_of(f * 256, 256), 256)
    w1s_full[f] = w1s[:, own_cols]
    w1n_full[f] = w1n[:, own_cols]
    for b in range(4):
        src[b] = xcat[0, 128 * b:128 * b + 128, :]

    for part, ref in enumerate((w2s_t, w2n_t)):
        wide[0, 0:CLASSES, 0:256] = ref[...].astype(F32)
        wide[1] = jnp.zeros((256, 256), F32)
        for g in range(4):
            wide[1, 64 * g:64 * g + CLS, :] = wide[0, CLS * g:CLS * g + CLS, 0:256]
        w2p_t[256 * part:256 * part + 256, :] = wide[1].astype(BF)

    srow = jnp.full((128, 128), 1 << 20, I32)
    for t in range(TILES):
        srow = jnp.where(lane(128) == t, tile_src[t // 16, t % 16], srow)
    scol = jnp.transpose(srow)
    sub = iota((128, 128), 0)
    lane128 = lane(128)
    same = (srow == scol) & (lane128 < sub)
    rank = jnp.sum(jnp.where((srow < scol) | same, 1, 0), axis=1, keepdims=True)
    goes = jnp.minimum(jnp.sum(jnp.where(same, 1, 0), axis=1, keepdims=True), 1)
    at = rank == lane128
    order_v[...] = jnp.zeros((8, 128), I32)
    order_v[0:1, :] = jnp.sum(jnp.where(at, sub, 0), axis=0, keepdims=True)
    order_v[1:2, :] = jnp.sum(jnp.where(at, goes, 0), axis=0, keepdims=True)
    upto = jnp.sum(jnp.where(scol <= lane128, 1, 0), axis=0, keepdims=True)
    order_v[2:3, :] = jnp.maximum(upto - 1, 0)
    order_v[3:4, :] = jnp.minimum(jnp.sum(jnp.where(scol == lane128, 1, 0), axis=0, keepdims=True), 1)
    order_copy = pltpu.make_async_copy(order_v, order, s_order)
    order_copy.start()

    def build_hot3(m, c):
        cols = []
        for d in (2 * m, 2 * m + 1):
            cols.append(jnp.sum(jnp.where(lane(SLOTS) == d, slot_col[...], 0), axis=1, keepdims=True))
        none = jnp.full((8, 1), -1, I32)
        at = pl.ds(pl.multiple_of(m * 48, 48), 48)
        for k, rows in enumerate((
            [cols[0][0:24], cols[1][0:24]],
            [cols[0][24:48], cols[1][24:48]],
            [cols[0][48:64], none, cols[1][48:64], none],
        )):
            col = jnp.concatenate(rows, axis=0)
            hot3[k, at, :] = jnp.where(col == lane(48, ROWS), 1.0, 0.0).astype(BF)
        return c

    lax.fori_loop(0, NODES // 2, build_hot3, 0, unroll=4)
    loads[9].wait()

    def turn(t, c):
        tiles_t[t] = jnp.transpose(tiles[t])
        return c

    lax.fori_loop(0, TILES, turn, 0, unroll=4)
    order_copy.wait()

    def row_bytes(buf, j):
        return buf.at[pl.ds(0, 15 if j == 3 else 16)]

    group = lane128 // 32

    def unpack_feats(ref, out):
        for b in range(4):
            acc = jnp.zeros((128, 128), F32)
            for g in range(4):
                acc = jnp.where(group == g, lane_roll(ref[g].astype(F32), 32 * (g - b)), acc)
            out[128 * b:128 * b + 128, :] = acc.astype(BF)

    wait_bytes(xrecv.at[three], r_x)
    wait_bytes(w1s_full.at[three], r_w.at[0])
    unpack_feats(xrecv, xfull)
    slope[...] = dot(xfull[...], w1s_full[...].reshape(128, 256))
    xa_t[0:128, :] = jnp.transpose(xfull[...])

    for j in (3, 1, 2, 0):
        rr = ring_at(j)
        wait_bytes(row_bytes(recv1, j), r_e1.at[rr])

        def unpack1(k, c):
            b = rr * 8 + k
            for p in range(2):
                v = recv1[2 * b + p].astype(F32)
                for q in range(4):
                    src[4 + b, 64 * p + 16 * q:64 * p + 16 * q + 16, :] = lane_roll(v, -32 * q).astype(BF)
            return c

        lax.fori_loop(0, 8, unpack1, 0, unroll=4)

    def tile_product(b):
        lhs = jnp.concatenate([tiles[16 * b + k] for k in range(16)], axis=1)
        rhs = jnp.concatenate([src[tile_src[b, k]] for k in range(16)], axis=0)
        return dot(lhs, rhs)

    packed = jnp.zeros((128, 128), F32)
    for b in range(4):
        packed = packed + lane_roll(jnp.where(group == 0, tile_product(b), 0.0), 32 * b)
    aggp[...] = packed.astype(BF)
    to_feats(aggp, agg_recv, s_agg, r_agg, same=True)
    agg_recv[f] = aggp[...]

    wait_bytes(w1n_full.at[three], r_w.at[1])
    wait_bytes(agg_recv.at[three], r_agg)
    unpack_feats(agg_recv, aggf)

    pre = slope[...] + dot(aggf[...], w1n_full[...].reshape(128, 256))
    th = jnp.tanh(GELU_C * (pre + 0.044715 * (pre * pre * pre)))
    cdf = 0.5 * (1.0 + th)
    slope[...] = cdf + pre * (0.5 * (1.0 - th * th)) * (GELU_C * (1.0 + 3.0 * 0.044715 * (pre * pre)))
    hid[...] = (pre * cdf).astype(BF)

    low256 = lane(256) < 64

    def pack_halves(v, g):
        a, b = v[0:256], v[256:512]
        return jnp.where(low256, a if g % 2 == 0 else lane_roll(a, 64), lane_roll(b, 64) if g % 2 == 0 else b)

    for half in range(2):
        v = dot_nt(hid[...], w2p_t[256 + 128 * half:256 + 128 * half + 128, :])
        for g in (2 * half, 2 * half + 1):
            yv = jnp.where(lane(ROWS) < 64, v if g % 2 == 0 else lane_roll(v, 64), 0.0)
            yv = pack_slots(yv.reshape(8, 64, 128)).reshape(192, 128)
            yown[g] = yv
            ypack[g] = yv.astype(BF)
    to_feats(ypack, yrecv, s_y, r_y)
    for half in range(2):
        v = dot_nt(hid[...], w2p_t[128 * half:128 * half + 128, :])
        for g in (2 * half, 2 * half + 1):
            spack[g] = pack_halves(v, g)
    to_feats(spack, srecv, s_s, r_s)
    yrecv[f] = jnp.zeros((192, 128), BF)
    srecv[f] = spack[f]
    wait_bytes(yrecv.at[three], r_y)
    ys = yown[f]
    for g in range(4):
        ys = ys + yrecv[g].astype(F32)
    y_lo = jnp.where(lane(ROWS) < CLS, unpack_slots(ys.reshape(8, MSG, 128)).reshape(ROWS, 128), 0.0)
    ycat[0] = y_lo.astype(BF)
    ycat[1] = lane_roll(y_lo, CLS).astype(BF)
    ycat[2] = lane_roll(jnp.where(lane(ROWS) < CLS - 1, y_lo, 0.0), 2 * CLS).astype(BF)
    ycat[3] = jnp.broadcast_to(y_lo[:, CLS - 1:CLS], (ROWS, 128)).astype(BF)

    for j in range(RINGS):
        rr = ring_at(j)
        d0 = pl.multiple_of(rr * 16, 16)
        at = pl.ds(pl.multiple_of(rr * RING_ROWS, RING_ROWS), RING_ROWS)
        third = hot3[2, at, :]
        acc = dot(hot3[0, at, :], ycat[0]) + dot(hot3[1, at, :], ycat[1]) + dot(third, ycat[2])
        acc = acc.reshape(16, MSG, 128)
        rest = third_rest(dot(third, ycat[3]).reshape(16, MSG, 128))
        acc = jnp.where((iota((16, MSG, 128), 1) == 16) & (iota((16, MSG, 128), 2) >= 2 * CLS), rest, acc)
        out2[pl.ds(d0, 16)] = acc.astype(BF)

        def send2(k, c):
            k = (16 if j < 3 else 15) - 1 - k + (0 if j < 3 else 1)
            p = rr * 16 + place_at(k // 2) * 2 + lax.rem(core + k, 2)
            send(out2.at[p], recv2.at[me], s_e2, r_e2.at[ring], p, f)
            return c

        lax.fori_loop(0, 16 if j < 3 else 15, send2, 0)

    recv2[me] = out2[me]
    for b in range(4):
        src[b] = ycat[0, 128 * b:128 * b + 128, :]
    xa_t[128:256, :] = jnp.transpose(aggf[...])

    def turn_hot(y, c):
        for h in range(3):
            for k in range(4):
                part = hot3[h, pl.ds(pl.multiple_of(y * RING_ROWS, RING_ROWS), RING_ROWS), 128 * k:128 * k + 128]
                hot_t[y, h, 128 * k:128 * k + 128, :] = jnp.transpose(part)
        return c

    lax.fori_loop(0, RINGS, turn_hot, 0)

    for j in (3, 1, 2, 0):
        rr = ring_at(j)
        wait_bytes(row_bytes(recv2, j), r_e2.at[rr])

        def unpack2(k, c):
            b = rr * 8 + k
            v = recv2[pl.ds(2 * b, 2)].astype(F32)
            src[4 + b] = unpack_slots(v).reshape(128, 128).astype(BF)
            return c

        lax.fori_loop(0, 8, unpack2, 0, unroll=4)

    wait_bytes(srecv.at[three], r_s)
    ss = srecv[0] + srecv[1] + srecv[2] + srecv[3]
    pf[0, 0:256, :] = ss
    pf[0, 256:512, :] = lane_roll(ss, 64)

    mine = lane128 < CLS
    for b in range(4):
        r = slice(128 * b, 128 * b + 128)
        lg = jnp.where(mine, pf[0, r, :] + tile_product(b), -1e30)
        top = jnp.max(lg, axis=1, keepdims=True)
        ex = jnp.exp(lg - top)
        tot = jnp.sum(ex, axis=1, keepdims=True)
        lab = jnp.transpose(jnp.broadcast_to(labels[b:b + 1, :].astype(F32), (128, 128))).astype(I32)
        want = mine & ((lab - CLS * f) == lane128)
        hit = jnp.sum(jnp.where(want, lg, 0.0), axis=1, keepdims=True)
        st = jnp.where(lane128 == 0, top, jnp.where(lane128 == 1, tot, jnp.where(lane128 == 2, hit, 0.0)))
        st_t = jnp.transpose(st)
        stat[f, b:b + 1, :] = st_t[0:1]
        stat[f, 4 + b:5 + b, :] = st_t[1:2]
        hits[f, b:b + 1, :] = st_t[2:3]
        pf[1, r, :] = ex
        pf[2, r, :] = jnp.where(want, 1.0, 0.0)
    to_feats(stat.at[f], stat, s_st, r_st, same=True)
    wait_bytes(stat.at[three], r_st)

    tops = [stat[g, 0:4, :] for g in range(4)]
    best = jnp.maximum(jnp.maximum(tops[0], tops[1]), jnp.maximum(tops[2], tops[3]))
    total = jnp.zeros_like(best)
    for g in range(4):
        total = total + stat[g, 4:8, :] * jnp.exp(tops[g] - best)
    factor = jnp.exp(stat[f, 0:4, :] - best) / total
    for b in range(4):
        r = slice(128 * b, 128 * b + 128)
        fac = jnp.transpose(jnp.broadcast_to(factor[b:b + 1, :], (128, 128)))
        dl = ((pf[1, r, :] * fac - pf[2, r, :]) * grad_scale).astype(BF)
        rows = slice(128 * (b % 2), 128 * (b % 2) + 128)
        if b < 2:
            dlp[f, rows, :] = dl
        else:
            dlp[f, rows, :] = (dlp[f, rows, :].astype(F32) + lane_roll(dl.astype(F32), 64)).astype(BF)
        lhs = tiles_t[16 * b:16 * b + 16].reshape(2048, 128)
        ptile[16 * b:16 * b + 16] = dot(lhs, dl).reshape(16, 128, 128)
    to_feats(dlp.at[f], dlp, s_dl, r_dl, same=True)
    to_feats(hits.at[f], hits, s_hit, r_hit, same=True)

    def gather_sum(t, acc):
        acc = acc * order[1, t].astype(F32) + ptile[order[0, t]]
        run[t] = acc
        return acc

    lax.fori_loop(0, TILES, gather_sum, jnp.zeros((128, 128), F32), unroll=4)

    def landed(j):
        return run[order[2, j]] * order[3, j].astype(F32)

    for j in range(RINGS):
        rr = ring_at(j)

        def pack_back(k, c):
            to = rr * 8 + place_at(7 - k)
            blk = landed(4 + to)
            v = pack_slots(blk.reshape(2, 64, 128))
            ret[pl.ds(2 * to, 2)] = v.astype(BF)
            return c

        lax.fori_loop(0, 8, pack_back, 0, unroll=4)

        def send_back(k, c):
            k = (16 if j < 3 else 15) - 1 - k + (0 if j < 3 else 1)
            p = rr * 16 + place_at(k // 2) * 2 + lax.rem(core + k, 2)
            send(ret.at[p], recvb.at[me], s_eb, r_eb.at[ring], p, f)
            return c

        lax.fori_loop(0, 16 if j < 3 else 15, send_back, 0)

    recvb[me] = ret[me]
    for b in range(4):
        pf[3, 128 * b:128 * b + 128, :] = landed(b)

    def join(ref, out):
        for pair in range(2):
            c = slice(128 * pair, 128 * pair + 128)
            a, b = ref[2 * pair].astype(F32), ref[2 * pair + 1].astype(F32)
            out[0:256, c] = jnp.where(low256, a, lane_roll(b, 64)).astype(BF)
            out[256:512, c] = jnp.where(low256, lane_roll(a, 64), b).astype(BF)

    def class_rows(v, d):
        for l in range(2):
            d[l, TALL - 8:TALL, :] = jnp.zeros((8, 128), F32)
            for g in range(4):
                d[l, CLS * g:CLS * g + CLS, :] = v[64 * g:64 * g + CLS, 128 * l:128 * l + 128]

    def rows8(t):
        return pl.ds(pl.multiple_of(t * 8, 8), 8)

    def chip_at(i):
        return lax.rem(ring + (i // 8) + 4, RINGS) * 8 + place_at(lax.rem(i, 8))

    def for_chips(body):
        lax.fori_loop(1, CHIPS, lambda i, c: (body(chip_at(CHIPS - i)), c)[1], 0)

    def reduce_class(d, peer, part, k):
        wait_bytes(peer, r_pair.at[k])
        d[core] = d[core] + peer[...]

        def one(p):
            @pl.when(p < CLS_TILES)
            def _():
                send(d.at[core, rows8(p)], part.at[chip], s_red.at[k], r_red.at[k], 2 * p + core, f)

        for_chips(one)

        @pl.when(chip < CLS_TILES)
        def _():
            part[chip] = d[core, rows8(chip), :]

    def spread_class(part, tile, fin, k):
        @pl.when(chip < CLS_TILES)
        def _():
            wait_bytes(part.at[pl.ds(0, CHIPS - 1)], r_red.at[k])
            tile[...] = jnp.sum(part[...], axis=0)
            for_chips(lambda p: send(tile, fin.at[chip], s_fin.at[k], r_fin.at[k], 2 * p + core, f))
            fin[chip] = tile[...]

    def gather_class(fin, half, k):
        @pl.when(chip < CLS_TILES)
        def _():
            wait_bytes(fin.at[pl.ds(0, CLS_TILES - 1)], r_fin.at[k])

        @pl.when(chip >= CLS_TILES)
        def _():
            wait_bytes(fin, r_fin.at[k])

        send(fin, half, s_half.at[k], r_half.at[k], partner, f)

    wait_bytes(hits.at[three], r_hit)
    hit_sum = hits[0, 0:4, :] + hits[1, 0:4, :] + hits[2, 0:4, :] + hits[3, 0:4, :]
    loss = jnp.sum(jnp.log(total) + best - hit_sum)
    wait_bytes(dlp.at[three], r_dl)
    join(dlp, dlcat)
    dlcat_t[...] = jnp.transpose(dlcat[...])
    class_rows(dot(dlcat_t[...], hid[...]), da)
    tail = (iota((8, 128), 0) == 7) & (lane(8) == 0)
    for l in range(2):
        da[l, TALL - 8:TALL, :] = da[l, TALL - 8:TALL, :] + jnp.where(tail, loss, 0.0)
    send(da.at[1 - core], pa, s_pair.at[0], r_pair.at[0], partner, f)

    g_sum = pf[3]
    valid = lane(ROWS) < CLS
    for j in (3, 1, 2, 0):
        rr = ring_at(j)
        wait_bytes(row_bytes(recvb, j), r_eb.at[rr])
        back = recvb[pl.ds(pl.multiple_of(rr * 16, 16), 16)].astype(F32)
        third = split_third(lane_roll(back, -2 * CLS))
        third = jnp.concatenate([third, jnp.zeros((16, 8, 128), F32)], axis=1).reshape(RING_ROWS, 128).astype(BF)
        back = back.reshape(RING_ROWS, 128).astype(BF)
        g_sum = g_sum + jnp.where(valid, dot(hot_t[rr, 0], back) + dot(hot_t[rr, 2], third), 0.0)
        g_sum = g_sum + jnp.where(valid, lane_roll(dot(hot_t[rr, 1], back), -CLS), 0.0)
    gp[f] = pack_slots(g_sum.reshape(8, 64, 128)).reshape(192, 128).astype(BF)
    to_feats(gp.at[f], gp, s_g, r_g, same=True)
    reduce_class(da, pa, ra, 0)
    bh0 = dot(dlcat[...], w2p_t[0:256, :])
    wait_bytes(gp.at[three], r_g)
    for pair in range(2):
        a, b = (
            jnp.where(valid, unpack_slots(gp[g].astype(F32).reshape(8, MSG, 128)).reshape(ROWS, 128), 0.0)
            for g in (2 * pair, 2 * pair + 1)
        )
        gcat[:, 128 * pair:128 * pair + 128] = (a + lane_roll(b, 64)).astype(BF)

    bh = bh0 + dot(gcat[...], w2p_t[256:512, :])
    g1 = dot(xa_t[...], (bh * slope[...]).astype(BF))
    for l in range(2):
        dc[l] = g1[:, 128 * l:128 * l + 128]
    send(dc.at[1 - core], pc, s_pair.at[2], r_pair.at[2], partner, f)
    class_rows(dot(jnp.transpose(gcat[...]), hid[...]), db)
    send(db.at[1 - core], pb, s_pair.at[1], r_pair.at[1], partner, f)
    wait_bytes(pc, r_pair.at[2])
    dc[core] = dc[core] + pc[...]

    def rows1(p):
        m = p // 4
        return pl.ds(pl.multiple_of((m // 4) * 128 + 32 * lax.rem(f + lax.rem(p, 4), 4) + 8 * lax.rem(m, 4), 8), 8)

    for_chips(lambda p: send(dc.at[core, rows1(p)], rc.at[chip], s_red.at[2], r_red.at[2], 2 * p + core, f))
    rc[chip] = dc[core, rows1(chip), :]
    reduce_class(db, pb, rb, 1)
    spread_class(ra, ta, fin_a, 0)

    wait_bytes(rc.at[pl.ds(0, CHIPS - 1)], r_red.at[2])
    tc[...] = jnp.sum(rc[...], axis=0)
    turn_by = lax.rem(chip, 4)
    came_from = lax.rem(f - turn_by + 4, 4)

    @pl.when(turn_by > 0)
    def _():
        send(tc, trecv, s_t, r_t, me, lax.rem(f + turn_by, 4))

    spread_class(rb, tb, fin_b, 1)

    @pl.when(turn_by > 0)
    def _():
        wait_bytes(trecv, r_t)

    @pl.when(turn_by == 0)
    def _():
        trecv[...] = tc[...]

    for_chips(lambda p: send(trecv, fin_c.at[chip // 4, came_from], s_fin.at[2], r_fin_c.at[ring], 2 * p + core, f))
    fin_c[chip // 4, came_from] = trecv[...]

    gather_class(fin_a, half_a, 0)
    gather_class(fin_b, half_b, 1)

    for j in (3, 1, 2, 0):
        rr = ring_at(j)
        wait_bytes(rc.at[pl.ds(0, 7 if j == 3 else 8)], r_fin_c.at[rr])
        part = pl.ds(2 * rr, 2)
        send(fin_c.at[part], half_c.at[part], s_half.at[2], r_half.at[2], partner, f)

    n63, c31 = pl.ds(0, NODES - 1), pl.ds(0, CHIPS - 1)
    wait_bytes(recv1.at[n63], s_e1)
    wait_bytes(xrecv.at[three], s_x)
    wait_bytes(w1s_full.at[three], s_w.at[0])
    wait_bytes(w1n_full.at[three], s_w.at[1])
    wait_bytes(agg_recv.at[three], s_agg)
    wait_bytes(yrecv.at[three], s_y)
    wait_bytes(srecv.at[three], s_s)
    wait_bytes(recv2.at[n63], s_e2)
    wait_bytes(stat.at[three], s_st)
    wait_bytes(dlp.at[three], s_dl)
    wait_bytes(hits.at[three], s_hit)
    wait_bytes(recvb.at[n63], s_eb)
    wait_bytes(gp.at[three], s_g)
    wait_bytes(pa, s_pair.at[0])
    wait_bytes(pb, s_pair.at[1])
    wait_bytes(pc, s_pair.at[2])
    wait_bytes(rc.at[c31], s_red.at[2])
    for k, part in ((0, ra), (1, rb)):
        @pl.when(chip < CLS_TILES)
        def _():
            wait_bytes(part.at[pl.ds(0, CLS_TILES - 1)], s_red.at[k])
            wait_bytes(part.at[c31], s_fin.at[k])

        @pl.when(chip >= CLS_TILES)
        def _():
            wait_bytes(part.at[pl.ds(0, CLS_TILES)], s_red.at[k])

    wait_bytes(rc.at[c31], s_fin.at[2])

    @pl.when(turn_by > 0)
    def _():
        wait_bytes(trecv, s_t)

    for k, ref in enumerate((half_a, half_b, half_c)):
        wait_bytes(ref, s_half.at[k])
        wait_bytes(ref, r_half.at[k])


def result_kernel(scale, fin_a, half_a, fin_b, half_b, fin_c, half_c, loss_ref, gs1_ref, gn1_ref, gs2_ref, gn2_ref):
    core = lax.rem(lax.axis_index("node"), 2)
    first = core == 0
    loss_ref[...] = fin_a[CLS_TILES - 1, 7:8, 0:1] * scale
    for l in range(2):
        c = slice(128 * l, 128 * l + 128)
        mine = first if l == 0 else jnp.logical_not(first)
        for fin, half, ref in ((fin_a, half_a, gs2_ref), (fin_b, half_b, gn2_ref)):
            ref[:, c] = jnp.where(mine, fin[...], half[...]).reshape(TALL, 128)[0:CLASSES]
        v = jnp.where(mine, fin_c[...], half_c[...])
        for g in range(4):
            cols = slice(256 * g + 128 * l, 256 * g + 128 * l + 128)
            gs1_ref[:, cols] = v[0:4, g].reshape(32, 128)
            gn1_ref[:, cols] = v[4:8, g].reshape(32, 128)


def shards(features, send_rows, send_count, tile_src, tile_val, labels, w_self1, w_neigh1, w_self2, w_neigh2):
    vm = lambda *shape, dt=F32: pltpu.VMEM(shape, dt)
    dma = pltpu.SemaphoreType.DMA
    whole = pl.BlockSpec(memory_space=pltpu.VMEM)
    half_class = jax.ShapeDtypeStruct((CLS_TILES, 8, 128), F32)
    half_first = jax.ShapeDtypeStruct((8, 4, 8, 128), F32)
    parts = pl.pallas_call(
        functools.partial(step_kernel, 1.0 / math.sqrt(ROWS * NODES)),
        out_shape=(half_class,) * 4 + (half_first,) * 2,
        in_specs=[pl.BlockSpec(memory_space=pltpu.HBM)] * 10,
        out_specs=(whole,) * 6,
        scratch_shapes=[
            pltpu.SMEM((4, 16), I32), vm(32, 512, dt=BF), vm(64, 64, dt=I32), vm(1, 64, dt=I32), vm(4, 128, dt=I32),
            vm(32, 1024, dt=BF), vm(32, 1024, dt=BF), vm(CLASSES, 256, dt=BF), vm(CLASSES, 256, dt=BF),
            vm(64, 128, 128, dt=BF), vm(4, 512, 128, dt=BF), vm(128, 128, dt=BF), vm(64, 128, dt=I32), vm(2, 256, 256),
            vm(512, 256, dt=BF), vm(8, 128, dt=I32), pltpu.SMEM((8, 128), I32),
            vm(64, 64, 512, dt=BF), vm(3, 1536, 512, dt=BF), vm(4, 3, 512, 384, dt=BF), vm(64, 128, 128, dt=BF), vm(36, 128, 128, dt=BF),
            vm(64, 128, 128), vm(64, 128, 128),
            vm(64, 16, 128, dt=BF), vm(64, 16, 128, dt=BF), vm(4, 128, 128, dt=BF),
            vm(4, 32, 256, dt=BF), vm(4, 32, 256, dt=BF), vm(128, 128, dt=BF), vm(4, 128, 128, dt=BF),
            vm(512, 128, dt=BF), vm(512, 128, dt=BF),
            vm(512, 256), vm(512, 256, dt=BF), vm(256, 512, dt=BF), vm(4, 512, 128),
            vm(4, 512, 128, dt=BF), vm(4, 192, 128, dt=BF), vm(4, 192, 128), vm(4, 192, 128, dt=BF),
            vm(4, 256, 128), vm(4, 256, 128),
            vm(64, MSG, 128, dt=BF), vm(64, MSG, 128, dt=BF), vm(4, 8, 128), vm(4, 8, 128), vm(4, 256, 128, dt=BF),
            vm(64, MSG, 128, dt=BF), vm(64, MSG, 128, dt=BF), vm(4, 192, 128, dt=BF),
            vm(512, 256, dt=BF), vm(256, 512, dt=BF), vm(512, 256, dt=BF),
            vm(2, TALL, 128), vm(TALL, 128), vm(2, TALL, 128), vm(TALL, 128), vm(2, 256, 128), vm(256, 128),
            vm(32, 8, 128), vm(32, 8, 128), vm(32, 8, 128), vm(8, 128), vm(8, 128), vm(8, 128), vm(8, 128),
            dma((10,)), dma, dma, dma, dma((2,)), dma((2,)), dma, dma((4,)), dma, dma, dma, dma, dma, dma, dma, dma((4,)),
            dma, dma, dma, dma, dma, dma((4,)), dma, dma, dma((3,)), dma((3,)), dma((3,)), dma((3,)),
            dma, dma, dma((3,)), dma((3,)), dma((3,)), dma((3,)), dma, dma, dma((4,)),
        ],
        compiler_params=pltpu.CompilerParams(
            collective_id=0, has_side_effects=True, vmem_limit_bytes=44 * 1024 * 1024
        ),
    )(*[
        pltpu.with_memory_space_constraint(a, pltpu.HBM)
        for a in (
            tile_src, features.T, send_rows[0], send_count, tile_val.reshape(TILES, 128, 128), labels.reshape(4, 128),
            w_self1, w_neigh1, w_self2.T, w_neigh2.T,
        )
    ])
    loss, gs1, gn1, gs2, gn2 = pl.pallas_call(
        functools.partial(result_kernel, 1.0 / (ROWS * NODES)),
        out_shape=(
            jax.ShapeDtypeStruct((1, 1), F32),
            jax.ShapeDtypeStruct((32, 1024), F32),
            jax.ShapeDtypeStruct((32, 1024), F32),
            jax.ShapeDtypeStruct((CLASSES, 256), F32),
            jax.ShapeDtypeStruct((CLASSES, 256), F32),
        ),
        in_specs=[whole] * 6,
        out_specs=(whole,) * 5,
        compiler_params=pltpu.CompilerParams(vmem_limit_bytes=8 * 1024 * 1024),
    )(*parts)
    return (loss[0, 0], gs1, gn1, gs2.T, gn2.T)


def solution(mesh):
    in_specs = (
        P("node", "feat"),
        P("node", None, None),
        P("node", None),
        P("node", None),
        P("node", None, None, None),
        P("node"),
        P("feat", None),
        P("feat", None),
        P("feat", None),
        P("feat", None),
    )
    out_specs = (P(), P("feat", None), P("feat", None), P("feat", None), P("feat", None))
    return jax.shard_map(shards, mesh=mesh, in_specs=in_specs, out_specs=out_specs, check_vma=False)
```

```python
import functools
import math

import jax
import jax.numpy as jnp
from jax import lax
from jax.experimental import pallas as pl
from jax.experimental.pallas import tpu as pltpu
from jax.sharding import PartitionSpec as P

MESH = pl.DeviceIdType.MESH
F32 = jnp.float32
BF = jnp.bfloat16
I32 = jnp.int32
ROWS = 512
SLOTS = 64
NODES = 64
FEATS = 4
CHIPS = NODES // 2
RINGS = 4
TILES = 64
CLASSES = 172
CLS = 43
TALL = 176
CLS_TILES = TALL // 8
MSG = 24
RING_ROWS = 16 * MSG
GELU_C = math.sqrt(2.0 / math.pi)


def lane_roll(value, shift):
    shift = shift % value.shape[-1]
    return pltpu.roll(value, shift, value.ndim - 1) if shift else value


def dot(a, b):
    return jnp.dot(a, b, preferred_element_type=F32)


def dot_nt(a, b):
    return lax.dot_general(a, b, (((1,), (1,)), ((), ())), preferred_element_type=F32)


def iota(shape, axis):
    return lax.broadcasted_iota(I32, shape, axis)


def split_third(w):
    n = w.shape[0]
    at = iota((n, 16, 128), 2)
    last = jnp.sum(jnp.where(at == iota((n, 16, 128), 1), w[:, 16:17, :], 0.0), axis=2, keepdims=True)
    return jnp.where(at == CLS - 1, last, w[:, 0:16, :])


def third_rest(col):
    shape = col.shape
    pick = (iota(shape, 2) == iota(shape, 1) + 2 * CLS) & (iota(shape, 1) < 16)
    return jnp.sum(jnp.where(pick, col, 0.0), axis=1, keepdims=True)


def pack_slots(blk):
    n = blk.shape[0]
    third = blk[:, 48:64, :]
    rest = third_rest(jnp.broadcast_to(third[:, :, CLS - 1:CLS], (n, 16, 128)))
    rest = jnp.where(iota((n, 8, 128), 1) == 0, rest, 0.0)
    turned = lane_roll(jnp.where(iota((n, 16, 128), 2) < CLS - 1, third, 0.0), 2 * CLS)
    return blk[:, 0:24, :] + lane_roll(blk[:, 24:48, :], CLS) + jnp.concatenate([turned, rest], axis=1)


def unpack_slots(v):
    return jnp.concatenate([v, lane_roll(v, -CLS), split_third(lane_roll(v, -2 * CLS))], axis=1)


def step_kernel(
    grad_scale,
    tile_src_in, feat_in, rows_in, count_in, tiles_in, labels_in, w1s_in, w1n_in, w2s_in, w2n_in,
    fin_a, half_a, fin_b, half_b, fin_c, half_c,
    tile_src, feat_t, send_rows, send_count, labels, w1s, w1n, w2s_t, w2n_t, tiles, xcat, xsend, slot_col, wide, w2p_t, order_v, order,
    hot, hot3, hot_t, tiles_t, src, run, ptile,
    out1, recv1, xrecv, w1s_full, w1n_full, aggp, agg_recv, xfull, aggf,
    slope, hid, xa_t, pf, ycat, ypack, yown, yrecv, spack, srecv,
    out2, recv2, stat, hits, dlp, ret, recvb, gp, dlcat, dlcat_t, gcat,
    da, pa, db, pb, dc, pc, ra, rb, rc, ta, tb, tc, trecv,
    s_load, s_order, s_x, r_x, s_w, r_w, s_e1, r_e1, s_agg, r_agg, s_y, r_y, s_s, r_s, s_e2, r_e2,
    s_st, r_st, s_dl, r_dl, s_eb, r_eb, s_g, r_g, s_pair, r_pair, s_red, r_red,
    s_t, r_t, s_fin, r_fin, s_half, r_half, s_hit, r_hit, r_fin_c,
):
    me = lax.axis_index("node")
    f = lax.axis_index("feat")
    chip, core = me // 2, lax.rem(me, 2)
    ring, place = me // 16, lax.rem(me // 2, 8)
    partner = me + 1 - 2 * core

    def wait_bytes(ref, sem):
        pltpu.make_async_copy(ref, ref, sem).wait()

    def send(s, d, ssem, rsem, node, feat):
        pltpu.make_async_remote_copy(
            src_ref=s, dst_ref=d, send_sem=ssem, recv_sem=rsem,
            device_id=(node, feat), device_id_type=MESH,
        ).start()

    def to_feats(s, d, ssem, rsem, same=False):
        for i in (2, 1, 3):
            g = lax.rem(f + i, FEATS)
            send(s if same else s.at[g], d.at[f], ssem, rsem, me, g)

    def place_at(k):
        off = ((k + 1) // 2) * (2 * lax.rem(k, 2) - 1)
        return lax.rem(place + off + 8, 8)

    def ring_at(j):
        return lax.rem(ring + (2, 1, 3, 0)[j], RINGS)

    lane = lambda r, n=128: iota((r, n), 1)
    three = pl.ds(0, FEATS - 1)

    loads = [
        pltpu.make_async_copy(a, b, s_load.at[k])
        for k, (a, b) in enumerate((
            (rows_in, send_rows), (count_in, send_count), (feat_in, feat_t), (w1s_in, w1s), (w1n_in, w1n),
            (tile_src_in, tile_src), (w2s_in, w2s_t), (w2n_in, w2n_t), (labels_in, labels), (tiles_in, tiles),
        ))
    ]
    for load in loads:
        load.start()

    bar = pltpu.get_barrier_semaphore()

    def hello(i, c):
        pl.semaphore_signal(bar, inc=1, device_id=(lax.rem(me + i, NODES), f), device_id_type=MESH)
        return c

    for lo, hi in ((25, 40), (1, 25), (40, NODES)):
        lax.fori_loop(lo, hi, hello, 0)
    for i in range(1, FEATS):
        pl.semaphore_signal(bar, inc=1, device_id=(me, lax.rem(f + i, FEATS)), device_id_type=MESH)

    for load in loads[0:3]:
        load.wait()

    x0 = jnp.transpose(jnp.concatenate([feat_t[...].astype(F32), jnp.zeros((96, ROWS), F32)], axis=0))
    for q in range(4):
        shifted = lane_roll(x0, 32 * q)
        xcat[q] = shifted.astype(BF)
        part = shifted[128 * q:128 * q + 128]
        xpack = part if q == 0 else xpack + part
    xsend[...] = xpack.astype(BF)

    wide[0, 0:64, 0:64] = send_rows[...].astype(F32)
    turned = jnp.transpose(wide[0, 0:128, 0:128]).astype(I32)[0:64]
    counts = jnp.concatenate([send_count[...], jnp.zeros((1, 64), I32)], axis=1)
    slot_col[...] = jnp.where(iota((64, 128), 0) < counts, turned, -1)

    def build_hot(d, c):
        col = jnp.sum(jnp.where(lane(SLOTS) == d, slot_col[...], 0), axis=1, keepdims=True)
        hot[d] = jnp.where(col == lane(SLOTS, ROWS), 1.0, 0.0).astype(BF)
        return c

    lax.fori_loop(0, NODES, build_hot, 0, unroll=8)

    def pack1(m, c):
        d0 = pl.multiple_of(m * 32, 32)
        acc = jnp.zeros((512, 128), F32)
        for q in range(4):
            acc = acc + dot(hot[pl.ds(d0, 32), 16 * q:16 * q + 16, :].reshape(512, ROWS), xcat[q])
        out1[pl.ds(d0, 32)] = acc.astype(BF).reshape(32, 16, 128)
        return c

    lax.fori_loop(0, 2, pack1, 0)
    recv1[me] = out1[me]
    xrecv[f] = xsend[...]
    for load in loads[3:9]:
        load.wait()
    pl.semaphore_wait(bar, NODES - 1 + FEATS - 1)

    for j in range(RINGS):
        rr = ring_at(j)

        def send1(k, c):
            k = (16 if j < 3 else 15) - 1 - k + (0 if j < 3 else 1)
            p = rr * 16 + place_at(k // 2) * 2 + lax.rem(core + k, 2)
            send(out1.at[p], recv1.at[me], s_e1, r_e1.at[ring], p, f)
            return c

        lax.fori_loop(0, 16 if j < 3 else 15, send1, 0)
    for i in (2, 1, 3):
        g = lax.rem(f + i, FEATS)
        cols = pl.ds(pl.multiple_of(g * 256, 256), 256)
        send(xsend, xrecv.at[f], s_x, r_x, me, g)
        send(w1s.at[:, cols], w1s_full.at[f], s_w.at[0], r_w.at[0], me, g)
        send(w1n.at[:, cols], w1n_full.at[f], s_w.at[1], r_w.at[1], me, g)

    own_cols = pl.ds(pl.multiple_of(f * 256, 256), 256)
    w1s_full[f] = w1s[:, own_cols]
    w1n_full[f] = w1n[:, own_cols]
    for b in range(4):
        src[b] = xcat[0, 128 * b:128 * b + 128, :]

    for part, ref in enumerate((w2s_t, w2n_t)):
        wide[0, 0:CLASSES, 0:256] = ref[...].astype(F32)
        wide[1] = jnp.zeros((256, 256), F32)
        for g in range(4):
            wide[1, 64 * g:64 * g + CLS, :] = wide[0, CLS * g:CLS * g + CLS, 0:256]
        w2p_t[256 * part:256 * part + 256, :] = wide[1].astype(BF)

    srow = jnp.full((128, 128), 1 << 20, I32)
    for t in range(TILES):
        srow = jnp.where(lane(128) == t, tile_src[t // 16, t % 16], srow)
    scol = jnp.transpose(srow)
    sub = iota((128, 128), 0)
    lane128 = lane(128)
    same = (srow == scol) & (lane128 < sub)
    rank = jnp.sum(jnp.where((srow < scol) | same, 1, 0), axis=1, keepdims=True)
    goes = jnp.minimum(jnp.sum(jnp.where(same, 1, 0), axis=1, keepdims=True), 1)
    at = rank == lane128
    order_v[...] = jnp.zeros((8, 128), I32)
    order_v[0:1, :] = jnp.sum(jnp.where(at, sub, 0), axis=0, keepdims=True)
    order_v[1:2, :] = jnp.sum(jnp.where(at, goes, 0), axis=0, keepdims=True)
    upto = jnp.sum(jnp.where(scol <= lane128, 1, 0), axis=0, keepdims=True)
    order_v[2:3, :] = jnp.maximum(upto - 1, 0)
    order_v[3:4, :] = jnp.minimum(jnp.sum(jnp.where(scol == lane128, 1, 0), axis=0, keepdims=True), 1)
    order_copy = pltpu.make_async_copy(order_v, order, s_order)
    order_copy.start()

    def build_hot3(m, c):
        cols = []
        for d in (2 * m, 2 * m + 1):
            cols.append(jnp.sum(jnp.where(lane(SLOTS) == d, slot_col[...], 0), axis=1, keepdims=True))
        none = jnp.full((8, 1), -1, I32)
        at = pl.ds(pl.multiple_of(m * 48, 48), 48)
        for k, rows in enumerate((
            [cols[0][0:24], cols[1][0:24]],
            [cols[0][24:48], cols[1][24:48]],
            [cols[0][48:64], none, cols[1][48:64], none],
        )):
            col = jnp.concatenate(rows, axis=0)
            hot3[k, at, :] = jnp.where(col == lane(48, ROWS), 1.0, 0.0).astype(BF)
        return c

    lax.fori_loop(0, NODES // 2, build_hot3, 0, unroll=4)
    loads[9].wait()

    def turn(t, c):
        tiles_t[t] = jnp.transpose(tiles[t])
        return c

    lax.fori_loop(0, TILES, turn, 0, unroll=4)
    order_copy.wait()

    def row_bytes(buf, j):
        return buf.at[pl.ds(0, 15 if j == 3 else 16)]

    group = lane128 // 32

    def unpack_feats(ref, out):
        for b in range(4):
            acc = jnp.zeros((128, 128), F32)
            for g in range(4):
                acc = jnp.where(group == g, lane_roll(ref[g].astype(F32), 32 * (g - b)), acc)
            out[128 * b:128 * b + 128, :] = acc.astype(BF)

    wait_bytes(xrecv.at[three], r_x)
    wait_bytes(w1s_full.at[three], r_w.at[0])
    unpack_feats(xrecv, xfull)
    slope[...] = dot(xfull[...], w1s_full[...].reshape(128, 256))
    xa_t[0:128, :] = jnp.transpose(xfull[...])

    for j in (3, 1, 2, 0):
        rr = ring_at(j)
        wait_bytes(row_bytes(recv1, j), r_e1.at[rr])

        def unpack1(k, c):
            b = rr * 8 + k
            for p in range(2):
                v = recv1[2 * b + p].astype(F32)
                for q in range(4):
                    src[4 + b, 64 * p + 16 * q:64 * p + 16 * q + 16, :] = lane_roll(v, -32 * q).astype(BF)
            return c

        lax.fori_loop(0, 8, unpack1, 0, unroll=8)

    def tile_product(b):
        lhs = jnp.concatenate([tiles[16 * b + k] for k in range(16)], axis=1)
        rhs = jnp.concatenate([src[tile_src[b, k]] for k in range(16)], axis=0)
        return dot(lhs, rhs)

    packed = jnp.zeros((128, 128), F32)
    for b in range(4):
        packed = packed + lane_roll(jnp.where(group == 0, tile_product(b), 0.0), 32 * b)
    aggp[...] = packed.astype(BF)
    to_feats(aggp, agg_recv, s_agg, r_agg, same=True)
    agg_recv[f] = aggp[...]

    wait_bytes(w1n_full.at[three], r_w.at[1])
    wait_bytes(agg_recv.at[three], r_agg)
    unpack_feats(agg_recv, aggf)

    pre = slope[...] + dot(aggf[...], w1n_full[...].reshape(128, 256))
    th = jnp.tanh(GELU_C * (pre + 0.044715 * (pre * pre * pre)))
    cdf = 0.5 * (1.0 + th)
    slope[...] = cdf + pre * (0.5 * (1.0 - th * th)) * (GELU_C * (1.0 + 3.0 * 0.044715 * (pre * pre)))
    hid[...] = (pre * cdf).astype(BF)

    low256 = lane(256) < 64

    def pack_halves(v, g):
        a, b = v[0:256], v[256:512]
        return jnp.where(low256, a if g % 2 == 0 else lane_roll(a, 64), lane_roll(b, 64) if g % 2 == 0 else b)

    for half in range(2):
        v = dot_nt(hid[...], w2p_t[256 + 128 * half:256 + 128 * half + 128, :])
        for g in (2 * half, 2 * half + 1):
            yv = jnp.where(lane(ROWS) < 64, v if g % 2 == 0 else lane_roll(v, 64), 0.0)
            yv = pack_slots(yv.reshape(8, 64, 128)).reshape(192, 128)
            yown[g] = yv
            ypack[g] = yv.astype(BF)
    to_feats(ypack, yrecv, s_y, r_y)
    for half in range(2):
        v = dot_nt(hid[...], w2p_t[128 * half:128 * half + 128, :])
        for g in (2 * half, 2 * half + 1):
            spack[g] = pack_halves(v, g)
    to_feats(spack, srecv, s_s, r_s)
    yrecv[f] = jnp.zeros((192, 128), BF)
    srecv[f] = spack[f]
    wait_bytes(yrecv.at[three], r_y)
    ys = yown[f]
    for g in range(4):
        ys = ys + yrecv[g].astype(F32)
    y_lo = jnp.where(lane(ROWS) < CLS, unpack_slots(ys.reshape(8, MSG, 128)).reshape(ROWS, 128), 0.0)
    ycat[0] = y_lo.astype(BF)
    ycat[1] = lane_roll(y_lo, CLS).astype(BF)
    ycat[2] = lane_roll(jnp.where(lane(ROWS) < CLS - 1, y_lo, 0.0), 2 * CLS).astype(BF)
    ycat[3] = jnp.broadcast_to(y_lo[:, CLS - 1:CLS], (ROWS, 128)).astype(BF)

    for j in range(RINGS):
        rr = ring_at(j)
        d0 = pl.multiple_of(rr * 16, 16)
        at = pl.ds(pl.multiple_of(rr * RING_ROWS, RING_ROWS), RING_ROWS)
        third = hot3[2, at, :]
        acc = dot(hot3[0, at, :], ycat[0]) + dot(hot3[1, at, :], ycat[1]) + dot(third, ycat[2])
        acc = acc.reshape(16, MSG, 128)
        rest = third_rest(dot(third, ycat[3]).reshape(16, MSG, 128))
        acc = jnp.where((iota((16, MSG, 128), 1) == 16) & (iota((16, MSG, 128), 2) >= 2 * CLS), rest, acc)
        out2[pl.ds(d0, 16)] = acc.astype(BF)

        def send2(k, c):
            k = (16 if j < 3 else 15) - 1 - k + (0 if j < 3 else 1)
            p = rr * 16 + place_at(k // 2) * 2 + lax.rem(core + k, 2)
            send(out2.at[p], recv2.at[me], s_e2, r_e2.at[ring], p, f)
            return c

        lax.fori_loop(0, 16 if j < 3 else 15, send2, 0)

    recv2[me] = out2[me]
    for b in range(4):
        src[b] = ycat[0, 128 * b:128 * b + 128, :]
    xa_t[128:256, :] = jnp.transpose(aggf[...])

    def turn_hot(y, c):
        for h in range(3):
            for k in range(4):
                part = hot3[h, pl.ds(pl.multiple_of(y * RING_ROWS, RING_ROWS), RING_ROWS), 128 * k:128 * k + 128]
                hot_t[y, h, 128 * k:128 * k + 128, :] = jnp.transpose(part)
        return c

    lax.fori_loop(0, RINGS, turn_hot, 0)

    for j in (3, 1, 2, 0):
        rr = ring_at(j)
        wait_bytes(row_bytes(recv2, j), r_e2.at[rr])

        def unpack2(k, c):
            b = rr * 8 + k
            v = recv2[pl.ds(2 * b, 2)].astype(F32)
            src[4 + b] = unpack_slots(v).reshape(128, 128).astype(BF)
            return c

        lax.fori_loop(0, 8, unpack2, 0, unroll=8)

    wait_bytes(srecv.at[three], r_s)
    ss = srecv[0] + srecv[1] + srecv[2] + srecv[3]
    pf[0, 0:256, :] = ss
    pf[0, 256:512, :] = lane_roll(ss, 64)

    mine = lane128 < CLS
    for b in range(4):
        r = slice(128 * b, 128 * b + 128)
        lg = jnp.where(mine, pf[0, r, :] + tile_product(b), -1e30)
        top = jnp.max(lg, axis=1, keepdims=True)
        ex = jnp.exp(lg - top)
        tot = jnp.sum(ex, axis=1, keepdims=True)
        lab = jnp.transpose(jnp.broadcast_to(labels[b:b + 1, :].astype(F32), (128, 128))).astype(I32)
        want = mine & ((lab - CLS * f) == lane128)
        hit = jnp.sum(jnp.where(want, lg, 0.0), axis=1, keepdims=True)
        st = jnp.where(lane128 == 0, top, jnp.where(lane128 == 1, tot, jnp.where(lane128 == 2, hit, 0.0)))
        st_t = jnp.transpose(st)
        stat[f, b:b + 1, :] = st_t[0:1]
        stat[f, 4 + b:5 + b, :] = st_t[1:2]
        hits[f, b:b + 1, :] = st_t[2:3]
        pf[1, r, :] = ex
        pf[2, r, :] = jnp.where(want, 1.0, 0.0)
    to_feats(stat.at[f], stat, s_st, r_st, same=True)
    wait_bytes(stat.at[three], r_st)

    tops = [stat[g, 0:4, :] for g in range(4)]
    best = jnp.maximum(jnp.maximum(tops[0], tops[1]), jnp.maximum(tops[2], tops[3]))
    total = jnp.zeros_like(best)
    for g in range(4):
        total = total + stat[g, 4:8, :] * jnp.exp(tops[g] - best)
    factor = jnp.exp(stat[f, 0:4, :] - best) / total
    for b in range(4):
        r = slice(128 * b, 128 * b + 128)
        fac = jnp.transpose(jnp.broadcast_to(factor[b:b + 1, :], (128, 128)))
        dl = ((pf[1, r, :] * fac - pf[2, r, :]) * grad_scale).astype(BF)
        rows = slice(128 * (b % 2), 128 * (b % 2) + 128)
        if b < 2:
            dlp[f, rows, :] = dl
        else:
            dlp[f, rows, :] = (dlp[f, rows, :].astype(F32) + lane_roll(dl.astype(F32), 64)).astype(BF)
        lhs = tiles_t[16 * b:16 * b + 16].reshape(2048, 128)
        ptile[16 * b:16 * b + 16] = dot(lhs, dl).reshape(16, 128, 128)
    to_feats(dlp.at[f], dlp, s_dl, r_dl, same=True)
    to_feats(hits.at[f], hits, s_hit, r_hit, same=True)

    def gather_sum(t, acc):
        acc = acc * order[1, t].astype(F32) + ptile[order[0, t]]
        run[t] = acc
        return acc

    lax.fori_loop(0, TILES, gather_sum, jnp.zeros((128, 128), F32), unroll=8)

    def landed(j):
        return run[order[2, j]] * order[3, j].astype(F32)

    for j in range(RINGS):
        rr = ring_at(j)

        def pack_back(k, c):
            to = rr * 8 + place_at(7 - k)
            blk = landed(4 + to)
            v = pack_slots(blk.reshape(2, 64, 128))
            ret[pl.ds(2 * to, 2)] = v.astype(BF)
            return c

        lax.fori_loop(0, 8, pack_back, 0, unroll=8)

        def send_back(k, c):
            k = (16 if j < 3 else 15) - 1 - k + (0 if j < 3 else 1)
            p = rr * 16 + place_at(k // 2) * 2 + lax.rem(core + k, 2)
            send(ret.at[p], recvb.at[me], s_eb, r_eb.at[ring], p, f)
            return c

        lax.fori_loop(0, 16 if j < 3 else 15, send_back, 0)

    recvb[me] = ret[me]
    for b in range(4):
        pf[3, 128 * b:128 * b + 128, :] = landed(b)

    def join(ref, out):
        for pair in range(2):
            c = slice(128 * pair, 128 * pair + 128)
            a, b = ref[2 * pair].astype(F32), ref[2 * pair + 1].astype(F32)
            out[0:256, c] = jnp.where(low256, a, lane_roll(b, 64)).astype(BF)
            out[256:512, c] = jnp.where(low256, lane_roll(a, 64), b).astype(BF)

    def class_rows(v, d):
        for l in range(2):
            d[l, TALL - 8:TALL, :] = jnp.zeros((8, 128), F32)
            for g in range(4):
                d[l, CLS * g:CLS * g + CLS, :] = v[64 * g:64 * g + CLS, 128 * l:128 * l + 128]

    def rows8(t):
        return pl.ds(pl.multiple_of(t * 8, 8), 8)

    def chip_at(i):
        return lax.rem(ring + (i // 8) + 4, RINGS) * 8 + place_at(lax.rem(i, 8))

    def for_chips(body):
        lax.fori_loop(1, CHIPS, lambda i, c: (body(chip_at(CHIPS - i)), c)[1], 0)

    def reduce_class(d, peer, part, k):
        wait_bytes(peer, r_pair.at[k])
        d[core] = d[core] + peer[...]

        def one(p):
            @pl.when(p < CLS_TILES)
            def _():
                send(d.at[core, rows8(p)], part.at[chip], s_red.at[k], r_red.at[k], 2 * p + core, f)

        for_chips(one)

        @pl.when(chip < CLS_TILES)
        def _():
            part[chip] = d[core, rows8(chip), :]

    def spread_class(part, tile, fin, k):
        @pl.when(chip < CLS_TILES)
        def _():
            wait_bytes(part.at[pl.ds(0, CHIPS - 1)], r_red.at[k])
            tile[...] = jnp.sum(part[...], axis=0)
            for_chips(lambda p: send(tile, fin.at[chip], s_fin.at[k], r_fin.at[k], 2 * p + core, f))
            fin[chip] = tile[...]

    def gather_class(fin, half, k):
        @pl.when(chip < CLS_TILES)
        def _():
            wait_bytes(fin.at[pl.ds(0, CLS_TILES - 1)], r_fin.at[k])

        @pl.when(chip >= CLS_TILES)
        def _():
            wait_bytes(fin, r_fin.at[k])

        send(fin, half, s_half.at[k], r_half.at[k], partner, f)

    wait_bytes(hits.at[three], r_hit)
    hit_sum = hits[0, 0:4, :] + hits[1, 0:4, :] + hits[2, 0:4, :] + hits[3, 0:4, :]
    loss = jnp.sum(jnp.log(total) + best - hit_sum)
    wait_bytes(dlp.at[three], r_dl)
    join(dlp, dlcat)
    dlcat_t[...] = jnp.transpose(dlcat[...])
    class_rows(dot(dlcat_t[...], hid[...]), da)
    tail = (iota((8, 128), 0) == 7) & (lane(8) == 0)
    for l in range(2):
        da[l, TALL - 8:TALL, :] = da[l, TALL - 8:TALL, :] + jnp.where(tail, loss, 0.0)
    send(da.at[1 - core], pa, s_pair.at[0], r_pair.at[0], partner, f)

    g_sum = pf[3]
    valid = lane(ROWS) < CLS
    for j in (3, 1, 2, 0):
        rr = ring_at(j)
        wait_bytes(row_bytes(recvb, j), r_eb.at[rr])
        back = recvb[pl.ds(pl.multiple_of(rr * 16, 16), 16)].astype(F32)
        third = split_third(lane_roll(back, -2 * CLS))
        third = jnp.concatenate([third, jnp.zeros((16, 8, 128), F32)], axis=1).reshape(RING_ROWS, 128).astype(BF)
        back = back.reshape(RING_ROWS, 128).astype(BF)
        g_sum = g_sum + jnp.where(valid, dot(hot_t[rr, 0], back) + dot(hot_t[rr, 2], third), 0.0)
        g_sum = g_sum + jnp.where(valid, lane_roll(dot(hot_t[rr, 1], back), -CLS), 0.0)
    gp[f] = pack_slots(g_sum.reshape(8, 64, 128)).reshape(192, 128).astype(BF)
    to_feats(gp.at[f], gp, s_g, r_g, same=True)
    reduce_class(da, pa, ra, 0)
    bh0 = dot(dlcat[...], w2p_t[0:256, :])
    wait_bytes(gp.at[three], r_g)
    for pair in range(2):
        a, b = (
            jnp.where(valid, unpack_slots(gp[g].astype(F32).reshape(8, MSG, 128)).reshape(ROWS, 128), 0.0)
            for g in (2 * pair, 2 * pair + 1)
        )
        gcat[:, 128 * pair:128 * pair + 128] = (a + lane_roll(b, 64)).astype(BF)

    bh = bh0 + dot(gcat[...], w2p_t[256:512, :])
    g1 = dot(xa_t[...], (bh * slope[...]).astype(BF))
    for l in range(2):
        dc[l] = g1[:, 128 * l:128 * l + 128]
    send(dc.at[1 - core], pc, s_pair.at[2], r_pair.at[2], partner, f)
    class_rows(dot(jnp.transpose(gcat[...]), hid[...]), db)
    send(db.at[1 - core], pb, s_pair.at[1], r_pair.at[1], partner, f)
    wait_bytes(pc, r_pair.at[2])
    dc[core] = dc[core] + pc[...]

    def rows1(p):
        m = p // 4
        return pl.ds(pl.multiple_of((m // 4) * 128 + 32 * lax.rem(f + lax.rem(p, 4), 4) + 8 * lax.rem(m, 4), 8), 8)

    for_chips(lambda p: send(dc.at[core, rows1(p)], rc.at[chip], s_red.at[2], r_red.at[2], 2 * p + core, f))
    rc[chip] = dc[core, rows1(chip), :]
    reduce_class(db, pb, rb, 1)
    spread_class(ra, ta, fin_a, 0)

    wait_bytes(rc.at[pl.ds(0, CHIPS - 1)], r_red.at[2])
    tc[...] = jnp.sum(rc[...], axis=0)
    turn_by = lax.rem(chip, 4)
    came_from = lax.rem(f - turn_by + 4, 4)

    @pl.when(turn_by > 0)
    def _():
        send(tc, trecv, s_t, r_t, me, lax.rem(f + turn_by, 4))

    spread_class(rb, tb, fin_b, 1)

    @pl.when(turn_by > 0)
    def _():
        wait_bytes(trecv, r_t)

    @pl.when(turn_by == 0)
    def _():
        trecv[...] = tc[...]

    for_chips(lambda p: send(trecv, fin_c.at[chip // 4, came_from], s_fin.at[2], r_fin_c.at[ring], 2 * p + core, f))
    fin_c[chip // 4, came_from] = trecv[...]

    gather_class(fin_a, half_a, 0)
    gather_class(fin_b, half_b, 1)

    for j in (3, 1, 2, 0):
        rr = ring_at(j)
        wait_bytes(rc.at[pl.ds(0, 7 if j == 3 else 8)], r_fin_c.at[rr])
        part = pl.ds(2 * rr, 2)
        send(fin_c.at[part], half_c.at[part], s_half.at[2], r_half.at[2], partner, f)

    n63, c31 = pl.ds(0, NODES - 1), pl.ds(0, CHIPS - 1)
    wait_bytes(recv1.at[n63], s_e1)
    wait_bytes(xrecv.at[three], s_x)
    wait_bytes(w1s_full.at[three], s_w.at[0])
    wait_bytes(w1n_full.at[three], s_w.at[1])
    wait_bytes(agg_recv.at[three], s_agg)
    wait_bytes(yrecv.at[three], s_y)
    wait_bytes(srecv.at[three], s_s)
    wait_bytes(recv2.at[n63], s_e2)
    wait_bytes(stat.at[three], s_st)
    wait_bytes(dlp.at[three], s_dl)
    wait_bytes(hits.at[three], s_hit)
    wait_bytes(recvb.at[n63], s_eb)
    wait_bytes(gp.at[three], s_g)
    wait_bytes(pa, s_pair.at[0])
    wait_bytes(pb, s_pair.at[1])
    wait_bytes(pc, s_pair.at[2])
    wait_bytes(rc.at[c31], s_red.at[2])
    for k, part in ((0, ra), (1, rb)):
        @pl.when(chip < CLS_TILES)
        def _():
            wait_bytes(part.at[pl.ds(0, CLS_TILES - 1)], s_red.at[k])
            wait_bytes(part.at[c31], s_fin.at[k])

        @pl.when(chip >= CLS_TILES)
        def _():
            wait_bytes(part.at[pl.ds(0, CLS_TILES)], s_red.at[k])

    wait_bytes(rc.at[c31], s_fin.at[2])

    @pl.when(turn_by > 0)
    def _():
        wait_bytes(trecv, s_t)

    for k, ref in enumerate((half_a, half_b, half_c)):
        wait_bytes(ref, s_half.at[k])
        wait_bytes(ref, r_half.at[k])


def result_kernel(scale, fin_a, half_a, fin_b, half_b, fin_c, half_c, loss_ref, gs1_ref, gn1_ref, gs2_ref, gn2_ref):
    core = lax.rem(lax.axis_index("node"), 2)
    first = core == 0
    loss_ref[...] = fin_a[CLS_TILES - 1, 7:8, 0:1] * scale
    for l in range(2):
        c = slice(128 * l, 128 * l + 128)
        mine = first if l == 0 else jnp.logical_not(first)
        for fin, half, ref in ((fin_a, half_a, gs2_ref), (fin_b, half_b, gn2_ref)):
            ref[:, c] = jnp.where(mine, fin[...], half[...]).reshape(TALL, 128)[0:CLASSES]
        v = jnp.where(mine, fin_c[...], half_c[...])
        for g in range(4):
            cols = slice(256 * g + 128 * l, 256 * g + 128 * l + 128)
            gs1_ref[:, cols] = v[0:4, g].reshape(32, 128)
            gn1_ref[:, cols] = v[4:8, g].reshape(32, 128)


def shards(features, send_rows, send_count, tile_src, tile_val, labels, w_self1, w_neigh1, w_self2, w_neigh2):
    vm = lambda *shape, dt=F32: pltpu.VMEM(shape, dt)
    dma = pltpu.SemaphoreType.DMA
    whole = pl.BlockSpec(memory_space=pltpu.VMEM)
    half_class = jax.ShapeDtypeStruct((CLS_TILES, 8, 128), F32)
    half_first = jax.ShapeDtypeStruct((8, 4, 8, 128), F32)
    parts = pl.pallas_call(
        functools.partial(step_kernel, 1.0 / math.sqrt(ROWS * NODES)),
        out_shape=(half_class,) * 4 + (half_first,) * 2,
        in_specs=[pl.BlockSpec(memory_space=pltpu.HBM)] * 10,
        out_specs=(whole,) * 6,
        scratch_shapes=[
            pltpu.SMEM((4, 16), I32), vm(32, 512, dt=BF), vm(64, 64, dt=I32), vm(1, 64, dt=I32), vm(4, 128, dt=I32),
            vm(32, 1024, dt=BF), vm(32, 1024, dt=BF), vm(CLASSES, 256, dt=BF), vm(CLASSES, 256, dt=BF),
            vm(64, 128, 128, dt=BF), vm(4, 512, 128, dt=BF), vm(128, 128, dt=BF), vm(64, 128, dt=I32), vm(2, 256, 256),
            vm(512, 256, dt=BF), vm(8, 128, dt=I32), pltpu.SMEM((8, 128), I32),
            vm(64, 64, 512, dt=BF), vm(3, 1536, 512, dt=BF), vm(4, 3, 512, 384, dt=BF), vm(64, 128, 128, dt=BF), vm(36, 128, 128, dt=BF),
            vm(64, 128, 128), vm(64, 128, 128),
            vm(64, 16, 128, dt=BF), vm(64, 16, 128, dt=BF), vm(4, 128, 128, dt=BF),
            vm(4, 32, 256, dt=BF), vm(4, 32, 256, dt=BF), vm(128, 128, dt=BF), vm(4, 128, 128, dt=BF),
            vm(512, 128, dt=BF), vm(512, 128, dt=BF),
            vm(512, 256), vm(512, 256, dt=BF), vm(256, 512, dt=BF), vm(4, 512, 128),
            vm(4, 512, 128, dt=BF), vm(4, 192, 128, dt=BF), vm(4, 192, 128), vm(4, 192, 128, dt=BF),
            vm(4, 256, 128), vm(4, 256, 128),
            vm(64, MSG, 128, dt=BF), vm(64, MSG, 128, dt=BF), vm(4, 8, 128), vm(4, 8, 128), vm(4, 256, 128, dt=BF),
            vm(64, MSG, 128, dt=BF), vm(64, MSG, 128, dt=BF), vm(4, 192, 128, dt=BF),
            vm(512, 256, dt=BF), vm(256, 512, dt=BF), vm(512, 256, dt=BF),
            vm(2, TALL, 128), vm(TALL, 128), vm(2, TALL, 128), vm(TALL, 128), vm(2, 256, 128), vm(256, 128),
            vm(32, 8, 128), vm(32, 8, 128), vm(32, 8, 128), vm(8, 128), vm(8, 128), vm(8, 128), vm(8, 128),
            dma((10,)), dma, dma, dma, dma((2,)), dma((2,)), dma, dma((4,)), dma, dma, dma, dma, dma, dma, dma, dma((4,)),
            dma, dma, dma, dma, dma, dma((4,)), dma, dma, dma((3,)), dma((3,)), dma((3,)), dma((3,)),
            dma, dma, dma((3,)), dma((3,)), dma((3,)), dma((3,)), dma, dma, dma((4,)),
        ],
        compiler_params=pltpu.CompilerParams(
            collective_id=0, has_side_effects=True, vmem_limit_bytes=44 * 1024 * 1024
        ),
    )(*[
        pltpu.with_memory_space_constraint(a, pltpu.HBM)
        for a in (
            tile_src, features.T, send_rows[0], send_count, tile_val.reshape(TILES, 128, 128), labels.reshape(4, 128),
            w_self1, w_neigh1, w_self2.T, w_neigh2.T,
        )
    ])
    loss, gs1, gn1, gs2, gn2 = pl.pallas_call(
        functools.partial(result_kernel, 1.0 / (ROWS * NODES)),
        out_shape=(
            jax.ShapeDtypeStruct((1, 1), F32),
            jax.ShapeDtypeStruct((32, 1024), F32),
            jax.ShapeDtypeStruct((32, 1024), F32),
            jax.ShapeDtypeStruct((CLASSES, 256), F32),
            jax.ShapeDtypeStruct((CLASSES, 256), F32),
        ),
        in_specs=[whole] * 6,
        out_specs=(whole,) * 5,
        compiler_params=pltpu.CompilerParams(vmem_limit_bytes=8 * 1024 * 1024),
    )(*parts)
    return (loss[0, 0], gs1, gn1, gs2.T, gn2.T)


def solution(mesh):
    in_specs = (
        P("node", "feat"),
        P("node", None, None),
        P("node", None),
        P("node", None),
        P("node", None, None, None),
        P("node"),
        P("feat", None),
        P("feat", None),
        P("feat", None),
        P("feat", None),
    )
    out_specs = (P(), P("feat", None), P("feat", None), P("feat", None), P("feat", None))
    return jax.shard_map(shards, mesh=mesh, in_specs=in_specs, out_specs=out_specs, check_vma=False)
```
